32 devices in a mesh: dp: 4 (over y, x), expert: 4 (over z), tok: 2 (over core).
Axes of the slice: x: 2, y: 2, z: 4, core: 2. Of those that a mesh axis runs over, the one named last changes fastest.
Arguments:
- tokens: bfloat16 [32768, 512], P(('dp', 'expert', 'tok')), may hold values from -6 to 6
- out_grad: bfloat16 [32768, 512], P(('dp', 'expert', 'tok')), may hold values from -6 to 6
- expert_ids: int32 [32768, 2], P(('dp', 'expert', 'tok')), may hold values from 0 to 3, all different within a row; in each aligned block of 1024 rows (0 to 1023, 1024 to 2047, ...) at most 768 rows name the same one
- sentence_ids: int32 [32, 1024], P(('dp', 'expert', 'tok')), may hold values from 0 to 15, never falling along the last dimension, each value on 1 to 128 neighbouring positions
- ln_attn: float32 [512], replicated, may hold values from 0.25 to 1.75
- w_kv: bfloat16 [512, 128], replicated, may hold values from -0.25 to 0.25
- w_router: bfloat16 [512, 4], replicated, may hold values from -0.1875 to 0.1875
- w_query: bfloat16 [4, 512, 64], P('expert'), may hold values from -0.25 to 0.25
- w_output: bfloat16 [4, 64, 512], P('expert'), may hold values from -4 to 4
- ln_ffn: float32 [512], replicated, may hold values from 0.25 to 1.75
- w_in: bfloat16 [512, 2048], replicated, may hold values from -0.25 to 0.25
- w_out: bfloat16 [2048, 512], replicated, may hold values from -0.1875 to 0.1875
Outputs:
- output: bfloat16 [32768, 512], P(('dp', 'expert', 'tok'))
- grad_tokens: bfloat16 [32768, 512], P(('dp', 'expert', 'tok'))
- grad_ln_attn: float32 [512], replicated
- grad_kv: float32 [512, 128], replicated
- grad_router: float32 [512, 4], replicated
- grad_query: float32 [4, 512, 64], P('expert')
- grad_output: float32 [4, 64, 512], P('expert')
- grad_ln_ffn: float32 [512], replicated
- grad_in: float32 [512, 2048], replicated
- grad_out: float32 [2048, 512], replicated
The draws below stay inside these ranges and needn't reach their ends.
Inputs may be any that keep to these rules, and one draw needn't show every extreme that they name: `expert_ids`: among the 1024 rows of one device no expert is named more than 768 times, a bound that some block reaches; a token's 2 ids differ. `sentence_ids`: in each device's row the ids never fall; each id covers 1 to 128 consecutive positions, one exactly 128.
All inputs are finite; a program needn't handle non-finite values.
Results may differ from the reference program's by a relative error of at most 0.017.
Values may be sent and summed in bfloat16 or wider, within the bound.
No kernel may reach another device: no remote copies, remote signals or barrier semaphores. Data moves between devices by JAX's collectives and lax.ppermute only.
A program may use at most 128 MiB of HBM per device.

```python
import math
import jax
import jax.numpy as jnp
import numpy as np
from jax import lax

D = 512
HEAD = 64
FF = 2048
TOP = 2
TOK_DEV = 1024
SENT_MOST = 128
EXPERTS = 4
S_DEV = 16
CAP = 768
TOKENS = 32768
DEVICES = 32


def shard_levels(rng, dims, split, low, high):
    def one(position, parts):
        heights = jax.random.uniform(jax.random.fold_in(jax.random.fold_in(rng, 6), position), (parts,), jnp.float32, low / len(split), high / len(split))
        return jnp.repeat(jnp.exp(heights), dims[position] // parts).reshape((-1,) + (1,) * (len(dims) - position - 1))

    loudness = one(*split[0])
    for cut in split[1:]:
        loudness = loudness * one(*cut)
    return loudness


def length_profile(amount, total, limit, skew):
    weights = [(1 << 20) // math.isqrt(rank ** skew) + 1 for rank in range(2, amount + 1)]
    surplus, given = total - limit - (amount - 1), [1] * (amount - 1)
    while surplus > 0:
        free = [i for i in range(amount - 1) if given[i] < limit]
        whole, left = sum([weights[i] for i in free]), surplus
        for i in free:
            addition = min(limit - given[i], max(1, left * weights[i] // whole), surplus)
            given[i] = given[i] + addition
            surplus = surplus - addition
    return np.array([limit] + given)


def uneven_parts(stream_key, number_of, total, limit, skew):
    if number_of == 2:
        one = jax.random.randint(stream_key, (), max(1, total - limit), min(limit, total - 1) + 1)
        return jnp.stack([one, total - one])
    sizes = jnp.asarray(length_profile(number_of, total, limit, skew), jnp.int32)
    twos = (number_of - 1) // 2
    source_of, sink = sizes[1:1 + 2 * twos:2], sizes[2:2 + 2 * twos:2]
    slack = jnp.minimum(source_of - 1, limit - sink)
    passed = jax.random.randint(jax.random.fold_in(stream_key, 1), (twos,), 0, 1 << 20) % (slack + 1)
    sizes = sizes.at[1:1 + 2 * twos:2].set(source_of - passed).at[2:2 + 2 * twos:2].set(sink + passed)
    return sizes[jax.random.permutation(jax.random.fold_in(stream_key, 2), number_of)]


def assign_block(stream_key, own, number, rows, count, top, reach, slope):
    ranking = jax.random.permutation(stream_key, count)
    heavy_load, common = shares(count, rows * top, reach, slope, True), shares(count, rows * top, reach, slope, False)
    places = jnp.arange(count)

    def named(tallies, turn):
        used = int((tallies > 0).sum())
        fixed = max(1, used // 4)
        shifted = fixed + (places - fixed + turn * (used - fixed)) % max(1, count - fixed)
        return jnp.zeros((count,), jnp.int32).at[ranking[jnp.where(places < fixed, places, shifted)]].set(jnp.asarray(tallies, jnp.int32))

    tallies = jnp.where(number % 4 == 0, named(heavy_load, number // 4), named(common, number - number // 4 - 1))
    mixed = jax.random.permutation(jax.random.fold_in(own, 3), count)
    donor, taker = mixed[0:count // 2 * 2:2], mixed[1:count // 2 * 2:2]
    room = jnp.minimum(tallies[donor] - 1, reach - tallies[taker]) // 2
    room = jnp.where((donor == ranking[0]) | (taker == ranking[0]) | (tallies[taker] == 0), 0, jnp.maximum(room, 0))
    shifted = jax.random.randint(jax.random.fold_in(own, 4), (count // 2,), 0, 1 << 20) % (room + 1)
    tallies = tallies.at[donor].add(-shifted).at[taker].add(shifted)
    labels = jnp.searchsorted(jnp.cumsum(tallies), jnp.arange(rows * top), side="right").astype(jnp.int32)
    grid = labels.reshape(top, rows).T
    grid = grid[jax.random.permutation(jax.random.fold_in(own, 1), rows)]
    turn = jax.random.randint(jax.random.fold_in(own, 2), (rows, 1), 0, top)
    return jnp.take_along_axis(grid, (jnp.arange(top)[None, :] + turn) % top, axis=1)


def shares(number_of, total, bound, lean, full):
    loads = [(1 << 20) // math.isqrt(rank ** lean) + 1 for rank in range(1, number_of + 1)]
    largest = bound if full else min(bound, max(-(-total // number_of), total * loads[0] // sum(loads)))
    least = 1 if total - largest >= number_of - 1 else 0
    given, surplus = [largest] + [least] * (number_of - 1), total - largest - least * (number_of - 1)
    while surplus > 0:
        free = [i for i in range(1, number_of) if given[i] < largest] or [i for i in range(1, number_of) if given[i] < bound]
        pool, remaining = sum([loads[i] for i in free]), surplus
        for i in free:
            more = min(bound - given[i], max(1, remaining * loads[i] // pool), surplus)
            given[i] = given[i] + more
            surplus = surplus - more
    return np.array(given)


def scatter_about(rng, dims, scale, reach, cuts=(), kind=jnp.bfloat16):
    level = shard_levels(rng, dims, cuts, -0.22, 0.18) if cuts else 1.0
    array = jax.random.normal(rng, dims, jnp.float32) * scale * level
    return jnp.minimum(jnp.maximum(array, -reach), reach).astype(kind)


def setup_inputs(seed: int = 0) -> dict:
    seeds = jax.random.split(jax.random.key(seed), 13)
    tokens = scatter_about(seeds[0], (TOKENS, D), 1.0, 6.0, ((0, 32),))
    out_grad = scatter_about(seeds[1], (TOKENS, D), 1.0, 6.0, ((0, 32),))
    expert_ids_keys = jax.random.split(jax.random.fold_in(seeds[2], 1), TOKENS // TOK_DEV)
    expert_ids_turns = jax.random.permutation(jax.random.fold_in(seeds[2], 3), TOKENS // TOK_DEV)
    expert_ids = jax.vmap(lambda own, number: assign_block(jax.random.fold_in(seeds[2], 2), own, number, TOK_DEV, EXPERTS, TOP, CAP, 1))(expert_ids_keys, expert_ids_turns).reshape((TOKENS, TOP))
    sentence_ids = jax.vmap(lambda own: jnp.searchsorted(jnp.cumsum(uneven_parts(own, S_DEV, TOK_DEV, SENT_MOST, 1)), jnp.arange(TOK_DEV), side="right"))(jax.random.split(seeds[3], DEVICES)).reshape((DEVICES, TOK_DEV)).astype(jnp.int32)
    ln_attn = jnp.clip(1.0 + 0.15 * jax.random.normal(seeds[4], (D,), jnp.float32), 0.25, 1.75)
    w_kv = scatter_about(seeds[5], (D, 2 * HEAD), D ** -0.5, 0.25)
    w_router = scatter_about(seeds[6], (D, EXPERTS), (2 * D) ** -0.5, 0.1875)
    w_query = scatter_about(seeds[7], (EXPERTS, D, HEAD), D ** -0.5, 0.25, ((0, 4),))
    w_output = scatter_about(seeds[8], (EXPERTS, HEAD, D), (max(1, HEAD // 32)) ** -0.5, 4.0, ((0, 4),))
    ln_ffn = jnp.clip(1.0 + 0.15 * jax.random.normal(seeds[9], (D,), jnp.float32), 0.25, 1.75)
    w_in = scatter_about(seeds[10], (D, FF), D ** -0.5, 0.25)
    w_out = scatter_about(seeds[11], (FF, D), (FF // 2) ** -0.5, 0.1875)
    return {"tokens": tokens, "out_grad": out_grad, "expert_ids": expert_ids, "sentence_ids": sentence_ids, "ln_attn": ln_attn, "w_kv": w_kv, "w_router": w_router, "w_query": w_query, "w_output": w_output, "ln_ffn": ln_ffn, "w_in": w_in, "w_out": w_out}


@jax.custom_vjp
def low(v):
    return lax.optimization_barrier(v.astype(jnp.bfloat16)).astype(jnp.float32)

@jax.custom_vjp
def low_back(v):
    return v

def low_keep(v):
    return (low(v), None)

def low_pass(kept, grad):
    return (grad,)

def back_keep(v):
    return (v, None)

def back_low(kept, grad):
    return (low(grad),)
low.defvjp(low_keep, low_pass)
low_back.defvjp(back_keep, back_low)

def matmul(left, right):
    return jnp.dot(left, right, precision=lax.Precision.HIGHEST)

def contract(form, left, right):
    return jnp.einsum(form, left, right, precision=lax.Precision.HIGHEST)

def plain_softmax(values):
    largest = lax.optimization_barrier(jnp.max(values, axis=-1, keepdims=True))
    raised = jnp.exp(values - largest)
    return raised / lax.optimization_barrier(jnp.sum(raised, axis=-1, keepdims=True))

def layer_norm(values, gain):
    centre = values - lax.optimization_barrier(jnp.mean(values, axis=-1, keepdims=True))
    spread = lax.optimization_barrier(jnp.mean(centre * centre, axis=-1, keepdims=True))
    return centre * lax.rsqrt(spread + 1e-05) * gain

def gelu_exact(values):
    return 0.5 * values * (1.0 + jax.scipy.special.erf(values * 0.7071067811865476))

def block_forward(params, inputs, routes, sentence):
    ln_one, kv_weight, router_weight, query_weight, output_weight, ln_two, in_weight, out_weight = params
    head_size = query_weight.shape[2]
    experts = query_weight.shape[0]
    length = inputs.shape[0]
    choose = routes.shape[1]
    normed = low(layer_norm(inputs, ln_one))
    shared = low_back(low(matmul(normed, kv_weight)))
    keys = shared[:, :head_size]
    values = shared[:, head_size:]
    logits = low_back(matmul(normed, router_weight))
    selector = (routes[:, :, None] == jnp.arange(experts, dtype=jnp.int32)[None, None, :]).astype(inputs.dtype)
    picked = contract('tre,te->tr', selector, logits)
    gates = plain_softmax(picked)
    query_list = []
    for route in range(choose):
        source_rows = low_back(normed)
        every_query = contract('td,edh->teh', source_rows, query_weight)
        query_list.append(low_back(low(contract('te,teh->th', selector[:, route], every_query))))
    queries = jnp.stack(query_list, axis=1)
    block_rows = min(512, length)
    blocks = length // block_rows

    def attend(block):
        query_block, sentence_block = block
        scores = low_back(contract('qrh,kh->qrk', query_block, keys) * 0.125)
        same = sentence_block[:, None, None] == sentence[None, None, :]
        scores = jnp.where(same, scores, -30000.0)
        weights = low(plain_softmax(scores))
        return contract('qrk,kh->qrh', weights, values)
    attended = lax.map(jax.checkpoint(attend), (queries.reshape(blocks, block_rows, choose, head_size), sentence.reshape(blocks, block_rows)))
    attended = low_back(low(attended.reshape(length, choose, head_size)))
    mixed = jnp.zeros_like(inputs)
    for route in range(choose):
        spread_rows = selector[:, route, :, None] * attended[:, route, None, :]
        expert_out = low_back(low(contract('teh,ehd->td', spread_rows, output_weight)))
        mixed = mixed + gates[:, route:route + 1] * expert_out
    hidden_in = inputs + mixed
    normed_two = low(layer_norm(hidden_in, ln_two))
    before = low_back(matmul(normed_two, in_weight))
    activated = low(gelu_exact(before))
    return hidden_in + matmul(activated, out_weight)

def reference(tokens, out_grad, expert_ids, sentence_ids, ln_attn, w_kv, w_router, w_query, w_output, ln_ffn, w_in, w_out):
    params = tuple((weight.astype(jnp.float32) for weight in (ln_attn, w_kv, w_router, w_query, w_output, ln_ffn, w_in, w_out)))
    count = TOKENS // TOK_DEV
    inputs = tokens.astype(jnp.float32).reshape(count, TOK_DEV, D)
    cotangent = out_grad.astype(jnp.float32).reshape(count, TOK_DEV, D)
    routes = expert_ids.astype(jnp.int32).reshape(count, TOK_DEV, TOP)
    sentences = sentence_ids.astype(jnp.int32)

    def step(totals, block):
        block_in, block_grad, block_routes, block_sentence = block
        result, pullback = jax.vjp(lambda weights, values: block_forward(weights, values, block_routes, block_sentence), params, block_in)
        weight_grads, input_grad = pullback(block_grad)
        totals = jax.tree.map(lambda left, right: left + right, totals, weight_grads)
        return (totals, (result.astype(jnp.bfloat16), input_grad.astype(jnp.bfloat16)))
    start = jax.tree.map(lambda weight: jnp.zeros(weight.shape, weight.dtype), params)
    totals, (results, input_grads) = lax.scan(step, start, (inputs, cotangent, routes, sentences))
    return (results.reshape(TOKENS, D), input_grads.reshape(TOKENS, D), totals[0], totals[1], totals[2], totals[3], totals[4], totals[5], totals[6], totals[7])
```

```python
import functools
import jax
import jax.numpy as jnp
from jax import lax
from jax.experimental import pallas as pl
from jax.experimental.pallas import tpu as pltpu
from jax.sharding import PartitionSpec as P

BF = jnp.bfloat16
F32 = jnp.float32
MASKED = -1e30
BAND = 128
ROWS = 256
VMEM_LIMIT = 56 * 1024 * 1024


def nn(left, right):
    return lax.dot_general(left, right, (((1,), (0,)), ((), ())), preferred_element_type=F32)


def nt(left, right):
    return lax.dot_general(left, right, (((1,), (1,)), ((), ())), preferred_element_type=F32)


def tn(left, right):
    return lax.dot_general(left, right, (((0,), (0,)), ((), ())), preferred_element_type=F32)


def normalize(values):
    centre = values - jnp.mean(values, axis=-1, keepdims=True)
    spread = jnp.mean(centre * centre, axis=-1, keepdims=True)
    inverse = lax.rsqrt(spread + 1e-05)
    return centre * inverse, inverse


def normalize_back(upstream, normalized, inverse, gain):
    scaled = upstream * gain
    inner = (
        scaled
        - jnp.mean(scaled, axis=-1, keepdims=True)
        - normalized * jnp.mean(scaled * normalized, axis=-1, keepdims=True)
    )
    return inner * inverse


def vmem(count):
    return [pl.BlockSpec(memory_space=pltpu.VMEM)] * count


def call(kernel, operands, outs, scratch=(), flops=0, **extra):
    moved = sum(a.size * a.dtype.itemsize for a in operands)
    moved += sum(o.size * jnp.dtype(o.dtype).itemsize for o in outs)
    return pl.pallas_call(
        kernel,
        out_shape=outs,
        in_specs=vmem(len(operands)),
        out_specs=vmem(len(outs)),
        scratch_shapes=list(scratch),
        compiler_params=pltpu.CompilerParams(vmem_limit_bytes=VMEM_LIMIT),
        cost_estimate=pl.CostEstimate(flops=flops, bytes_accessed=moved, transcendentals=0),
        **extra,
    )(*operands)


def sds(shape, dtype):
    return jax.ShapeDtypeStruct(shape, dtype)


def prepare_kernel(x_ref, g_ref, ids_ref, ln_ref, small_ref, xn_ref, kv_ref, kvt_ref, gates_ref, gt_ref, *, experts, pair):
    length = x_ref.shape[0]
    gain = ln_ref[...]
    for start in range(0, length, ROWS):
        rows = pl.ds(start, ROWS)
        normalized, _ = normalize(x_ref[rows, :].astype(F32))
        xn_ref[rows, :] = (normalized * gain).astype(BF)
    normed = xn_ref[...]
    small = small_ref[...]
    both = nt(small, normed)
    kvt_ref[...] = both[:pair].astype(BF)
    kv_ref[...] = nt(normed, small[:pair]).astype(BF)
    choose = ids_ref.shape[0]
    picked = []
    for route in range(choose):
        ids = ids_ref[route : route + 1, :]
        value = jnp.zeros((1, length), F32)
        for expert in range(experts):
            value = jnp.where(ids == expert, both[pair + expert : pair + expert + 1], value)
        picked.append(value)
    top = functools.reduce(jnp.maximum, picked)
    raised = [jnp.exp(value - top) for value in picked]
    total = functools.reduce(lambda a, b: a + b, raised)
    for route in range(choose):
        gates_ref[route : route + 1, :] = raised[route] / total
    gt_ref[...] = g_ref[...].T


def column_ids(sent_ref, keyid_ref):
    length = sent_ref.shape[1]
    for start in range(0, length, BAND):
        row = jnp.broadcast_to(sent_ref[:, start : start + BAND].astype(F32), (BAND, BAND))
        keyid_ref[pl.ds(start, BAND), :] = row.T


def masked_scores(kv_ref, keyid_ref, sent_ref, queries, start, low, high, head, choose):
    padded = jnp.concatenate([queries, jnp.zeros_like(queries)], axis=0)
    scores = nn(kv_ref[low:high, :], padded) * 0.125
    same = keyid_ref[low:high, :] == sent_ref[:, start : start + BAND].astype(F32)
    parts = [
        jnp.where(same, scores[:, route * BAND : (route + 1) * BAND], MASKED)
        for route in range(choose)
    ]
    return jnp.concatenate(parts, axis=1)


def window(start, length):
    return max(start - BAND, 0), min(start + 2 * BAND, length)


def attend_kernel(
    x_ref, xn_ref, kv_ref, kvt_ref, ids_ref, sent_ref, gates_ref, wq_ref, wo_ref, ln_ref,
    qt_ref, at_ref, lse_ref, gat_ref, h_ref, hn_ref, hnt_ref, all_ref, keyid_ref, *, experts, head,
):
    length = x_ref.shape[0]
    choose = ids_ref.shape[0]
    column_ids(sent_ref, keyid_ref)
    all_ref[...] = nt(wq_ref[...], xn_ref[...])
    for start in range(0, length, BAND):
        lanes = slice(start, start + BAND)
        block = slice(start * choose, (start + BAND) * choose)
        low, high = window(start, length)
        chosen = []
        for route in range(choose):
            ids = ids_ref[route : route + 1, lanes]
            value = jnp.zeros((head, BAND), F32)
            for expert in range(experts):
                value = jnp.where(
                    ids == expert, all_ref[expert * head : (expert + 1) * head, lanes], value
                )
            chosen.append(value)
        queries = jnp.concatenate(chosen, axis=1).astype(BF)
        qt_ref[:, block] = queries
        scores = masked_scores(kv_ref, keyid_ref, sent_ref, queries, start, low, high, head, choose)
        largest = jnp.max(scores, axis=0, keepdims=True)
        raised = jnp.exp(scores - largest)
        total = jnp.sum(raised, axis=0, keepdims=True)
        probs = (raised * (1.0 / total)).astype(BF)
        lse_ref[:, block] = largest + jnp.log(total)
        attended = nn(kvt_ref[head:, low:high], probs).astype(BF)
        at_ref[:, block] = attended
        spread = [jnp.zeros((head, BAND), F32) for _ in range(experts)]
        for route in range(choose):
            ids = ids_ref[route : route + 1, lanes]
            gated = attended[:, route * BAND : (route + 1) * BAND].astype(F32) * gates_ref[
                route : route + 1, lanes
            ]
            for expert in range(experts):
                spread[expert] = jnp.where(ids == expert, gated, spread[expert])
        for expert in range(experts):
            gat_ref[expert * head : (expert + 1) * head, lanes] = spread[expert].astype(BF)
    gain = ln_ref[...]
    for start in range(0, length, ROWS):
        rows = slice(start, start + ROWS)
        mixed = tn(gat_ref[:, rows], wo_ref[...])
        hidden = x_ref[rows, :].astype(F32) + mixed
        h_ref[rows, :] = hidden
        normalized, _ = normalize(hidden)
        low_value = (normalized * gain).astype(BF)
        hn_ref[rows, :] = low_value
        hnt_ref[:, rows] = low_value.T


def gelu_both(values):
    bell = jnp.exp(-0.5 * values * values)
    t = 1.0 / (1.0 + 0.23164188 * jnp.abs(values))
    poly = 0.5 * t * (
        0.254829592
        + t * (-0.284496736 + t * (1.421413741 + t * (-1.453152027 + t * 1.061405429)))
    )
    tail = poly * bell
    cumulative = jnp.where(values >= 0.0, 1.0 - tail, tail)
    return values * cumulative, cumulative + values * bell * 0.3989422804014327


def ffn_kernel(hn_ref, hnt_ref, g_ref, gt_ref, win_ref, wout_ref, u_ref, dpre_ref, gin_ref, gout_ref):
    length = hn_ref.shape[0]
    win = win_ref[...]
    wout = wout_ref[...]
    for start in range(0, length, ROWS):
        rows = slice(start, start + ROWS)
        before = nn(hn_ref[rows, :], win)
        upstream = nt(g_ref[rows, :], wout)
        activated, slope = gelu_both(before)
        u_ref[rows, :] = activated.astype(BF)
        dpre_ref[rows, :] = (upstream * slope).astype(BF)
    gin_ref[...] = nn(hnt_ref[...], dpre_ref[...]).astype(gin_ref.dtype)
    gout_ref[...] = nn(gt_ref[...], u_ref[...]).T.astype(gout_ref.dtype)


def finish_kernel(h_ref, g_ref, u_ref, dpre_ref, win_ref, wout_ref, ln_ref, out_ref, dh_ref, gain_ref):
    hidden = h_ref[...]
    out_ref[...] = (hidden + nn(u_ref[...], wout_ref[...])).astype(BF)
    upstream = nt(dpre_ref[...], win_ref[...])
    normalized, inverse = normalize(hidden)
    dh_ref[...] = g_ref[...].astype(F32) + normalize_back(upstream, normalized, inverse, ln_ref[...])

    @pl.when(pl.program_id(0) == 0)
    def _():
        gain_ref[...] = jnp.zeros_like(gain_ref)

    gain_ref[...] += jnp.sum(upstream * normalized, axis=0, keepdims=True)


def back_kernel(
    x_ref, xn_ref, kv_ref, kvt_ref, ids_ref, sent_ref, gates_ref, wcat_ref, wo_ref, ln_ref,
    qt_ref, at_ref, lse_ref, gat_ref, dh_ref,
    dx_ref, grads_ref, gout_ref, gain_ref, all_ref, keyid_ref, z_ref, dkv_ref, *, experts, head,
):
    length = x_ref.shape[0]
    choose = ids_ref.shape[0]
    wide = experts * head
    column_ids(sent_ref, keyid_ref)
    dh_low = dh_ref[...].astype(BF)
    all_ref[...] = nt(wo_ref[...], dh_low)
    gout_ref[...] = nn(gat_ref[...], dh_low).astype(gout_ref.dtype)
    dkv_ref[...] = jnp.zeros_like(dkv_ref)
    z_ref[...] = jnp.zeros_like(z_ref)
    for start in range(0, length, BAND):
        lanes = slice(start, start + BAND)
        block = slice(start * choose, (start + BAND) * choose)
        low, high = window(start, length)
        raw, gate_grads = [], []
        for route in range(choose):
            ids = ids_ref[route : route + 1, lanes]
            value = jnp.zeros((head, BAND), F32)
            for expert in range(experts):
                value = jnp.where(
                    ids == expert, all_ref[expert * head : (expert + 1) * head, lanes], value
                )
            raw.append(value)
            attended = at_ref[:, start * choose + route * BAND : start * choose + (route + 1) * BAND]
            gate_grads.append(jnp.sum(value * attended.astype(F32), axis=0, keepdims=True))
        gates = [gates_ref[route : route + 1, lanes] for route in range(choose)]
        common = functools.reduce(
            lambda a, b: a + b, [gate * grad for gate, grad in zip(gates, gate_grads)]
        )
        logit_rows = [jnp.zeros((1, BAND), F32) for _ in range(experts)]
        for route in range(choose):
            ids = ids_ref[route : route + 1, lanes]
            picked = gates[route] * (gate_grads[route] - common)
            for expert in range(experts):
                logit_rows[expert] = jnp.where(ids == expert, picked, logit_rows[expert])
        logit_pad = jnp.concatenate(
            logit_rows + [jnp.zeros((16 - experts, BAND), F32)], axis=0
        )
        z_ref[wide + 2 * head :, lanes] = logit_pad.astype(BF)
        queries = qt_ref[:, block]
        scores = masked_scores(kv_ref, keyid_ref, sent_ref, queries, start, low, high, head, choose)
        probs = jnp.exp(scores - lse_ref[:, block])
        prob_low = probs.astype(BF)
        upstream = jnp.concatenate(
            [gate * value for gate, value in zip(gates, raw)], axis=1
        ).astype(BF)
        padded = jnp.concatenate([jnp.zeros_like(upstream), upstream], axis=0)
        prob_grad = nn(kv_ref[low:high, :], padded)
        mean = jnp.sum(probs * prob_grad, axis=0, keepdims=True)
        score_grad = (probs * (prob_grad - mean)).astype(BF)
        query_grad = (nn(kvt_ref[:head, low:high], score_grad) * 0.125).astype(BF)
        spread = [jnp.zeros((head, BAND), BF) for _ in range(experts)]
        for route in range(choose):
            ids = ids_ref[route : route + 1, lanes]
            piece = query_grad[:, route * BAND : (route + 1) * BAND]
            for expert in range(experts):
                spread[expert] = jnp.where(ids == expert, piece, spread[expert])
        for expert in range(experts):
            z_ref[expert * head : (expert + 1) * head, lanes] = spread[expert]
        dkv_ref[:head, low:high] += nt(queries, score_grad) * 0.125
        dkv_ref[head:, low:high] += nt(upstream, prob_low)
    z_ref[wide : wide + 2 * head, :] = dkv_ref[...].astype(BF)
    grads_ref[...] = nn(z_ref[...], xn_ref[...]).astype(grads_ref.dtype)
    gain = ln_ref[...]
    total = jnp.zeros_like(gain)
    for start in range(0, length, ROWS):
        rows = slice(start, start + ROWS)
        normed_grad = tn(z_ref[:, rows], wcat_ref[...])
        normalized, inverse = normalize(x_ref[rows, :].astype(F32))
        total = total + jnp.sum(normed_grad * normalized, axis=0, keepdims=True)
        back = normalize_back(normed_grad, normalized, inverse, gain)
        dx_ref[rows, :] = (dh_ref[rows, :] + back).astype(BF)
    gain_ref[...] = total


def transposed_weights(w_kv, w_router):
    pad = jnp.zeros((16 - w_router.shape[1], w_router.shape[0]), BF)
    return jnp.concatenate([w_kv.T, w_router.T, pad], axis=0)


def local_prepare(tokens, out_grad, ids, ln, small, experts, pair):
    length, width = tokens.shape
    kernel = functools.partial(prepare_kernel, experts=experts, pair=pair)
    return call(
        kernel,
        (tokens, out_grad, ids, ln, small),
        [
            sds((length, width), BF),
            sds((length, pair), BF),
            sds((pair, length), BF),
            sds(ids.shape, F32),
            sds((width, length), BF),
        ],
        flops=2 * length * width * 2 * pair,
    )


def local_attend(tokens, normed, kv, kvt, ids, sent, gates, wq, wo, ln, experts, head):
    length, width = tokens.shape
    choose = ids.shape[0]
    kernel = functools.partial(attend_kernel, experts=experts, head=head)
    return call(
        kernel,
        (tokens, normed, kv, kvt, ids, sent, gates, wq, wo, ln),
        [
            sds((head, choose * length), BF),
            sds((head, choose * length), BF),
            sds((1, choose * length), F32),
            sds((experts * head, length), BF),
            sds((length, width), F32),
            sds((length, width), BF),
            sds((width, length), BF),
        ],
        scratch=(pltpu.VMEM((experts * head, length), F32), pltpu.VMEM((length, BAND), F32)),
        flops=4 * length * width * experts * head,
    )


def local_ffn(hn, hnt, g, gt, w_in, w_out, chunk, chunks):
    length, width = hn.shape
    hidden = w_in.shape[1] // chunks
    whole = pl.BlockSpec((length, width), lambda i: (0, 0))
    turned = pl.BlockSpec((width, length), lambda i: (0, 0))
    return pl.pallas_call(
        ffn_kernel,
        grid=(1,),
        out_shape=[
            sds((length, hidden), BF),
            sds((length, hidden), BF),
            sds((width, hidden), BF),
            sds((hidden, width), BF),
        ],
        in_specs=[
            whole, turned, whole, turned,
            pl.BlockSpec((width, hidden), lambda i: (0, chunk)),
            pl.BlockSpec((hidden, width), lambda i: (chunk, 0)),
        ],
        out_specs=[
            pl.BlockSpec((length, hidden), lambda i: (0, 0)),
            pl.BlockSpec((length, hidden), lambda i: (0, 0)),
            pl.BlockSpec((width, hidden), lambda i: (0, 0)),
            pl.BlockSpec((hidden, width), lambda i: (0, 0)),
        ],
        compiler_params=pltpu.CompilerParams(vmem_limit_bytes=VMEM_LIMIT),
        cost_estimate=pl.CostEstimate(
            flops=8 * length * width * hidden, bytes_accessed=8 << 20, transcendentals=0
        ),
    )(hn, hnt, g, gt, w_in, w_out)


def local_finish(h, g, us, dpres, w_in, w_out, ln):
    length, width = h.shape
    chunks = len(us)
    hidden = us[0].shape[1]

    def kernel(h_ref, g_ref, *refs):
        u_refs, dpre_refs = refs[:chunks], refs[chunks : 2 * chunks]
        win_ref, wout_ref, ln_ref, out_ref, dh_ref, gain_ref = refs[2 * chunks :]
        value = h_ref[...]
        total, upstream = value, None
        for c in range(chunks):
            total = total + nn(u_refs[c][...], wout_ref[c * hidden : (c + 1) * hidden, :])
            part = nt(dpre_refs[c][...], win_ref[:, c * hidden : (c + 1) * hidden])
            upstream = part if upstream is None else upstream + part
        out_ref[...] = total.astype(BF)
        normalized, inverse = normalize(value)
        dh_ref[...] = g_ref[...].astype(F32) + normalize_back(
            upstream, normalized, inverse, ln_ref[...]
        )

        @pl.when(pl.program_id(0) == 0)
        def _():
            gain_ref[...] = jnp.zeros_like(gain_ref)

        gain_ref[...] += jnp.sum(upstream * normalized, axis=0, keepdims=True)

    row = pl.BlockSpec((ROWS, width), lambda i: (i, 0))
    part = pl.BlockSpec((ROWS, hidden), lambda i: (i, 0))
    fixed = lambda a: pl.BlockSpec(a.shape, lambda i: (0, 0))
    return pl.pallas_call(
        kernel,
        grid=(length // ROWS,),
        out_shape=[sds((length, width), BF), sds((length, width), F32), sds((1, width), F32)],
        in_specs=[row, row] + [part] * (2 * chunks) + [fixed(w_in), fixed(w_out), fixed(ln)],
        out_specs=[row, row, pl.BlockSpec((1, width), lambda i: (0, 0))],
        compiler_params=pltpu.CompilerParams(vmem_limit_bytes=VMEM_LIMIT),
        cost_estimate=pl.CostEstimate(
            flops=4 * length * width * hidden * chunks, bytes_accessed=20 << 20, transcendentals=0
        ),
    )(h, g, *us, *dpres, w_in, w_out, ln)


def local_back(tokens, normed, kv, kvt, ids, sent, gates, wcat, wo, ln, kept, dh, experts, head):
    length, width = tokens.shape
    rows = experts * head + 2 * head + 16
    kernel = functools.partial(back_kernel, experts=experts, head=head)
    qt, at, lse, gat = kept
    return call(
        kernel,
        (tokens, normed, kv, kvt, ids, sent, gates, wcat, wo, ln, qt, at, lse, gat, dh),
        [
            sds((length, width), BF),
            sds((rows, width), BF),
            sds((experts * head, width), BF),
            sds((1, width), F32),
        ],
        scratch=(
            pltpu.VMEM((experts * head, length), F32),
            pltpu.VMEM((length, BAND), F32),
            pltpu.VMEM((rows, length), BF),
            pltpu.VMEM((2 * head, length), F32),
        ),
        flops=8 * length * width * experts * head,
    )


CHUNKS = 4
AXES = ("dp", "expert", "tok")


def body(tokens, out_grad, expert_ids, sentence_ids, ln_attn, w_kv, w_router, w_query, w_output, ln_ffn, w_in, w_out):
    width = tokens.shape[1]
    head = w_query.shape[2]
    pair = w_kv.shape[1]
    experts = lax.axis_size("expert")
    wq = lax.all_gather(w_query[0].T, "expert", axis=0, tiled=True)
    wo = lax.all_gather(w_output[0], "expert", axis=0, tiled=True)
    ids = expert_ids.T
    ln_one = ln_attn.reshape(1, width)
    ln_two = ln_ffn.reshape(1, width)
    small = transposed_weights(w_kv, w_router)
    normed, kv, kvt, gates, gt = local_prepare(tokens, out_grad, ids, ln_one, small, experts, pair)
    qt, at, lse, gat, h, hn, hnt = local_attend(
        tokens, normed, kv, kvt, ids, sentence_ids, gates, wq, wo, ln_two, experts, head
    )
    us, dpres, gins, gouts = [], [], [], []
    for chunk in range(CHUNKS):
        u, dpre, gin, gout = local_ffn(hn, hnt, out_grad, gt, w_in, w_out, chunk, CHUNKS)
        us.append(u)
        dpres.append(dpre)
        gins.append(gin)
        gouts.append(gout)
    output, dh, ln_two_grad = local_finish(h, out_grad, us, dpres, w_in, w_out, ln_two)
    wcat = jnp.concatenate([wq, small], axis=0)
    dx, grads, wo_grad, ln_one_grad = local_back(
        tokens, normed, kv, kvt, ids, sentence_ids, gates, wcat, wo, ln_one, (qt, at, lse, gat), dh, experts, head
    )
    wide = experts * head
    gin, gout, small_grad, gain_grads = lax.psum(
        (
            jnp.concatenate(gins, axis=1),
            jnp.concatenate(gouts, axis=0),
            grads[wide:],
            jnp.concatenate([ln_one_grad, ln_two_grad], axis=0),
        ),
        AXES,
    )
    experts_grad = jnp.concatenate([grads[:wide].reshape(experts, head, width), wo_grad.reshape(experts, head, width)], axis=1)
    own = lax.psum(lax.psum_scatter(experts_grad, "expert", scatter_dimension=0, tiled=True), ("dp", "tok"))[0].astype(F32)
    return (
        output,
        dx,
        gain_grads[0],
        small_grad[:pair].T.astype(F32),
        small_grad[pair : pair + experts].T.astype(F32),
        own[:head].T[None],
        own[head:][None],
        gain_grads[1],
        gin.astype(F32),
        gout.astype(F32),
    )


def solution(mesh):
    rows = P(AXES, None)
    heads = P("expert", None, None)
    return jax.shard_map(
        body,
        mesh=mesh,
        in_specs=(rows, rows, rows, rows, P(), P(), P(), heads, heads, P(), P(), P()),
        out_specs=(rows, rows, P(), P(), P(), heads, heads, P(), P(), P()),
        check_vma=False,
    )
```

```python
import functools

import jax
import jax.numpy as jnp
from jax import lax
from jax.experimental import pallas as pl
from jax.experimental.pallas import tpu as pltpu
from jax.sharding import PartitionSpec as P

BF = jnp.bfloat16
F32 = jnp.float32
MASKED = -1e30
BAND = 128
ROWS = 256
AXES = ("dp", "expert", "tok")


def nn(left, right):
    return lax.dot_general(left, right, (((1,), (0,)), ((), ())), preferred_element_type=F32)


def nt(left, right):
    return lax.dot_general(left, right, (((1,), (1,)), ((), ())), preferred_element_type=F32)


def tn(left, right):
    return lax.dot_general(left, right, (((0,), (0,)), ((), ())), preferred_element_type=F32)


def normalize(values):
    centre = values - jnp.mean(values, axis=-1, keepdims=True)
    spread = jnp.mean(centre * centre, axis=-1, keepdims=True)
    inverse = lax.rsqrt(spread + 1e-05)
    return centre * inverse, inverse


def normalize_back(upstream, normalized, inverse, gain):
    scaled = upstream * gain
    inner = (
        scaled
        - jnp.mean(scaled, axis=-1, keepdims=True)
        - normalized * jnp.mean(scaled * normalized, axis=-1, keepdims=True)
    )
    return inner * inverse


def sds(shape, dtype):
    return jax.ShapeDtypeStruct(shape, dtype)


def size_of(array):
    lanes = -(-array.shape[-1] // 128) * 128
    rows = -(-array.shape[-2] // 16) * 16
    lead = 1
    for extent in array.shape[:-2]:
        lead = lead * extent
    return lead * rows * lanes * jnp.dtype(array.dtype).itemsize


class Line:
    def __init__(self):
        self.last = None

    def call(self, kernel, operands, outs, fetched=(), scalars=(), scratch=(), room=2 << 20, flops=0):
        n, f, s = len(operands), len(fetched), len(scalars)
        late = () if self.last is None else (self.last,)
        skip = len(late)

        def wrapped(*refs):
            ins = refs[:n]
            sources = refs[n : n + f]
            smem = refs[n + f : n + f + s]
            rest = refs[n + f + s + skip :]
            body = rest[: len(rest) - f - (1 if f else 0)] if f else rest
            waits = []
            if f:
                buffers, sems = rest[len(body) : len(body) + f], rest[-1]
                for i in range(f):
                    copy = pltpu.make_async_copy(sources[i], buffers[i], sems.at[i])
                    copy.start()

                    def wait(copy=copy, buffer=buffers[i]):
                        copy.wait()
                        return buffer

                    waits.append(wait)
            kernel(*ins, *waits, *smem, *body)

        need = sum(size_of(a) for a in (*operands, *fetched, *outs)) + sum(
            size_of(a) for a in scratch
        )
        moved = sum(a.size * jnp.dtype(a.dtype).itemsize for a in (*operands, *fetched, *outs))
        extra = [pltpu.VMEM(a.shape, a.dtype) for a in fetched]
        if f:
            extra.append(pltpu.SemaphoreType.DMA((f,)))
        results = pl.pallas_call(
            wrapped,
            out_shape=list(outs),
            in_specs=[pl.BlockSpec(memory_space=pltpu.VMEM)] * n
            + [pl.BlockSpec(memory_space=pltpu.HBM)] * f
            + [pl.BlockSpec(memory_space=pltpu.SMEM)] * s
            + [pl.BlockSpec(memory_space=pl.ANY)] * skip,
            out_specs=[pl.BlockSpec(memory_space=pltpu.VMEM)] * len(outs),
            scratch_shapes=[pltpu.VMEM(a.shape, a.dtype) for a in scratch] + extra,
            compiler_params=pltpu.CompilerParams(vmem_limit_bytes=need + room),
            cost_estimate=pl.CostEstimate(flops=flops, bytes_accessed=moved, transcendentals=0),
        )(*operands, *fetched, *scalars, *late)
        self.last = min(results, key=lambda a: a.size)
        return results


def prepare_kernel(
    x_wait, g_wait, ids_wait, ln_wait, wkv_wait, wr_wait,
    xn_ref, kv_ref, kvt_ref, gates_ref, gt_ref, small_ref,
):
    ln_ref, x_ref = ln_wait(), x_wait()
    length = x_ref.shape[0]
    gain = ln_ref[...]
    for start in range(0, length, ROWS):
        rows = pl.ds(start, ROWS)
        normalized, _ = normalize(x_ref[rows, :].astype(F32))
        xn_ref[rows, :] = (normalized * gain).astype(BF)
    normed = xn_ref[...]
    wkv_ref, wr_ref, ids_ref = wkv_wait(), wr_wait(), ids_wait()
    pair = wkv_ref.shape[1]
    experts = wr_ref.shape[0]
    small_ref[:pair, :] = wkv_ref[...].T
    small_ref[pair:, :] = jnp.concatenate(
        [wr_ref[...].astype(F32), jnp.zeros((16 - experts, wr_ref.shape[1]), F32)], axis=0
    ).astype(BF)
    small = small_ref[...]
    both = nt(small, normed)
    kvt_ref[...] = both[:pair].astype(BF)
    kv_ref[...] = nn(normed, wkv_ref[...]).astype(BF)
    choose = ids_ref.shape[0]
    picked = []
    for route in range(choose):
        ids = ids_ref[route : route + 1, :]
        value = jnp.zeros((1, length), F32)
        for expert in range(experts):
            value = jnp.where(ids == expert, both[pair + expert : pair + expert + 1], value)
        picked.append(value)
    top = functools.reduce(jnp.maximum, picked)
    raised = [jnp.exp(value - top) for value in picked]
    total = functools.reduce(lambda a, b: a + b, raised)
    for route in range(choose):
        gates_ref[route : route + 1, :] = raised[route] / total
    g_ref = g_wait()
    gt_ref[...] = g_ref[...].T


def upstream_kernel(g_ref, wout_ref, ag_ref):
    for start in range(0, g_ref.shape[0], ROWS):
        rows = slice(start, start + ROWS)
        ag_ref[rows, :] = nt(g_ref[rows, :], wout_ref[...]).astype(BF)


def column_ids(sent_ref, keyid_ref):
    length = sent_ref.shape[1]
    for start in range(0, length, BAND):
        row = jnp.broadcast_to(sent_ref[:, start : start + BAND].astype(F32), (BAND, BAND))
        keyid_ref[pl.ds(start, BAND), :] = row.T


def masked_scores(kv_ref, keyid_ref, sent_ref, queries, start, low, high, choose):
    padded = jnp.concatenate([queries, jnp.zeros_like(queries)], axis=0)
    scores = nn(kv_ref[low:high, :], padded) * 0.125
    same = keyid_ref[low:high, :] == sent_ref[:, start : start + BAND].astype(F32)
    parts = [
        jnp.where(same, scores[:, route * BAND : (route + 1) * BAND], MASKED)
        for route in range(choose)
    ]
    return jnp.concatenate(parts, axis=1)


def window(start, length):
    return max(start - BAND, 0), min(start + 2 * BAND, length)


def attend_kernel(*refs, experts, head):
    piece_refs, refs = refs[:experts], refs[experts:]
    (
        xn_ref, kv_ref, kvt_ref, gates_ref, x_wait, ids_wait, sent_wait, ln_wait, place_ref,
        wq_ref, wo_ref, qt_ref, at_ref, lse_ref, gat_ref, h_ref, hn_ref, hnt_ref, all_ref, keyid_ref,
    ) = refs
    for k in range(experts):
        rows = pl.ds((place_ref[1] ^ k) * head, head)
        wq_ref[rows, :] = piece_refs[k][:head, :]
        wo_ref[rows, :] = piece_refs[k][head:, :]
    length = xn_ref.shape[0]
    sent_ref, ids_ref = sent_wait(), ids_wait()
    choose = ids_ref.shape[0]
    column_ids(sent_ref, keyid_ref)
    all_ref[...] = nt(wq_ref[...], xn_ref[...])
    for start in range(0, length, BAND):
        lanes = slice(start, start + BAND)
        block = slice(start * choose, (start + BAND) * choose)
        low, high = window(start, length)
        chosen = []
        for route in range(choose):
            ids = ids_ref[route : route + 1, lanes]
            value = jnp.zeros((head, BAND), F32)
            for expert in range(experts):
                value = jnp.where(
                    ids == expert, all_ref[expert * head : (expert + 1) * head, lanes], value
                )
            chosen.append(value)
        queries = jnp.concatenate(chosen, axis=1).astype(BF)
        qt_ref[:, block] = queries
        scores = masked_scores(kv_ref, keyid_ref, sent_ref, queries, start, low, high, choose)
        largest = jnp.max(scores, axis=0, keepdims=True)
        raised = jnp.exp(scores - largest)
        total = jnp.sum(raised, axis=0, keepdims=True)
        probs = (raised * (1.0 / total)).astype(BF)
        lse_ref[:, block] = largest + jnp.log(total)
        attended = nn(kvt_ref[head:, low:high], probs).astype(BF)
        at_ref[:, block] = attended
        spread = [jnp.zeros((head, BAND), F32) for _ in range(experts)]
        for route in range(choose):
            ids = ids_ref[route : route + 1, lanes]
            gated = attended[:, route * BAND : (route + 1) * BAND].astype(F32) * gates_ref[
                route : route + 1, lanes
            ]
            for expert in range(experts):
                spread[expert] = jnp.where(ids == expert, gated, spread[expert])
        for expert in range(experts):
            gat_ref[expert * head : (expert + 1) * head, lanes] = spread[expert].astype(BF)
    x_ref, ln_ref = x_wait(), ln_wait()
    gain = ln_ref[...]
    for start in range(0, length, ROWS):
        rows = slice(start, start + ROWS)
        mixed = tn(gat_ref[:, rows], wo_ref[...])
        hidden = x_ref[rows, :].astype(F32) + mixed
        h_ref[rows, :] = hidden
        normalized, _ = normalize(hidden)
        low_value = (normalized * gain).astype(BF)
        hn_ref[rows, :] = low_value
        hnt_ref[:, rows] = low_value.T


def gelu_both(values):
    bell = jnp.exp(-0.5 * values * values)
    t = 1.0 / (1.0 + 0.23164188 * jnp.abs(values))
    poly = t * (
        0.127414796
        + t * (-0.142248368 + t * (0.7107068705 + t * (-0.7265760135 + t * 0.5307027145)))
    )
    tail = poly * bell
    cumulative = jnp.where(values >= 0.0, 1.0 - tail, tail)
    return values * cumulative, cumulative + values * bell * 0.3989422804014327


def ffn_kernel(*refs, first, hidden, peers):
    hn_ref, hnt_ref, gt_ref, ag_ref, win_ref, place_ref, u_ref, dpre_ref = refs[:8]
    part_refs, sum_ref = refs[8 : 8 + peers], refs[8 + peers]
    length, width = hn_ref.shape
    for column in range(0, hidden, width):
        span = slice(column, column + width)
        far = slice(first + column, first + column + width)
        for start in range(0, length, ROWS):
            rows = slice(start, start + ROWS)
            activated, slope = gelu_both(nn(hn_ref[rows, :], win_ref[:, far]))
            u_ref[rows, span] = activated.astype(BF)
            dpre_ref[rows, span] = (ag_ref[rows, far].astype(F32) * slope).astype(BF)
        sum_ref[hidden + column : hidden + column + width, :] = nn(
            hnt_ref[...], dpre_ref[:, span]
        ).astype(BF)
        sum_ref[span, :] = nn(gt_ref[...], u_ref[:, span]).astype(BF).T
    rows = 2 * hidden // peers
    for k in range(peers):
        part_refs[k][...] = sum_ref[pl.ds((place_ref[0] ^ k) * rows, rows), :]


def finish_kernel(*refs, chunks):
    h_ref, g_ref, win_ref, wout_ref = refs[:4]
    u_refs, dpre_refs = refs[4 : 4 + chunks], refs[4 + chunks : 4 + 2 * chunks]
    ln_wait, out_ref, dh_ref, gain_ref = refs[4 + 2 * chunks :]
    ln_ref = ln_wait()
    gain = ln_ref[...]
    length = h_ref.shape[0]
    gain_sum = jnp.zeros_like(gain)
    for start in range(0, length, ROWS):
        rows = slice(start, start + ROWS)
        hidden = h_ref[rows, :]
        total, upstream, first = hidden, None, 0
        for c in range(chunks):
            size = u_refs[c].shape[1]
            total = total + nn(u_refs[c][rows, :], wout_ref[first : first + size, :])
            part = nt(dpre_refs[c][rows, :], win_ref[:, first : first + size])
            upstream = part if upstream is None else upstream + part
            first = first + size
        out_ref[rows, :] = total.astype(BF)
        normalized, inverse = normalize(hidden)
        dh_ref[rows, :] = g_ref[rows, :].astype(F32) + normalize_back(
            upstream, normalized, inverse, gain
        )
        gain_sum = gain_sum + jnp.sum(upstream * normalized, axis=0, keepdims=True)
    gain_ref[...] = gain_sum


def back_kernel(*refs, experts, head, peers, misc):
    (
        xn_ref, kv_ref, kvt_ref, gates_ref, small_ref, wq_ref, wo_ref, qt_ref, at_ref, lse_ref, gat_ref,
        dh_ref, gain_two_ref, x_wait, ids_wait, sent_wait, ln_wait, place_ref, dx_ref,
    ) = refs[:19]
    part_refs = refs[19 : 19 + peers]
    all_ref, keyid_ref, z_ref, dkv_ref, grads_ref, pair_ref, misc_ref = refs[19 + peers :]
    length = xn_ref.shape[0]
    wide, pair = experts * head, 2 * head
    sent_ref, ids_ref = sent_wait(), ids_wait()
    choose = ids_ref.shape[0]
    column_ids(sent_ref, keyid_ref)
    dh_low = dh_ref[...].astype(BF)
    all_ref[...] = nt(wo_ref[...], dh_low)
    out_grads = nn(gat_ref[...], dh_low)
    for expert in range(experts):
        pair_ref[expert * pair + head : (expert + 1) * pair, :] = out_grads[
            expert * head : (expert + 1) * head
        ]
    dkv_ref[...] = jnp.zeros_like(dkv_ref)
    for start in range(0, length, BAND):
        lanes = slice(start, start + BAND)
        block = slice(start * choose, (start + BAND) * choose)
        low, high = window(start, length)
        raw, gate_grads = [], []
        for route in range(choose):
            ids = ids_ref[route : route + 1, lanes]
            value = jnp.zeros((head, BAND), F32)
            for expert in range(experts):
                value = jnp.where(
                    ids == expert, all_ref[expert * head : (expert + 1) * head, lanes], value
                )
            raw.append(value)
            attended = at_ref[:, start * choose + route * BAND : start * choose + (route + 1) * BAND]
            gate_grads.append(jnp.sum(value * attended.astype(F32), axis=0, keepdims=True))
        gates = [gates_ref[route : route + 1, lanes] for route in range(choose)]
        common = functools.reduce(
            lambda a, b: a + b, [gate * grad for gate, grad in zip(gates, gate_grads)]
        )
        logit_rows = [jnp.zeros((1, BAND), F32) for _ in range(experts)]
        for route in range(choose):
            ids = ids_ref[route : route + 1, lanes]
            picked = gates[route] * (gate_grads[route] - common)
            for expert in range(experts):
                logit_rows[expert] = jnp.where(ids == expert, picked, logit_rows[expert])
        logit_pad = jnp.concatenate(
            logit_rows + [jnp.zeros((16 - experts, BAND), F32)], axis=0
        )
        z_ref[wide + pair :, lanes] = logit_pad.astype(BF)
        queries = qt_ref[:, block]
        scores = masked_scores(kv_ref, keyid_ref, sent_ref, queries, start, low, high, choose)
        probs = jnp.exp(scores - lse_ref[:, block])
        upstream = jnp.concatenate(
            [gate * value for gate, value in zip(gates, raw)], axis=1
        ).astype(BF)
        padded = jnp.concatenate([jnp.zeros_like(upstream), upstream], axis=0)
        prob_grad = nn(kv_ref[low:high, :], padded)
        mean = jnp.sum(probs * prob_grad, axis=0, keepdims=True)
        score_grad = (probs * (prob_grad - mean)).astype(BF)
        query_grad = (nn(kvt_ref[:head, low:high], score_grad) * 0.125).astype(BF)
        spread = [jnp.zeros((head, BAND), BF) for _ in range(experts)]
        for route in range(choose):
            ids = ids_ref[route : route + 1, lanes]
            piece = query_grad[:, route * BAND : (route + 1) * BAND]
            for expert in range(experts):
                spread[expert] = jnp.where(ids == expert, piece, spread[expert])
        for expert in range(experts):
            z_ref[expert * head : (expert + 1) * head, lanes] = spread[expert]
        dkv_ref[:head, low:high] += nt(queries, score_grad) * 0.125
        dkv_ref[head:, low:high] += nt(upstream, probs.astype(BF))
    z_ref[wide : wide + pair, :] = dkv_ref[...].astype(BF)
    grads_ref[...] = nn(z_ref[...], xn_ref[...])
    for expert in range(experts):
        pair_ref[expert * pair : expert * pair + head, :] = grads_ref[
            expert * head : (expert + 1) * head, :
        ]
    x_ref, ln_ref = x_wait(), ln_wait()
    gain = ln_ref[...]
    total = jnp.zeros_like(gain)
    for start in range(0, length, ROWS):
        rows = slice(start, start + ROWS)
        normed_grad = tn(z_ref[:wide, rows], wq_ref[...]) + tn(z_ref[wide:, rows], small_ref[...])
        normalized, inverse = normalize(x_ref[rows, :].astype(F32))
        total = total + jnp.sum(normed_grad * normalized, axis=0, keepdims=True)
        back = normalize_back(normed_grad, normalized, inverse, gain)
        dx_ref[rows, :] = (dh_ref[rows, :] + back).astype(BF)
    misc_ref[...] = jnp.zeros_like(misc_ref)
    misc_ref[:pair, :] = grads_ref[wide : wide + pair, :]
    misc_ref[pair : pair + 16, :] = jnp.concatenate(
        [
            grads_ref[wide + pair : wide + pair + experts, :],
            total,
            gain_two_ref[...],
            jnp.zeros((14 - experts, total.shape[1]), F32),
        ],
        axis=0,
    )
    each, share = pair // peers, misc // peers
    for k in range(peers):
        part = place_ref[0] ^ k
        for expert in range(experts):
            rows = pl.ds(expert * pair + part * each, each)
            part_refs[k][expert * each : (expert + 1) * each, :] = pair_ref[rows, :].astype(BF)
        part_refs[k][experts * each :, :] = misc_ref[pl.ds(part * share, share), :].astype(BF)


def added(refs, span):
    total = refs[0][span, :].astype(F32)
    for ref in refs[1:]:
        total = total + ref[span, :].astype(F32)
    return total.astype(BF)


def exchange(parts, axis):
    size = len(parts)
    return [
        lax.ppermute(parts[k], axis, [(i, i ^ k) for i in range(size)]) for k in range(1, size)
    ]


def bits(size):
    return size.bit_length() - 1


def dp_bit(stage, parity):
    count = bits(lax.axis_size("dp"))
    return (stage + parity) % count


def swap_dp(array, stage):
    dp, expert, tok = (lax.axis_size(axis) for axis in AXES)
    pairs = []
    for d in range(dp):
        for e in range(expert):
            for t in range(tok):
                other = d ^ (1 << dp_bit(stage, t % 2))
                pairs.append(((d * expert + e) * tok + t, (other * expert + e) * tok + t))
    return lax.ppermute(array, AXES, pairs)


def swap_expert(array, stage):
    size = lax.axis_size("expert")
    return lax.ppermute(array, "expert", [(i, i ^ (1 << stage)) for i in range(size)])


def split_step(line, place, arrays, row):
    rows, width = arrays[0].shape
    half, count = rows // 2, len(arrays)

    def kernel(*refs):
        place_ref, keep_ref, send_ref = refs[count:]
        bit = place_ref[row]
        keep_ref[...] = added(refs[:count], pl.ds(bit * half, half))
        send_ref[...] = added(refs[:count], pl.ds((1 - bit) * half, half))

    return line.call(kernel, arrays, [sds((half, width), BF)] * 2, scalars=(place,))


def add_step(line, arrays):
    count = len(arrays)

    def kernel(*refs):
        refs[count][...] = added(refs[:count], slice(None))

    return line.call(kernel, arrays, [sds(arrays[0].shape, BF)])[0]


def join_step(line, place, own, other, row):
    half, width = own.shape

    def kernel(own_ref, other_ref, place_ref, out_ref):
        bit = place_ref[row]
        out_ref[pl.ds(bit * half, half), :] = own_ref[...]
        out_ref[pl.ds((1 - bit) * half, half), :] = other_ref[...]

    return line.call(kernel, (own, other), [sds((2 * half, width), BF)], scalars=(place,))[0]


def tail_step(line, place, arrays, row, count, each):
    rows, width = arrays[0].shape
    rest = rows - count * each
    half, many = count // 2 * each, len(arrays)

    def kernel(*refs):
        place_ref, keep_ref, send_ref = refs[many:]
        bit = place_ref[row]
        for q in range(count // 2):
            span = slice(q * each, (q + 1) * each)
            keep_ref[span, :] = added(refs[:many], pl.ds((2 * q + bit) * each, each))
            send_ref[span, :] = added(refs[:many], pl.ds((2 * q + 1 - bit) * each, each))
        small = added(refs[:many], slice(count * each, rows))
        keep_ref[half:, :] = small
        send_ref[half:, :] = small

    return line.call(kernel, arrays, [sds((half + rest, width), BF)] * 2, scalars=(place,))


def chunk_steps(line, place, parts):
    arrays = [parts[0]] + exchange(parts, "tok")
    yield
    stages = bits(lax.axis_size("dp"))
    for stage in range(stages):
        keep, send = split_step(line, place, arrays, 2 + stage)
        arrays = [keep, swap_dp(send, stage)]
        yield
    for stage in range(bits(lax.axis_size("expert"))):
        own = add_step(line, arrays)
        arrays = [own, swap_expert(own, stage)]
        yield
    own = add_step(line, arrays)
    for stage in reversed(range(stages)):
        other = swap_dp(own, stage)
        yield
        own = join_step(line, place, own, other, 2 + stage)
    others = exchange([own] * lax.axis_size("tok"), "tok")
    yield
    return [own] + others


def place_chunk(line, place, parts, first, hidden, full, before):
    peers = len(parts)
    rows, width = parts[0].shape
    block = width

    def kernel(*refs):
        part_refs, place_ref = refs[:peers], refs[peers]
        gin_ref, gout_ref, sum_ref = refs[-3:]
        for k in range(peers):
            sum_ref[pl.ds((place_ref[0] ^ k) * rows, rows), :] = part_refs[k][...]
        for column in range(0, hidden, block):
            span = slice(column, column + block)
            gout_ref[span, :] = sum_ref[span, :].astype(F32)
            gin_ref[:, span] = sum_ref[hidden + column : hidden + column + block, :].astype(F32)

    late = () if line.last is None else (line.last,)
    operands = [*parts, place, *late, *before]
    base = peers + 1 + len(late)
    results = pl.pallas_call(
        kernel,
        grid=(1,),
        out_shape=[sds((width, full), F32), sds((full, width), F32)],
        in_specs=[pl.BlockSpec((rows, width), lambda i: (0, 0), pipeline_mode=pl.Buffered(1))] * peers
        + [pl.BlockSpec(memory_space=pltpu.SMEM)]
        + [pl.BlockSpec(memory_space=pl.ANY)] * (len(late) + len(before)),
        out_specs=[
            pl.BlockSpec((width, hidden), lambda i: (0, first // hidden), pipeline_mode=pl.Buffered(1)),
            pl.BlockSpec((hidden, width), lambda i: (first // hidden, 0), pipeline_mode=pl.Buffered(1)),
        ],
        scratch_shapes=[pltpu.VMEM((2 * hidden, width), BF)],
        input_output_aliases={base + n: n for n in range(len(before))},
        compiler_params=pltpu.CompilerParams(vmem_limit_bytes=20 << 20),
        cost_estimate=pl.CostEstimate(flops=0, bytes_accessed=6 << 20, transcendentals=0),
    )(*operands)
    return results


def tail_steps(line, place, parts, experts, head, misc):
    peers = len(parts)
    pair = 2 * head
    each, share = pair // peers, misc // peers
    width = parts[0].shape[1]
    arrays = [parts[0]] + exchange(parts, "tok")
    yield
    stages = bits(lax.axis_size("dp"))
    for stage in range(bits(experts)):
        keep, send = tail_step(line, place, arrays, 2 + stages + stage, experts >> stage, each)
        arrays = [keep, swap_expert(send, stage)]
        yield
    for stage in range(stages):
        own = add_step(line, arrays)
        arrays = [own, swap_dp(own, stage)]
        yield
    own = add_step(line, arrays)
    arrays = [own] + exchange([own] * peers, "tok")
    yield

    def last(*refs):
        part_refs, place_ref = refs[:peers], refs[peers]
        query_ref, output_ref, kv_ref, router_ref, one_ref, two_ref, pair_ref, misc_ref = refs[
            peers + 1 :
        ]
        for k in range(peers):
            part = place_ref[0] ^ k
            pair_ref[pl.ds(part * each, each), :] = part_refs[k][:each, :].astype(F32)
            misc_ref[pl.ds(part * share, share), :] = part_refs[k][each:, :].astype(F32)
        query_ref[0] = pair_ref[:head, :]
        output_ref[0] = pair_ref[head:, :]
        kv_ref[...] = misc_ref[:pair, :].T
        router_ref[...] = misc_ref[pair : pair + experts, :]
        one_ref[...] = misc_ref[pair + experts : pair + experts + 1, :]
        two_ref[...] = misc_ref[pair + experts + 1 : pair + experts + 2, :]

    return line.call(
        last,
        arrays,
        [
            sds((1, head, width), F32),
            sds((1, head, width), F32),
            sds((width, pair), F32),
            sds((experts, width), F32),
            sds((1, width), F32),
            sds((1, width), F32),
        ],
        scalars=(place,),
        scratch=(sds((pair, width), F32), sds((misc, width), F32)),
    )


def step(walk):
    try:
        next(walk)
    except StopIteration as end:
        return end.value
    return None


def body(
    tokens, out_grad, expert_ids, sentence_ids, ln_attn, w_kv, w_router, w_query, w_output, ln_ffn, w_in, w_out
):
    length, width = tokens.shape
    head = w_query.shape[2]
    pair = w_kv.shape[1]
    full = w_in.shape[1]
    experts = lax.axis_size("expert")
    peers = lax.axis_size("tok")
    choose = expert_ids.shape[1]
    tok, dp, expert = lax.axis_index("tok"), lax.axis_index("dp"), lax.axis_index("expert")
    odd = tok % 2
    stages = bits(lax.axis_size("dp"))
    dp_bits = [
        jnp.where(odd == 1, (dp >> dp_bit(s, 1)) & 1, (dp >> dp_bit(s, 0)) & 1) for s in range(stages)
    ]
    place = jnp.stack(
        [tok, expert] + dp_bits + [(expert >> s) & 1 for s in range(bits(experts))]
    ).astype(jnp.int32)
    weights = jnp.concatenate([w_query[0].T, w_output[0]], axis=0)
    pieces = [weights] + exchange([weights] * experts, "expert")
    ids = expert_ids.T
    ln_one = ln_attn.reshape(1, width)
    ln_two = ln_ffn.reshape(1, width)
    line = Line()
    normed, kv, kvt, gates, gt, small = line.call(
        prepare_kernel,
        (),
        [
            sds((length, width), BF),
            sds((length, pair), BF),
            sds((pair, length), BF),
            sds((choose, length), F32),
            sds((width, length), BF),
            sds((pair + 16, width), BF),
        ],
        fetched=(tokens, out_grad, ids, ln_one, w_kv, w_router.T),
        room=8 << 20,
        flops=4 * length * width * pair,
    )
    [ag] = line.call(
        upstream_kernel, (out_grad, w_out), [sds((length, full), BF)], room=8 << 20,
        flops=2 * length * width * full,
    )
    wq, wo, qt, at, lse, gat, h, hn, hnt = line.call(
        functools.partial(attend_kernel, experts=experts, head=head),
        (*pieces, normed, kv, kvt, gates),
        [
            sds((experts * head, width), BF),
            sds((experts * head, width), BF),
            sds((head, choose * length), BF),
            sds((head, choose * length), BF),
            sds((1, choose * length), F32),
            sds((experts * head, length), BF),
            sds((length, width), F32),
            sds((length, width), BF),
            sds((width, length), BF),
        ],
        fetched=(tokens, ids, sentence_ids, ln_two),
        scalars=(place,),
        scratch=(sds((experts * head, length), F32), sds((length, BAND), F32)),
        room=8 << 20,
        flops=8 * length * width * experts * head,
    )

    def ffn(first, hidden):
        u, dpre, *parts = line.call(
            functools.partial(ffn_kernel, first=first, hidden=hidden, peers=peers),
            (hn, hnt, gt, ag, w_in),
            [sds((length, hidden), BF)] * 2 + [sds((2 * hidden // peers, width), BF)] * peers,
            scalars=(place,),
            scratch=(sds((2 * hidden, width), BF),),
            room=8 << 20,
            flops=6 * length * width * hidden,
        )
        return u, dpre, chunk_steps(line, place, parts)

    half = full // 2
    u_one, dpre_one, walk_one = ffn(0, half)
    step(walk_one)
    u_two, dpre_two, walk_two = ffn(half, half)
    step(walk_one)
    step(walk_two)
    output, dh, gain_two = line.call(
        functools.partial(finish_kernel, chunks=2),
        (h, out_grad, w_in, w_out, u_one, u_two, dpre_one, dpre_two),
        [sds((length, width), BF), sds((length, width), F32), sds((1, width), F32)],
        fetched=(ln_two,),
        room=8 << 20,
        flops=4 * length * width * full,
    )
    step(walk_one)
    step(walk_two)
    misc = -(-(pair + 16) // (16 * peers)) * 16 * peers
    dx, *parts = line.call(
        functools.partial(back_kernel, experts=experts, head=head, peers=peers, misc=misc),
        (normed, kv, kvt, gates, small, wq, wo, qt, at, lse, gat, dh, gain_two),
        [sds((length, width), BF)] + [sds(((experts * pair + misc) // peers, width), BF)] * peers,
        fetched=(tokens, ids, sentence_ids, ln_one),
        scalars=(place,),
        scratch=(
            sds((experts * head, length), F32),
            sds((length, BAND), F32),
            sds((experts * head + pair + 16, length), BF),
            sds((pair, length), F32),
            sds((experts * head + pair + 16, width), F32),
            sds((experts * pair, width), F32),
            sds((misc, width), F32),
        ),
        room=8 << 20,
        flops=12 * length * width * experts * head,
    )
    walk_three = tail_steps(line, place, parts, experts, head, misc)
    step(walk_three)
    walks = {1: walk_one, 2: walk_two, 3: walk_three}
    done = {}
    while walks:
        for name in list(walks):
            result = step(walks[name])
            if result is not None:
                done[name] = result
                del walks[name]
    query, outp, kv_grad, router, one, two = done[3]
    both = place_chunk(line, place, done[1], 0, half, full, ())
    both = place_chunk(line, place, done[2], half, half, full, both)
    return (
        output,
        dx,
        one.reshape(width),
        kv_grad,
        router.T,
        jnp.swapaxes(query, 1, 2),
        outp,
        two.reshape(width),
        both[0],
        both[1],
    )


def solution(mesh):
    rows = P(AXES, None)
    heads = P("expert", None, None)
    return jax.shard_map(
        body,
        mesh=mesh,
        in_specs=(rows, rows, rows, rows, P(), P(), P(), heads, heads, P(), P(), P()),
        out_specs=(rows, rows, P(), P(), P(), heads, heads, P(), P(), P()),
        check_vma=False,
    )
```

```python
import functools

import jax
import jax.numpy as jnp
from jax import lax
from jax.experimental import pallas as pl
from jax.experimental.pallas import tpu as pltpu
from jax.sharding import PartitionSpec as P

BF = jnp.bfloat16
F32 = jnp.float32
MASKED = -1e30
BAND = 128
ROWS = 256
PIECE = 256
AXES = ("dp", "expert", "tok")
GLUE = 23 * 10**9
COPIES = 8
WORK = 1
ORDER = (
    "f", "A", "f", "a", "B", "ab", "n", "h", "a", "b", "r", "a", "t", "b", "t", "a", "b", "o", "t",
    "a", "b", "t", "a", "bt", "a", "P", "bt", "p", "bt", "Q", "T", "q",
)


def nn(left, right):
    return lax.dot_general(left, right, (((1,), (0,)), ((), ())), preferred_element_type=F32)


def nt(left, right):
    return lax.dot_general(left, right, (((1,), (1,)), ((), ())), preferred_element_type=F32)


def tn(left, right):
    return lax.dot_general(left, right, (((0,), (0,)), ((), ())), preferred_element_type=F32)


def normalize(values):
    centre = values - jnp.mean(values, axis=-1, keepdims=True)
    spread = jnp.mean(centre * centre, axis=-1, keepdims=True)
    inverse = lax.rsqrt(spread + 1e-05)
    return centre * inverse, inverse


def normalize_back(upstream, normalized, inverse, gain):
    scaled = upstream * gain
    inner = (
        scaled
        - jnp.mean(scaled, axis=-1, keepdims=True)
        - normalized * jnp.mean(scaled * normalized, axis=-1, keepdims=True)
    )
    return inner * inverse


def sds(shape, dtype):
    return jax.ShapeDtypeStruct(shape, dtype)


def size_of(array):
    lanes = -(-array.shape[-1] // 128) * 128
    rows = -(-array.shape[-2] // 16) * 16
    lead = 1
    for extent in array.shape[:-2]:
        lead = lead * extent
    return lead * rows * lanes * jnp.dtype(array.dtype).itemsize


class Place:
    def __init__(self, ref):
        self.ref = ref

    def __getitem__(self, row):
        return self.ref[row, 0]


class Line:
    def __init__(self):
        self.last = None

    def call(
        self, kernel, operands, outs, fetched=(), scalars=(), scratch=(), room=2 << 20, weight=WORK,
        sent=(), aliased=(), kept=(), numbers=(),
    ):
        n, f, s = len(operands), len(fetched) + len(kept), len(scalars)
        late = () if self.last is None else (self.last,)
        skip = len(late) + len(aliased)
        outs = list(outs)
        h = len(sent)
        if not outs:
            outs = [sds((8, 128), F32)]
        outs = outs + [sds(a.shape, a.dtype) for a in kept]
        scratch_copies, fetched = len(fetched), (*fetched, *kept)

        def wrapped(*refs):
            ins = refs[:n]
            sources = refs[n : n + f]
            smem = [Place(ref) for ref in refs[n + f : n + f + s]] + list(
                refs[n + f + s : n + f + s + len(numbers)]
            )
            rest = list(refs[n + f + s + len(numbers) + skip :])
            far = rest[len(outs) : len(outs) + h]
            del rest[len(outs) : len(outs) + h]
            open_copies, send_sem = [], rest.pop() if h else None
            sems = rest.pop() if f else None
            buffers = rest[len(rest) - scratch_copies :] if scratch_copies else []
            del rest[len(rest) - scratch_copies :]
            first = len(outs) - len(kept)
            buffers = buffers + rest[first : len(outs)]
            del rest[first : len(outs)]
            body, waits, waiting = rest, [], {}
            for i in range(f):
                copy = pltpu.make_async_copy(sources[i], buffers[i], sems.at[i])
                copy.start()
                waiting[i] = copy

                def wait(i=i):
                    if i in waiting:
                        waiting.pop(i).wait()
                    return buffers[i]

                waits.append(wait)
            def send(source, target, other=None, near=None):
                sem = send_sem.at[len(open_copies)]
                copy = pltpu.make_async_copy(source, target, sem)
                open_copies.append(copy)
                if other is None:
                    copy.start()
                    return
                pl.when(near)(copy.start)
                pl.when(jnp.logical_not(near))(pltpu.make_async_copy(source, other, sem).start)

            if h:
                kernel(*ins, *waits, *smem, *body, send, *far)
                for copy in open_copies:
                    copy.wait()
            else:
                kernel(*ins, *waits, *smem, *body)
            for copy in waiting.values():
                copy.wait()

        need = sum(size_of(a) for a in (*fetched[:scratch_copies], *scratch))
        extra = [pltpu.VMEM(a.shape, a.dtype) for a in fetched[:scratch_copies]]
        if f:
            extra.append(pltpu.SemaphoreType.DMA((f,)))
        if h:
            extra.append(pltpu.SemaphoreType.DMA((COPIES,)))
        results = pl.pallas_call(
            wrapped,
            out_shape=outs + list(sent),
            in_specs=[pl.BlockSpec(memory_space=pltpu.VMEM)] * n
            + [pl.BlockSpec(memory_space=pltpu.HBM)] * f
            + [pl.BlockSpec(memory_space=pltpu.VMEM)] * s
            + [pl.BlockSpec(memory_space=pltpu.SMEM)] * len(numbers)
            + [pl.BlockSpec(memory_space=pl.ANY)] * skip,
            out_specs=[pl.BlockSpec(memory_space=pltpu.VMEM)] * len(outs)
            + [pl.BlockSpec(memory_space=pltpu.HBM)] * h,
            input_output_aliases={
                n + f + s + len(numbers) + len(late) + i: len(outs) + i for i in range(len(aliased))
            },
            scratch_shapes=[pltpu.VMEM(a.shape, a.dtype) for a in scratch] + extra,
            compiler_params=pltpu.CompilerParams(vmem_limit_bytes=need + room),
            cost_estimate=pl.CostEstimate(flops=weight, bytes_accessed=1024, transcendentals=0),
        )(
            *operands,
            *[pltpu.with_memory_space_constraint(a, pltpu.HBM) for a in fetched],
            *scalars,
            *numbers,
            *late,
            *aliased,
        )
        self.last = min(results[: len(outs)], key=lambda a: a.size)
        return results


def prepare_kernel(
    ln_wait, wkv_wait, wr_wait, sent_wait, ln_two_wait, x_wait, g_wait, ids_wait, win_wait, wout_wait,
    wq_wait, wo_wait, spots_ref, xn_ref, kv_ref, kvt_ref, gates_ref, gt_ref, small_ref, sent_keep, gains_keep, keyid_ref,
    place_ref,
):
    for i in range(spots_ref.shape[0]):
        place_ref[i : i + 1, :] = jnp.full((1, place_ref.shape[1]), spots_ref[i], jnp.int32)
    ln_ref, x_ref = ln_wait(), x_wait()
    length = x_ref.shape[0]
    gain = ln_ref[...]
    gains_keep[0:1, :] = gain
    for start in range(0, length, ROWS):
        rows = pl.ds(start, ROWS)
        normalized, _ = normalize(x_ref[rows, :].astype(F32))
        xn_ref[rows, :] = (normalized * gain).astype(BF)
    normed = xn_ref[...]
    wkv_ref, wr_ref, ids_ref = wkv_wait(), wr_wait(), ids_wait()
    pair = wkv_ref.shape[1]
    experts = wr_ref.shape[0]
    small_ref[:pair, :] = wkv_ref[...].T
    small_ref[pair:, :] = jnp.concatenate(
        [wr_ref[...].astype(F32), jnp.zeros((16 - experts, wr_ref.shape[1]), F32)], axis=0
    ).astype(BF)
    small = small_ref[...]
    both = nt(small, normed)
    kvt_ref[...] = both[:pair].astype(BF)
    kv_ref[...] = nn(normed, wkv_ref[...]).astype(BF)
    choose = ids_ref.shape[0]
    picked = []
    for route in range(choose):
        ids = ids_ref[route : route + 1, :]
        value = jnp.zeros((1, length), F32)
        for expert in range(experts):
            value = jnp.where(ids == expert, both[pair + expert : pair + expert + 1], value)
        picked.append(value)
    top = functools.reduce(jnp.maximum, picked)
    raised = [jnp.exp(value - top) for value in picked]
    total = functools.reduce(lambda a, b: a + b, raised)
    for route in range(choose):
        gates_ref[route : route + 1, :] = raised[route] / total
    gains_keep[1:2, :] = ln_two_wait()[...]
    sent_ref = sent_wait()
    sent_keep[...] = sent_ref[...].astype(F32)
    column_ids(sent_keep, keyid_ref)
    g_ref = g_wait()
    gt_ref[...] = g_ref[...].T


def upstream_kernel(g_ref, wout_ref, ag_ref):
    for start in range(0, g_ref.shape[0], ROWS):
        rows = slice(start, start + ROWS)
        ag_ref[rows, :] = nt(g_ref[rows, :], wout_ref[...]).astype(BF)


def column_ids(sent_ref, keyid_ref):
    length = sent_ref.shape[1]
    for start in range(0, length, BAND):
        row = jnp.broadcast_to(sent_ref[:, start : start + BAND], (BAND, BAND))
        keyid_ref[pl.ds(start, BAND), :] = row.T


def masked_scores(kv_ref, keyid_ref, sent_ref, queries, start, low, high, choose):
    padded = jnp.concatenate([queries, jnp.zeros_like(queries)], axis=0)
    scores = nn(kv_ref[low:high, :], padded) * 0.125
    same = keyid_ref[low:high, :] == sent_ref[:, start : start + BAND]
    parts = [
        jnp.where(same, scores[:, route * BAND : (route + 1) * BAND], MASKED)
        for route in range(choose)
    ]
    return jnp.concatenate(parts, axis=1)


def window(start, length):
    return max(start - BAND, 0), min(start + 2 * BAND, length)


def attend_kernel(*refs, experts, head, peers):
    slab_refs, refs = refs[:peers], refs[peers:]
    (
        xn_ref, kv_ref, kvt_ref, gates_ref, x_ref, ids_ref, sent_ref, ln_ref, keyid_ref, wq_own, wo_own,
        place_ref, wq_ref, wo_ref, qt_ref, at_ref, lse_ref, gat_ref, h_ref, hn_ref, hnt_ref, all_ref,
        pair_ref,
    ) = refs
    own = place_ref[1]
    each = 2 * head // peers
    wq_ref[pl.ds(own * head, head), :] = wq_own[...]
    wo_ref[pl.ds(own * head, head), :] = wo_own[...]
    for k in range(1, experts):
        for j in range(peers):
            rows = pl.ds((place_ref[0] ^ j) * each, each)
            pair_ref[rows, :] = slab_refs[j][(k - 1) * each : k * each, :]
        rows = pl.ds((own ^ k) * head, head)
        wq_ref[rows, :] = pair_ref[:head, :]
        wo_ref[rows, :] = pair_ref[head:, :]
    length = xn_ref.shape[0]
    choose = ids_ref.shape[0]
    all_ref[...] = nt(wq_ref[...], xn_ref[...])
    for start in range(0, length, BAND):
        lanes = slice(start, start + BAND)
        block = slice(start * choose, (start + BAND) * choose)
        low, high = window(start, length)
        chosen = []
        for route in range(choose):
            ids = ids_ref[route : route + 1, lanes]
            value = jnp.zeros((head, BAND), F32)
            for expert in range(experts):
                value = jnp.where(
                    ids == expert, all_ref[expert * head : (expert + 1) * head, lanes], value
                )
            chosen.append(value)
        queries = jnp.concatenate(chosen, axis=1).astype(BF)
        qt_ref[:, block] = queries
        scores = masked_scores(kv_ref, keyid_ref, sent_ref, queries, start, low, high, choose)
        largest = jnp.max(scores, axis=0, keepdims=True)
        raised = jnp.exp(scores - largest)
        total = jnp.sum(raised, axis=0, keepdims=True)
        probs = (raised * (1.0 / total)).astype(BF)
        lse_ref[:, block] = largest + jnp.log(total)
        attended = nn(kvt_ref[head:, low:high], probs).astype(BF)
        at_ref[:, block] = attended
        spread = [jnp.zeros((head, BAND), F32) for _ in range(experts)]
        for route in range(choose):
            ids = ids_ref[route : route + 1, lanes]
            gated = attended[:, route * BAND : (route + 1) * BAND].astype(F32) * gates_ref[
                route : route + 1, lanes
            ]
            for expert in range(experts):
                spread[expert] = jnp.where(ids == expert, gated, spread[expert])
        for expert in range(experts):
            gat_ref[expert * head : (expert + 1) * head, lanes] = spread[expert].astype(BF)
    gain = ln_ref[1:2, :]
    for start in range(0, length, ROWS):
        rows = slice(start, start + ROWS)
        mixed = tn(gat_ref[:, rows], wo_ref[...])
        hidden = x_ref[rows, :].astype(F32) + mixed
        h_ref[rows, :] = hidden
        normalized, _ = normalize(hidden)
        low_value = (normalized * gain).astype(BF)
        hn_ref[rows, :] = low_value
        hnt_ref[:, rows] = low_value.T


def gelu_both(values):
    bell = jnp.exp2(values * values * -0.7213475204444817)
    t = 1.0 / (1.0 + 0.23164188 * jnp.abs(values))
    poly = t * (
        0.127414796
        + t * (-0.142248368 + t * (0.7107068705 + t * (-0.7265760135 + t * 0.5307027145)))
    )
    tail = poly * bell
    cumulative = jnp.where(values >= 0.0, 1.0 - tail, tail)
    return values * cumulative, cumulative + values * (bell * 0.3989422804014327)


def ffn_block(refs, first):
    hn_ref, hnt_ref, gt_ref, ag_ref, win_ref, u_ref, dpre_ref = refs
    length, width = hn_ref.shape
    far = slice(first, first + width)
    out_grad = in_grad = None
    for start in range(0, length, 2 * ROWS):
        rows = slice(start, start + 2 * ROWS)
        activated, slope = gelu_both(nn(hn_ref[rows, :], win_ref[:, far]))
        activated = activated.astype(BF)
        before = (ag_ref[rows, far].astype(F32) * slope).astype(BF)
        u_ref[rows, :], dpre_ref[rows, :] = activated, before
        out_part, in_part = nn(gt_ref[:, rows], activated), nn(hnt_ref[:, rows], before)
        out_grad = out_part if out_grad is None else out_grad + out_part
        in_grad = in_part if in_grad is None else in_grad + in_part
    return out_grad.astype(BF).T, in_grad.astype(BF)


def ffn_kernel(*refs, first, peers):
    place_ref, part_refs = refs[5], list(refs[8:])
    width = refs[0].shape[1]
    tok = place_ref[0]
    out_grad, in_grad = ffn_block((*refs[:5], *refs[6:8]), first)
    if peers == 2:
        pieces = len(part_refs) // 2
        size = part_refs[0].shape[0]
        for i in range(pieces):
            span = slice(i * size, (i + 1) * size)
            one, two = out_grad[span, :], in_grad[span, :]
            part_refs[i][...] = jnp.where(tok == 0, one, two)
            part_refs[pieces + i][...] = jnp.where(tok == 0, two, one)
        return
    sum_ref = part_refs.pop()
    sum_ref[:width, :], sum_ref[width:, :] = out_grad, in_grad
    size = part_refs[0].shape[0]
    pieces = len(part_refs) // peers
    for k in range(peers):
        for i in range(pieces):
            start = (tok ^ k) * size * pieces + i * size
            part_refs[k * pieces + i][...] = sum_ref[pl.ds(start, size), :]


def output_kernel(*refs):
    h_ref, wout_ref = refs[:2]
    out_ref, send, far_ref = refs[-3:]
    u_refs = refs[2:-4]
    for start in range(0, h_ref.shape[0], ROWS):
        rows = slice(start, start + ROWS)
        total, first = h_ref[rows, :], 0
        for ref in u_refs:
            size = ref.shape[1]
            total = total + nn(ref[rows, :], wout_ref[first : first + size, :])
            first = first + size
        out_ref[rows, :] = total.astype(BF)
        send(out_ref.at[rows, :], far_ref.at[rows, :])


def hidden_kernel(*refs):
    h_ref, g_ref, win_ref, ln_ref = refs[:4]
    dh_ref, low_ref, gain_ref = refs[-3:]
    dpre_refs = refs[4:-3]
    gain = ln_ref[1:2, :]
    gain_sum = jnp.zeros_like(gain)
    for start in range(0, h_ref.shape[0], ROWS):
        rows = slice(start, start + ROWS)
        upstream, first = None, 0
        for ref in dpre_refs:
            size = ref.shape[1]
            part = nt(ref[rows, :], win_ref[:, first : first + size])
            upstream = part if upstream is None else upstream + part
            first = first + size
        normalized, inverse = normalize(h_ref[rows, :])
        value = g_ref[rows, :].astype(F32) + normalize_back(upstream, normalized, inverse, gain)
        dh_ref[rows, :] = value
        low_ref[rows, :] = value.astype(BF)
        gain_sum = gain_sum + jnp.sum(upstream * normalized, axis=0, keepdims=True)
    gain_ref[...] = gain_sum


def heads_back_kernel(
    kv_ref, kvt_ref, gates_ref, wo_ref, qt_ref, at_ref, lse_ref, gat_ref, low_ref, ids_ref, sent_ref,
    keyid_ref, z_ref, gout_ref, all_ref, dkv_ref, *, experts, head,
):
    length = kv_ref.shape[0]
    wide, pair = experts * head, 2 * head
    choose = ids_ref.shape[0]
    all_ref[...] = nt(wo_ref[...], low_ref[...])
    gout_ref[...] = nn(gat_ref[...], low_ref[...]).astype(BF)
    dkv_ref[...] = jnp.zeros_like(dkv_ref)
    for start in range(0, length, BAND):
        lanes = slice(start, start + BAND)
        block = slice(start * choose, (start + BAND) * choose)
        low, high = window(start, length)
        raw, gate_grads = [], []
        for route in range(choose):
            ids = ids_ref[route : route + 1, lanes]
            value = jnp.zeros((head, BAND), F32)
            for expert in range(experts):
                value = jnp.where(
                    ids == expert, all_ref[expert * head : (expert + 1) * head, lanes], value
                )
            raw.append(value)
            attended = at_ref[:, start * choose + route * BAND : start * choose + (route + 1) * BAND]
            gate_grads.append(jnp.sum(value * attended.astype(F32), axis=0, keepdims=True))
        gates = [gates_ref[route : route + 1, lanes] for route in range(choose)]
        common = functools.reduce(
            lambda a, b: a + b, [gate * grad for gate, grad in zip(gates, gate_grads)]
        )
        logit_rows = [jnp.zeros((1, BAND), F32) for _ in range(experts)]
        for route in range(choose):
            ids = ids_ref[route : route + 1, lanes]
            picked = gates[route] * (gate_grads[route] - common)
            for expert in range(experts):
                logit_rows[expert] = jnp.where(ids == expert, picked, logit_rows[expert])
        logit_pad = jnp.concatenate(
            logit_rows + [jnp.zeros((16 - experts, BAND), F32)], axis=0
        )
        z_ref[wide + pair :, lanes] = logit_pad.astype(BF)
        queries = qt_ref[:, block]
        scores = masked_scores(kv_ref, keyid_ref, sent_ref, queries, start, low, high, choose)
        probs = jnp.exp(scores - lse_ref[:, block])
        upstream = jnp.concatenate(
            [gate * value for gate, value in zip(gates, raw)], axis=1
        ).astype(BF)
        padded = jnp.concatenate([jnp.zeros_like(upstream), upstream], axis=0)
        prob_grad = nn(kv_ref[low:high, :], padded)
        mean = jnp.sum(probs * prob_grad, axis=0, keepdims=True)
        score_grad = (probs * (prob_grad - mean)).astype(BF)
        query_grad = (nn(kvt_ref[:head, low:high], score_grad) * 0.125).astype(BF)
        spread = [jnp.zeros((head, BAND), BF) for _ in range(experts)]
        for route in range(choose):
            ids = ids_ref[route : route + 1, lanes]
            piece = query_grad[:, route * BAND : (route + 1) * BAND]
            for expert in range(experts):
                spread[expert] = jnp.where(ids == expert, piece, spread[expert])
        for expert in range(experts):
            z_ref[expert * head : (expert + 1) * head, lanes] = spread[expert]
        dkv_ref[:head, low:high] += nt(queries, score_grad) * 0.125
        dkv_ref[head:, low:high] += nt(upstream, probs.astype(BF))
    z_ref[wide : wide + pair, :] = dkv_ref[...].astype(BF)


def rows_back_kernel(*refs, experts, head, peers, misc):
    (
        z_ref, gout_ref, xn_ref, wq_ref, small_ref, dh_ref, gain_two_ref, x_ref, ln_ref, place_ref,
    ) = refs[:10]
    pieces = experts // 2 + 1
    part_refs = refs[10 : 10 + peers * pieces]
    grads_ref, pair_ref, misc_ref, dx_ref, send, far_ref = refs[10 + peers * pieces :]
    length = xn_ref.shape[0]
    wide, pair = experts * head, 2 * head
    grads_ref[...] = nn(z_ref[...], xn_ref[...])
    for expert in range(experts):
        rows = slice(expert * head, (expert + 1) * head)
        pair_ref[expert * pair : expert * pair + head, :] = grads_ref[rows, :].astype(BF)
        pair_ref[expert * pair + head : (expert + 1) * pair, :] = gout_ref[rows, :]
    gain = ln_ref[0:1, :]
    total = jnp.zeros_like(gain)
    for start in range(0, length, ROWS):
        rows = slice(start, start + ROWS)
        normed_grad = tn(z_ref[:wide, rows], wq_ref[...]) + tn(z_ref[wide:, rows], small_ref[...])
        normalized, inverse = normalize(x_ref[rows, :].astype(F32))
        total = total + jnp.sum(normed_grad * normalized, axis=0, keepdims=True)
        back = normalize_back(normed_grad, normalized, inverse, gain)
        dx_ref[rows, :] = (dh_ref[rows, :] + back).astype(BF)
        send(dx_ref.at[rows, :], far_ref.at[rows, :])
    misc_ref[...] = jnp.zeros_like(misc_ref)
    misc_ref[:pair, :] = grads_ref[wide : wide + pair, :]
    misc_ref[pair : pair + 16, :] = jnp.concatenate(
        [
            grads_ref[wide + pair : wide + pair + experts, :],
            total,
            gain_two_ref[...],
            jnp.zeros((14 - experts, total.shape[1]), F32),
        ],
        axis=0,
    )
    each, share = pair // peers, misc // peers
    for k in range(peers):
        part = place_ref[0] ^ k
        for expert in range(experts):
            rows = pl.ds(expert * pair + part * each, each)
            low = expert % 2 * each
            part_refs[k * pieces + expert // 2][low : low + each, :] = pair_ref[rows, :]
        part_refs[(k + 1) * pieces - 1][...] = misc_ref[pl.ds(part * share, share), :].astype(BF)


def exchange(parts, axis):
    size = len(parts)
    return [
        lax.ppermute(parts[k], axis, [(i, i ^ k) for i in range(size)]) for k in range(1, size)
    ]


def tok_views(parts, peers):
    pieces = len(parts) // peers
    others = [exchange(parts[i::pieces], "tok") for i in range(pieces)]
    own = [View(parts[0], more=parts[1:pieces])]
    return own + [View(others[0][k], more=[o[k] for o in others[1:]]) for k in range(peers - 1)]


def bits(size):
    return size.bit_length() - 1


def swap(array, key):
    kind, stage = key
    if kind == "expert":
        size = lax.axis_size("expert")
        return lax.ppermute(array, "expert", [(i, i ^ (1 << stage)) for i in range(size)])
    dp, expert, tok = (lax.axis_size(axis) for axis in AXES)
    pairs = []
    for d in range(dp):
        for e in range(expert):
            for t in range(tok):
                other = d ^ (1 << ((stage + t) % bits(dp)))
                pairs.append(((d * expert + e) * tok + t, (other * expert + e) * tok + t))
    return lax.ppermute(array, AXES, pairs)


def place_row(key):
    kind, stage = key
    return 2 + stage if kind == "dp" else 2 + bits(lax.axis_size("dp")) + stage


class View:
    def __init__(self, array, start=0, rows=None, more=()):
        self.arrays, self.start = [array, *more], start
        self.rows = sum(a.shape[0] for a in self.arrays) if rows is None else rows
        self.array = array

    def read(self, refs, base, stride, bit, rows):
        if len(self.arrays) == 1:
            return refs[0][pl.ds(self.start + base + bit * stride, rows), :].astype(F32)
        size = self.arrays[0].shape[0]
        if stride == 0:
            at = min(base // size, len(self.arrays) - 1)
            return refs[at][base - at * size : base - at * size + rows, :].astype(F32)
        near, far = base // size, (base + stride) // size
        if near == far:
            return refs[near][pl.ds(base - near * size + bit * stride, rows), :].astype(F32)
        if rows > size:
            parts = [
                self.read(refs, base + i * size, stride, bit, size) for i in range(rows // size)
            ]
            return jnp.concatenate(parts, axis=0)
        one = refs[near][base - near * size : base - near * size + rows, :]
        two = refs[far][base + stride - far * size : base + stride - far * size + rows, :]
        return jnp.where(bit == 0, one.astype(F32), two.astype(F32))


class Job:
    def __init__(self, kind, views, key, row=0, count=0, each=0):
        self.kind, self.views, self.key, self.row = kind, views, key, row
        self.count, self.each = count, each
        rows = views[0].rows
        self.kept = rows // 2
        if kind == "add":
            self.sent = rows
        elif kind == "join":
            self.sent = 2 * rows
        elif kind == "weave":
            self.sent = 2 * rows
        elif kind in ("split", "halve"):
            self.sent = rows // 2
        else:
            self.sent = self.kept = count // 2 * each + rows - count * each
        self.keeps = kind in ("split", "pick", "halve")


def glue(line, place, jobs):
    arrays = []
    for job in jobs:
        for view in job.views:
            for array in view.arrays:
                if not any(array is a for a in arrays):
                    arrays.append(array)
    width = arrays[0].shape[1]
    offsets, total = [], 0
    for job in jobs:
        offsets.append(total)
        total += job.sent
    n = len(arrays)

    def kernel(*refs):
        place_ref, send_ref, keep_refs = refs[n], refs[n + 1], list(refs[n + 2 :])

        def ref_of(array):
            return refs[[array is a for a in arrays].index(True)]

        def added(job, base, rows, stride=0, bit=0):
            value = None
            for view in job.views:
                part = view.read([ref_of(a) for a in view.arrays], base, stride, bit, rows)
                value = part if value is None else value + part
            return value.astype(BF)

        for job, offset in zip(jobs, offsets):
            rows, bit = job.views[0].rows, place_ref[job.row]
            if job.kind == "add":
                send_ref[offset : offset + rows, :] = added(job, 0, rows)
            elif job.kind == "join":
                for view, turn in zip(job.views, (bit, 1 - bit)):
                    send_ref[pl.ds(offset + turn * rows, rows), :] = ref_of(view.array)[
                        view.start : view.start + rows, :
                    ]
            elif job.kind == "weave":
                spans = [(q * job.each, job.each) for q in range(job.count)]
                if rows > job.count * job.each:
                    spans.append((job.count * job.each, rows - job.count * job.each))
                for view, turn in zip(job.views, (bit, 1 - bit)):
                    ref = ref_of(view.array)
                    for base, size in spans:
                        send_ref[pl.ds(offset + 2 * base + turn * size, size), :] = ref[
                            view.start + base : view.start + base + size, :
                        ]
            elif job.kind == "halve":
                keep_ref, to = keep_refs.pop(0), 0
                spans = [(q * job.each, job.each) for q in range(job.count)]
                if rows > job.count * job.each:
                    spans.append((job.count * job.each, rows - job.count * job.each))
                for base, size in spans:
                    half = size // 2
                    keep_ref[to : to + half, :] = added(job, base, half, half, bit)
                    send_ref[offset + to : offset + to + half, :] = added(job, base, half, half, 1 - bit)
                    to += half
            elif job.kind == "split":
                half, keep_ref = job.sent, keep_refs.pop(0)
                keep_ref[...] = added(job, 0, half, half, bit)
                send_ref[offset : offset + half, :] = added(job, 0, half, half, 1 - bit)
            else:
                keep_ref, each = keep_refs.pop(0), job.each
                for q in range(job.count // 2):
                    keep_ref[q * each : (q + 1) * each, :] = added(job, 2 * q * each, each, each, bit)
                    send_ref[offset + q * each : offset + (q + 1) * each, :] = added(
                        job, 2 * q * each, each, each, 1 - bit
                    )
                done, base = job.count // 2 * each, job.count * each
                rest = added(job, base, rows - base)
                keep_ref[done:, :] = rest
                send_ref[offset + done : offset + job.sent, :] = rest

    outs = [sds((total, width), BF)] + [sds((job.kept, width), BF) for job in jobs if job.keeps]
    send, *keeps = line.call(kernel, arrays, outs, scalars=(place,), weight=GLUE)
    owns = []
    for job, offset in zip(jobs, offsets):
        owns.append(View(keeps.pop(0)) if job.keeps else View(send, offset, job.sent))
    return send, owns, offsets


class Chains:
    def __init__(self, line, place):
        self.line, self.place = line, place
        self.walks, self.jobs, self.done = {}, {}, {}

    def take(self, name, value):
        try:
            self.jobs[name] = self.walks[name].send(value)
        except StopIteration as end:
            self.done[name] = end.value
            del self.walks[name]

    def begin(self, name, walk):
        self.walks[name] = walk
        self.take(name, None)

    def advance(self, *names):
        names = [name for name in names if name in self.walks]
        while names:
            key = self.jobs[names[0]].key
            group = [name for name in names if self.jobs[name].key == key]
            names = [name for name in names if name not in group]
            jobs = [self.jobs[name] for name in group]
            send, owns, offsets = glue(self.line, self.place, jobs)
            if key[0] == "tok":
                others = exchange([send] * lax.axis_size("tok"), "tok")
            else:
                others = [swap(send, key)]
            for name, job, own, offset in zip(group, jobs, owns, offsets):
                self.take(name, [own] + [View(other, offset, job.sent) for other in others])

    def finish(self, name):
        while name in self.walks:
            self.advance(name)
        return self.done[name]


def chunk_walk(views, mirror, count, each):
    order = [("dp", (s + mirror) % 2) for s in range(bits(lax.axis_size("dp")))]
    experts = [("expert", s) for s in range(bits(lax.axis_size("expert")))]
    halved = []
    for key in order + experts[:-1]:
        if each < 32:
            break
        views = yield Job("halve", views, key, place_row(key), count, each)
        each //= 2
        halved.append(key)
    for key in (order + experts)[len(halved) :]:
        views = yield Job("add", views, key)
    views = [views]
    for key in reversed(halved):
        if len(views) == 1:
            views = yield Job("add", views[0], key)
        else:
            views = yield Job("weave", views, key, place_row(before), count, each)
            each *= 2
        before = key
    views = yield Job("weave", views, ("tok", 0), place_row(before), count, each)
    return views


def tail_walk(views, experts, each, mirror):
    stages = bits(lax.axis_size("dp"))
    order = [("dp", (s + mirror) % 2) for s in range(stages)]
    halves = each >> stages >= 16
    for key in order if halves else ():
        views = yield Job("halve", views, key, place_row(key), experts, each)
        each //= 2
    for stage in range(bits(experts)):
        key = ("expert", stage)
        views = yield Job("pick", views, key, place_row(key), experts >> stage, each)
    before = None
    for key in reversed(order):
        if before is None or not halves:
            views = yield Job("add", views, key)
        else:
            views = yield Job("weave", views, key, place_row(before), 1, each)
            each *= 2
        before = key
    if halves:
        views = yield Job("weave", views, ("tok", 0), place_row(before), 1, each)
    else:
        views = yield Job("add", views, ("tok", 0))
    return views


def place_part(line, place, view, turn, first, hidden, full, before):
    rows, width = view.rows, view.array.shape[1]
    many = hidden // width
    block = rows // many

    def kernel(part_ref, place_ref, _, wide_ref, send, gin_ref, gout_ref):
        part = place_ref[0] ^ turn
        for i in range(many):
            span = slice(i * block, (i + 1) * block)
            wide_ref[span, :] = part_ref[
                view.start + i * block : view.start + (i + 1) * block, :
            ].astype(F32)
            column, at = first + i * width, part * block
            to = pl.multiple_of(column + jnp.minimum(at, width - block), block)
            row = pl.multiple_of(jnp.maximum(at - width, 0), block)
            send(
                wide_ref.at[span, :],
                gout_ref.at[pl.ds(to, block), :],
                gin_ref.at[pl.ds(row, block), column : column + width],
                at < width,
            )

    _, *grads = line.call(
        kernel,
        (view.array,),
        (),
        scalars=(place,),
        scratch=(sds((rows, width), F32),),
        sent=(sds((width, full), F32), sds((full, width), F32)),
        aliased=before,
    )
    return tuple(grads)


def place_tail(line, place, views, experts, head, misc):
    peers = len(views)
    parts = [view.array for view in views]
    pair, width = 2 * head, parts[0].shape[1]
    each, share = pair // peers, misc // peers

    def last(*refs):
        part_refs, place_ref = refs[:peers], refs[peers]
        query_ref, output_ref, kv_ref, router_ref, one_ref, two_ref, pair_ref, misc_ref = refs[
            peers + 1 :
        ]
        for k, view in enumerate(views):
            part, start = place_ref[0] ^ k, view.start
            pair_ref[pl.ds(part * each, each), :] = part_refs[k][start : start + each, :].astype(F32)
            misc_ref[pl.ds(part * share, share), :] = part_refs[k][
                start + each : start + view.rows, :
            ].astype(F32)
        query_ref[0] = pair_ref[:head, :]
        output_ref[0] = pair_ref[head:, :]
        kv_ref[...] = misc_ref[:pair, :].T
        router_ref[...] = misc_ref[pair : pair + experts, :]
        one_ref[...] = misc_ref[pair + experts : pair + experts + 1, :]
        two_ref[...] = misc_ref[pair + experts + 1 : pair + experts + 2, :]

    return line.call(
        last,
        parts,
        [
            sds((1, head, width), F32),
            sds((1, head, width), F32),
            sds((width, pair), F32),
            sds((experts, width), F32),
            sds((1, width), F32),
            sds((1, width), F32),
        ],
        scalars=(place,),
        scratch=(sds((pair, width), F32), sds((misc, width), F32)),
    )


def join_all(line, arrays):
    rows, width = arrays[0].shape
    count = len(arrays)

    def kernel(*refs):
        for k in range(count):
            refs[count][k * rows : (k + 1) * rows, :] = refs[k][...]

    return line.call(kernel, arrays, [sds((count * rows, width), BF)])[0]


def body(
    tokens, out_grad, expert_ids, sentence_ids, ln_attn, w_kv, w_router, w_query, w_output, ln_ffn, w_in, w_out
):
    length, width = tokens.shape
    head = w_query.shape[2]
    pair = w_kv.shape[1]
    full = w_in.shape[1]
    experts = lax.axis_size("expert")
    peers = lax.axis_size("tok")
    choose = expert_ids.shape[1]
    tok, dp, expert = lax.axis_index("tok"), lax.axis_index("dp"), lax.axis_index("expert")
    stages = bits(lax.axis_size("dp"))
    dp_bits = [(dp >> ((s + tok) % stages)) & 1 for s in range(stages)]
    spots = jnp.stack(
        [tok, expert] + dp_bits + [(expert >> s) & 1 for s in range(bits(experts))]
    ).astype(jnp.int32)
    weights = jnp.concatenate([w_query[0].T, w_output[0]], axis=0)
    each = weights.shape[0] // peers
    weights = lax.dynamic_slice_in_dim(weights, tok * each, each, axis=0)
    pieces = exchange([weights] * experts, "expert")
    ids = expert_ids.T
    ln_one = ln_attn.reshape(1, width)
    ln_two = ln_ffn.reshape(1, width)
    line = Line()
    line.last = spots
    (
        normed, kv, kvt, gates, gt, small, sent, gains, keyid, place, x, g, ids, in_weight, out_weight, own_query,
        own_output,
    ) = line.call(
        prepare_kernel,
        (),
        [
            sds((length, width), BF),
            sds((length, pair), BF),
            sds((pair, length), BF),
            sds((choose, length), F32),
            sds((width, length), BF),
            sds((pair + 16, width), BF),
            sds((1, length), F32),
            sds((2, width), F32),
            sds((length, BAND), F32),
            sds((8, 128), jnp.int32),
        ],
        fetched=(ln_one, w_kv, w_router.T, sentence_ids, ln_two),
        numbers=(spots,),
        kept=(tokens, out_grad, ids, w_in, w_out, w_query[0].T, w_output[0]),
        room=8 << 20,
    )
    [ag] = line.call(
        upstream_kernel, (g, out_weight), [sds((length, full), BF)], room=8 << 20,
    )
    slab = join_all(line, pieces)
    slabs = [slab] + exchange([slab] * peers, "tok")
    wq, wo, qt, at, lse, gat, h, hn, hnt = line.call(
        functools.partial(attend_kernel, experts=experts, head=head, peers=peers),
        (*slabs, normed, kv, kvt, gates, x, ids, sent, gains, keyid, own_query, own_output),
        [
            sds((experts * head, width), BF),
            sds((experts * head, width), BF),
            sds((head, choose * length), BF),
            sds((head, choose * length), BF),
            sds((1, choose * length), F32),
            sds((experts * head, length), BF),
            sds((length, width), F32),
            sds((length, width), BF),
            sds((width, length), BF),
        ],
        scalars=(place,),
        scratch=(
            sds((experts * head, length), F32),
            sds((2 * head, width), BF),
        ),
        room=8 << 20,
    )

    chains = Chains(line, place)
    us, dpres, sums = [], [], []

    def ffn(last=None, mirror=0):
        rows = 2 * width // peers
        pieces = max(1, rows // PIECE)
        rows = rows // pieces
        u, dpre, *parts = line.call(
            functools.partial(ffn_kernel, first=len(us) * width, peers=peers),
            (hn, hnt, gt, ag, in_weight),
            [sds((length, width), BF)] * 2 + [sds((rows, width), BF)] * (peers * pieces),
            scalars=(place,),
            scratch=() if peers == 2 else (sds((2 * width, width), BF),),
            room=6 << 20,
        )
        us.append(u)
        dpres.append(dpre)
        for i in range(pieces):
            sums.append([parts[i]] + exchange(parts[i::pieces], "tok"))
        if last is not None:
            views = [View(same[0], more=same[1:]) for same in zip(*sums)]
            chains.begin(last, chunk_walk(views, mirror, len(sums), rows))
            sums.clear()

    misc = -(-(pair + 16) // (64 * peers)) * 64 * peers
    half = full // 2

    def hidden():
        made["dh"], made["low"], made["gain"] = line.call(
            hidden_kernel,
            (h, g, in_weight, gains, *dpres),
            [sds((length, width), F32), sds((length, width), BF), sds((1, width), F32)],
            room=6 << 20,
        )

    def heads_back():
        made["z"], made["gout"] = line.call(
            functools.partial(heads_back_kernel, experts=experts, head=head),
            (kv, kvt, gates, wo, qt, at, lse, gat, made["low"], ids, sent, keyid),
            [sds((experts * head + pair + 16, length), BF), sds((experts * head, width), BF)],
            scratch=(sds((experts * head, length), F32), sds((pair, length), F32)),
            room=6 << 20,
        )

    def rows_back():
        *parts, made["dx"] = line.call(
            functools.partial(rows_back_kernel, experts=experts, head=head, peers=peers, misc=misc),
            (made["z"], made["gout"], normed, wq, small, made["dh"], made["gain"], x, gains),
            ([sds((2 * pair // peers, width), BF)] * (experts // 2) + [sds((misc // peers, width), BF)])
            * peers,
            sent=(sds((length, width), BF),),
            scalars=(place,),
            scratch=(
                sds((experts * head + pair + 16, width), F32),
                sds((experts * pair, width), BF),
                sds((misc, width), F32),
                sds((length, width), BF),
            ),
            room=6 << 20,
        )
        chains.begin("t", tail_walk(tok_views(parts, peers), experts, pair // peers, 1))

    def out():
        _, made["output"] = line.call(
            output_kernel,
            (h, out_weight, *us),
            (),
            sent=(sds((length, width), BF),),
            scratch=(sds((length, width), BF),),
            room=6 << 20,
        )

    def place_one(name, first, turn):
        if turn == 0:
            made[name] = chains.finish(name)
            views = made[name][:1]
        else:
            views = made[name][1:]
        for view in views:
            made["both"] = place_part(
                line, place, view, turn, first, half, full, made.get("both", ())
            )
            turn += 1

    def last():
        made["t"] = place_tail(line, place, chains.finish("t"), experts, head, misc)

    made = {}
    acts = {
        "f": ffn,
        "A": lambda: ffn("a"),
        "B": lambda: ffn("b", 1),
        "n": hidden,
        "h": heads_back,
        "r": rows_back,
        "o": out,
        "P": lambda: place_one("a", 0, 0),
        "p": lambda: place_one("a", 0, 1),
        "Q": lambda: place_one("b", half, 0),
        "q": lambda: place_one("b", half, 1),
        "T": last,
    }
    for word in ORDER:
        if word in acts:
            acts[word]()
        else:
            chains.advance(*word)
    query, outp, kv_grad, router, one, two = made["t"]
    output, dx, both = made["output"], made["dx"], made["both"]
    return (
        output,
        dx,
        one.reshape(width),
        kv_grad,
        router.T,
        jnp.swapaxes(query, 1, 2),
        outp,
        two.reshape(width),
        both[0],
        both[1],
    )


def solution(mesh):
    rows = P(AXES, None)
    heads = P("expert", None, None)
    return jax.shard_map(
        body,
        mesh=mesh,
        in_specs=(rows, rows, rows, rows, P(), P(), P(), heads, heads, P(), P(), P()),
        out_specs=(rows, rows, P(), P(), P(), heads, heads, P(), P(), P()),
        check_vma=False,
    )
```

```python
import functools

import jax
import jax.numpy as jnp
from jax import lax
from jax.experimental import pallas as pl
from jax.experimental.pallas import tpu as pltpu
from jax.sharding import PartitionSpec as P

BF = jnp.bfloat16
F32 = jnp.float32
MASKED = -1e30
BAND = 128
ROWS = 256
PIECE = 256
AXES = ("dp", "expert", "tok")
GLUE = 23 * 10**9
COPIES = 8
WORK = 1
ORDER = (
    "f", "A", "f", "a", "B", "n", "a", "b", "h", "a", "r", "b", "a", "o", "b", "t", "a", "b", "t",
    "a", "t", "b", "a", "t", "b", "t", "a", "1", "b", "2", "t", "b", "3", "t", "4", "T",
)


def nn(left, right):
    return lax.dot_general(left, right, (((1,), (0,)), ((), ())), preferred_element_type=F32)


def nt(left, right):
    return lax.dot_general(left, right, (((1,), (1,)), ((), ())), preferred_element_type=F32)


def tn(left, right):
    return lax.dot_general(left, right, (((0,), (0,)), ((), ())), preferred_element_type=F32)


def normalize(values):
    centre = values - jnp.mean(values, axis=-1, keepdims=True)
    spread = jnp.mean(centre * centre, axis=-1, keepdims=True)
    inverse = lax.rsqrt(spread + 1e-05)
    return centre * inverse, inverse


def normalize_back(upstream, normalized, inverse, gain):
    scaled = upstream * gain
    inner = (
        scaled
        - jnp.mean(scaled, axis=-1, keepdims=True)
        - normalized * jnp.mean(scaled * normalized, axis=-1, keepdims=True)
    )
    return inner * inverse


def sds(shape, dtype):
    return jax.ShapeDtypeStruct(shape, dtype)


def size_of(array):
    lanes = -(-array.shape[-1] // 128) * 128
    rows = -(-array.shape[-2] // 16) * 16
    lead = 1
    for extent in array.shape[:-2]:
        lead = lead * extent
    return lead * rows * lanes * jnp.dtype(array.dtype).itemsize


class Place:
    def __init__(self, ref):
        self.ref = ref

    def __getitem__(self, row):
        return self.ref[row, 0]


class Line:
    def __init__(self):
        self.last = None

    def call(
        self, kernel, operands, outs, fetched=(), scalars=(), scratch=(), room=2 << 20, weight=WORK,
        sent=(), aliased=(), kept=(), numbers=(), delayed=0,
    ):
        n, f, s = len(operands), len(fetched) + len(kept), len(scalars)
        late = () if self.last is None else (self.last,)
        skip = len(late) + len(aliased)
        outs = list(outs)
        h = len(sent)
        if not outs:
            outs = [sds((8, 128), F32)]
        outs = outs + [sds(a.shape, a.dtype) for a in kept]
        scratch_copies, fetched = len(fetched), (*fetched, *kept)

        def wrapped(*refs):
            ins = refs[:n]
            sources = refs[n : n + f]
            smem = [Place(ref) for ref in refs[n + f : n + f + s]]
            rest = list(refs[n + f + s + len(numbers) + skip :])
            if numbers:
                number_sem, number_ref = rest.pop(), rest.pop()
                number = pltpu.make_async_copy(refs[n + f + s], number_ref, number_sem.at[0])
                number.start()

                def number_wait():
                    number.wait()
                    return number_ref

                smem = smem + [number_wait]
            far = rest[len(outs) : len(outs) + h]
            del rest[len(outs) : len(outs) + h]
            open_copies, send_sem = [], rest.pop() if h else None
            sems = rest.pop() if f else None
            buffers = rest[len(rest) - scratch_copies :] if scratch_copies else []
            del rest[len(rest) - scratch_copies :]
            first = len(outs) - len(kept)
            buffers = buffers + rest[first : len(outs)]
            del rest[first : len(outs)]
            body, waits, waiting = rest, [], {}
            for i in range(f):
                copy = pltpu.make_async_copy(sources[i], buffers[i], sems.at[i])
                if i < f - delayed:
                    copy.start()
                waiting[i] = copy

                def wait(i=i):
                    if i in waiting:
                        waiting.pop(i).wait()
                        if i == f - delayed - 1:
                            for j in range(f - delayed, f):
                                waiting[j].start()
                    return buffers[i]

                waits.append(wait)
            def send(source, target, other=None, near=None):
                sem = send_sem.at[len(open_copies)]
                copy = pltpu.make_async_copy(source, target, sem)
                open_copies.append(copy)
                if other is None:
                    copy.start()
                    return
                pl.when(near)(copy.start)
                pl.when(jnp.logical_not(near))(pltpu.make_async_copy(source, other, sem).start)

            if h:
                kernel(*ins, *waits, *smem, *body, send, *far)
                for copy in open_copies:
                    copy.wait()
            else:
                kernel(*ins, *waits, *smem, *body)
            for copy in waiting.values():
                copy.wait()

        need = sum(size_of(a) for a in (*fetched[:scratch_copies], *scratch))
        extra = [pltpu.VMEM(a.shape, a.dtype) for a in fetched[:scratch_copies]]
        if f:
            extra.append(pltpu.SemaphoreType.DMA((f,)))
        if h:
            extra.append(pltpu.SemaphoreType.DMA((COPIES,)))
        if numbers:
            extra += [pltpu.SMEM(numbers[0].shape, jnp.int32), pltpu.SemaphoreType.DMA((1,))]
        results = pl.pallas_call(
            wrapped,
            out_shape=outs + list(sent),
            in_specs=[pl.BlockSpec(memory_space=pltpu.VMEM)] * n
            + [pl.BlockSpec(memory_space=pltpu.HBM)] * f
            + [pl.BlockSpec(memory_space=pltpu.VMEM)] * s
            + [pl.BlockSpec(memory_space=pl.ANY)] * len(numbers)
            + [pl.BlockSpec(memory_space=pl.ANY)] * skip,
            out_specs=[pl.BlockSpec(memory_space=pltpu.VMEM)] * len(outs)
            + [pl.BlockSpec(memory_space=pltpu.HBM)] * h,
            input_output_aliases={
                n + f + s + len(numbers) + len(late) + i: len(outs) + i for i in range(len(aliased))
            },
            scratch_shapes=[pltpu.VMEM(a.shape, a.dtype) for a in scratch] + extra,
            compiler_params=pltpu.CompilerParams(vmem_limit_bytes=need + room),
            cost_estimate=pl.CostEstimate(flops=weight, bytes_accessed=1024, transcendentals=0),
        )(
            *operands,
            *[pltpu.with_memory_space_constraint(a, pltpu.HBM) for a in fetched],
            *scalars,
            *numbers,
            *late,
            *aliased,
        )
        self.last = min(results[: len(outs)], key=lambda a: a.size)
        return results


def prepare_kernel(
    ln_wait, wkv_wait, wr_wait, sent_wait, ln_two_wait, ids_wait, wq_wait, wo_wait, x_wait, g_wait, wout_wait,
    spots_wait, xn_ref, kv_ref, kvt_ref, gates_ref, gt_ref, small_ref, sent_keep, gains_keep, keyid_ref,
    place_ref,
):
    ln_ref, x_ref = ln_wait(), x_wait()
    length = x_ref.shape[0]
    gain = ln_ref[...]
    gains_keep[0:1, :] = gain
    for start in range(0, length, ROWS):
        rows = pl.ds(start, ROWS)
        normalized, _ = normalize(x_ref[rows, :].astype(F32))
        xn_ref[rows, :] = (normalized * gain).astype(BF)
    normed = xn_ref[...]
    wkv_ref, wr_ref, ids_ref = wkv_wait(), wr_wait(), ids_wait()
    pair = wkv_ref.shape[1]
    experts = wr_ref.shape[0]
    small_ref[:pair, :] = wkv_ref[...].T
    small_ref[pair:, :] = jnp.concatenate(
        [wr_ref[...].astype(F32), jnp.zeros((16 - experts, wr_ref.shape[1]), F32)], axis=0
    ).astype(BF)
    small = small_ref[...]
    both = nt(small, normed)
    kvt_ref[...] = both[:pair].astype(BF)
    kv_ref[...] = nn(normed, wkv_ref[...]).astype(BF)
    choose = ids_ref.shape[0]
    picked = []
    for route in range(choose):
        ids = ids_ref[route : route + 1, :]
        value = jnp.zeros((1, length), F32)
        for expert in range(experts):
            value = jnp.where(ids == expert, both[pair + expert : pair + expert + 1], value)
        picked.append(value)
    top = functools.reduce(jnp.maximum, picked)
    raised = [jnp.exp(value - top) for value in picked]
    total = functools.reduce(lambda a, b: a + b, raised)
    for route in range(choose):
        gates_ref[route : route + 1, :] = raised[route] / total
    gains_keep[1:2, :] = ln_two_wait()[...]
    sent_ref = sent_wait()
    sent_keep[...] = sent_ref[...].astype(F32)
    column_ids(sent_keep, keyid_ref)
    g_ref = g_wait()
    gt_ref[...] = g_ref[...].T
    spots_ref = spots_wait()
    for i in range(spots_ref.shape[0]):
        place_ref[i : i + 1, :] = jnp.full((1, place_ref.shape[1]), spots_ref[i], jnp.int32)


def upstream_kernel(g_ref, wout_ref, win_wait, ag_ref):
    for start in range(0, g_ref.shape[0], ROWS):
        rows = slice(start, start + ROWS)
        ag_ref[rows, :] = nt(g_ref[rows, :], wout_ref[...]).astype(BF)


def column_ids(sent_ref, keyid_ref):
    length = sent_ref.shape[1]
    for start in range(0, length, BAND):
        row = jnp.broadcast_to(sent_ref[:, start : start + BAND], (BAND, BAND))
        keyid_ref[pl.ds(start, BAND), :] = row.T


def masked_scores(kv_ref, keyid_ref, sent_ref, queries, start, low, high, choose):
    padded = jnp.concatenate([queries * 0.125, jnp.zeros_like(queries)], axis=0)
    scores = nn(kv_ref[low:high, :], padded)
    same = keyid_ref[low:high, :] == sent_ref[:, start : start + BAND]
    parts = [
        jnp.where(same, scores[:, route * BAND : (route + 1) * BAND], MASKED)
        for route in range(choose)
    ]
    return jnp.concatenate(parts, axis=1)


def window(start, length):
    return max(start - BAND, 0), min(start + 2 * BAND, length)


def attend_kernel(*refs, experts, head, peers):
    slab_refs, refs = refs[:peers], refs[peers:]
    (
        xn_ref, kv_ref, kvt_ref, gates_ref, x_ref, ids_ref, sent_ref, ln_ref, keyid_ref, wq_own, wo_own,
        place_ref, wq_ref, wo_ref, qt_ref, at_ref, lse_ref, gat_ref, h_ref, hn_ref, hnt_ref, all_ref,
        pair_ref, score_ref, prob_ref,
    ) = refs
    own = place_ref[1]
    each = 2 * head // peers
    wq_ref[pl.ds(own * head, head), :] = wq_own[...]
    wo_ref[pl.ds(own * head, head), :] = wo_own[...]
    for k in range(1, experts):
        for j in range(peers):
            rows = pl.ds((place_ref[0] ^ j) * each, each)
            pair_ref[rows, :] = slab_refs[j][(k - 1) * each : k * each, :]
        rows = pl.ds((own ^ k) * head, head)
        wq_ref[rows, :] = pair_ref[:head, :]
        wo_ref[rows, :] = pair_ref[head:, :]
    length = xn_ref.shape[0]
    choose = ids_ref.shape[0]
    all_ref[...] = nt(wq_ref[...], xn_ref[...])
    starts = range(0, length, BAND)
    spans = [slice(start * choose, (start + BAND) * choose) for start in starts]
    bounds = [window(start, length) for start in starts]
    for start, block in zip(starts, spans):
        lanes = slice(start, start + BAND)
        chosen = []
        for route in range(choose):
            ids = ids_ref[route : route + 1, lanes]
            value = all_ref[:head, lanes]
            for expert in range(1, experts):
                value = jnp.where(
                    ids == expert, all_ref[expert * head : (expert + 1) * head, lanes], value
                )
            chosen.append(value)
        qt_ref[:, block] = jnp.concatenate(chosen, axis=1).astype(BF)
    for i, start in enumerate(starts):
        low, high = bounds[i]
        score_ref[i, : high - low, :] = masked_scores(
            kv_ref, keyid_ref, sent_ref, qt_ref[:, spans[i]], start, low, high, choose
        )
    for i, block in enumerate(spans):
        size = bounds[i][1] - bounds[i][0]
        scores = score_ref[i, :size, :]
        largest = jnp.max(scores, axis=0, keepdims=True)
        raised = jnp.exp(scores - largest)
        total = jnp.sum(raised, axis=0, keepdims=True)
        prob_ref[i, :size, :] = (raised * (1.0 / total)).astype(BF)
        lse_ref[:, block] = largest + jnp.log(total)
    for i, block in enumerate(spans):
        low, high = bounds[i]
        at_ref[:, block] = nn(kvt_ref[head:, low:high], prob_ref[i, : high - low, :]).astype(BF)
    for start in starts:
        lanes = slice(start, start + BAND)
        spread = [jnp.zeros((head, BAND), F32) for _ in range(experts)]
        for route in range(choose):
            ids = ids_ref[route : route + 1, lanes]
            first = start * choose + route * BAND
            gated = at_ref[:, first : first + BAND].astype(F32) * gates_ref[route : route + 1, lanes]
            for expert in range(experts):
                spread[expert] = jnp.where(ids == expert, gated, spread[expert])
        for expert in range(experts):
            gat_ref[expert * head : (expert + 1) * head, lanes] = spread[expert].astype(BF)
    gain = ln_ref[1:2, :]
    for start in range(0, length, ROWS):
        rows = slice(start, start + ROWS)
        mixed = tn(gat_ref[:, rows], wo_ref[...])
        hidden = x_ref[rows, :].astype(F32) + mixed
        h_ref[rows, :] = hidden
        normalized, _ = normalize(hidden)
        low_value = (normalized * gain).astype(BF)
        hn_ref[rows, :] = low_value
        hnt_ref[:, rows] = low_value.T


def gelu_both(values):
    bell = jnp.exp2(values * values * -0.7213475204444817)
    t = 1.0 / (1.0 + 0.23164188 * jnp.abs(values))
    poly = t * (
        0.127414796
        + t * (-0.142248368 + t * (0.7107068705 + t * (-0.7265760135 + t * 0.5307027145)))
    )
    tail = poly * bell
    cumulative = jnp.where(values >= 0.0, 1.0 - tail, tail)
    return values * cumulative, cumulative + values * (bell * 0.3989422804014327)


def ffn_block(refs, first):
    hn_ref, hnt_ref, gt_ref, ag_ref, win_ref, u_ref, dpre_ref = refs
    length, width = hn_ref.shape
    far = slice(first, first + width)
    out_grad = in_grad = None
    for start in range(0, length, 2 * ROWS):
        rows = slice(start, start + 2 * ROWS)
        activated, slope = gelu_both(nn(hn_ref[rows, :], win_ref[:, far]))
        activated = activated.astype(BF)
        before = (ag_ref[rows, far].astype(F32) * slope).astype(BF)
        u_ref[rows, :], dpre_ref[rows, :] = activated, before
        out_part, in_part = nn(gt_ref[:, rows], activated), nn(hnt_ref[:, rows], before)
        out_grad = out_part if out_grad is None else out_grad + out_part
        in_grad = in_part if in_grad is None else in_grad + in_part
    return out_grad.astype(BF).T, in_grad.astype(BF)


def ffn_kernel(*refs, first, peers):
    place_ref, part_refs = refs[5], list(refs[8:])
    width = refs[0].shape[1]
    tok = place_ref[0]
    out_grad, in_grad = ffn_block((*refs[:5], *refs[6:8]), first)
    if peers == 2:
        pieces = len(part_refs) // 2
        size = part_refs[0].shape[0]
        for i in range(pieces):
            span = slice(i * size, (i + 1) * size)
            one, two = out_grad[span, :], in_grad[span, :]
            part_refs[i][...] = jnp.where(tok == 0, one, two)
            part_refs[pieces + i][...] = jnp.where(tok == 0, two, one)
        return
    sum_ref = part_refs.pop()
    sum_ref[:width, :], sum_ref[width:, :] = out_grad, in_grad
    size = part_refs[0].shape[0]
    pieces = len(part_refs) // peers
    for k in range(peers):
        for i in range(pieces):
            start = (tok ^ k) * size * pieces + i * size
            part_refs[k * pieces + i][...] = sum_ref[pl.ds(start, size), :]


def output_kernel(*refs):
    h_ref, wout_ref = refs[:2]
    out_ref, send, far_ref = refs[-3:]
    u_refs = refs[2:-4]
    for start in range(0, h_ref.shape[0], ROWS):
        rows = slice(start, start + ROWS)
        total, first = h_ref[rows, :], 0
        for ref in u_refs:
            size = ref.shape[1]
            total = total + nn(ref[rows, :], wout_ref[first : first + size, :])
            first = first + size
        out_ref[rows, :] = total.astype(BF)
        send(out_ref.at[rows, :], far_ref.at[rows, :])


def hidden_kernel(*refs):
    h_ref, g_ref, win_ref, ln_ref = refs[:4]
    dh_ref, low_ref, gain_ref = refs[-3:]
    dpre_refs = refs[4:-3]
    gain = ln_ref[1:2, :]
    gain_sum = jnp.zeros_like(gain)
    for start in range(0, h_ref.shape[0], ROWS):
        rows = slice(start, start + ROWS)
        upstream, first = None, 0
        for ref in dpre_refs:
            size = ref.shape[1]
            part = nt(ref[rows, :], win_ref[:, first : first + size])
            upstream = part if upstream is None else upstream + part
            first = first + size
        normalized, inverse = normalize(h_ref[rows, :])
        value = g_ref[rows, :].astype(F32) + normalize_back(upstream, normalized, inverse, gain)
        dh_ref[rows, :] = value
        low_ref[rows, :] = value.astype(BF)
        gain_sum = gain_sum + jnp.sum(upstream * normalized, axis=0, keepdims=True)
    gain_ref[...] = gain_sum


def heads_back_kernel(
    kv_ref, kvt_ref, gates_ref, wo_ref, qt_ref, at_ref, lse_ref, gat_ref, low_ref, ids_ref, sent_ref,
    keyid_ref, z_ref, gout_ref, all_ref, dkv_ref, up_ref, prob_ref, grad_ref, soft_ref, ds_ref, *, experts,
    head,
):
    length = kv_ref.shape[0]
    wide, pair = experts * head, 2 * head
    choose = ids_ref.shape[0]
    all_ref[...] = nt(wo_ref[...], low_ref[...])
    gout_ref[...] = nn(gat_ref[...], low_ref[...]).astype(BF)
    dkv_ref[...] = jnp.zeros_like(dkv_ref)
    starts = range(0, length, BAND)
    spans = [slice(start * choose, (start + BAND) * choose) for start in starts]
    bounds = [window(start, length) for start in starts]
    for start, block in zip(starts, spans):
        lanes = slice(start, start + BAND)
        raw, gate_grads = [], []
        for route in range(choose):
            ids = ids_ref[route : route + 1, lanes]
            value = all_ref[:head, lanes]
            for expert in range(1, experts):
                value = jnp.where(
                    ids == expert, all_ref[expert * head : (expert + 1) * head, lanes], value
                )
            raw.append(value)
            first = start * choose + route * BAND
            attended = at_ref[:, first : first + BAND].astype(F32)
            gate_grads.append(jnp.sum(value * attended, axis=0, keepdims=True))
        gates = [gates_ref[route : route + 1, lanes] for route in range(choose)]
        common = functools.reduce(
            lambda a, b: a + b, [gate * grad for gate, grad in zip(gates, gate_grads)]
        )
        logit_rows = [jnp.zeros((1, BAND), F32) for _ in range(experts)]
        for route in range(choose):
            ids = ids_ref[route : route + 1, lanes]
            picked = gates[route] * (gate_grads[route] - common)
            for expert in range(experts):
                logit_rows[expert] = jnp.where(ids == expert, picked, logit_rows[expert])
        logit_pad = jnp.concatenate(
            logit_rows + [jnp.zeros((16 - experts, BAND), F32)], axis=0
        )
        z_ref[wide + pair :, lanes] = logit_pad.astype(BF)
        up_ref[:, block] = jnp.concatenate(
            [gate * value for gate, value in zip(gates, raw)], axis=1
        ).astype(BF)
    for i, start in enumerate(starts):
        low, high = bounds[i]
        prob_ref[i, : high - low, :] = masked_scores(
            kv_ref, keyid_ref, sent_ref, qt_ref[:, spans[i]], start, low, high, choose
        )
        upstream = up_ref[:, spans[i]]
        padded = jnp.concatenate([jnp.zeros_like(upstream), upstream], axis=0)
        grad_ref[i, : high - low, :] = nn(kv_ref[low:high, :], padded)
    for i, block in enumerate(spans):
        size = bounds[i][1] - bounds[i][0]
        probs = jnp.exp(prob_ref[i, :size, :] - lse_ref[:, block])
        soft_ref[i, :size, :] = probs.astype(BF)
        prob_grad = grad_ref[i, :size, :]
        mean = jnp.sum(probs * prob_grad, axis=0, keepdims=True)
        ds_ref[i, :size, :] = (probs * (prob_grad - mean)).astype(BF)
    for i, start in enumerate(starts):
        low, high = bounds[i]
        lanes = slice(start, start + BAND)
        score_grad = ds_ref[i, : high - low, :]
        query_grad = (nn(kvt_ref[:head, low:high], score_grad) * 0.125).astype(BF)
        spread = [jnp.zeros((head, BAND), BF) for _ in range(experts)]
        for route in range(choose):
            ids = ids_ref[route : route + 1, lanes]
            piece = query_grad[:, route * BAND : (route + 1) * BAND]
            for expert in range(experts):
                spread[expert] = jnp.where(ids == expert, piece, spread[expert])
        for expert in range(experts):
            z_ref[expert * head : (expert + 1) * head, lanes] = spread[expert]
        dkv_ref[:head, low:high] += nt(qt_ref[:, spans[i]], score_grad) * 0.125
        dkv_ref[head:, low:high] += nt(up_ref[:, spans[i]], soft_ref[i, : high - low, :])
    z_ref[wide : wide + pair, :] = dkv_ref[...].astype(BF)


def rows_back_kernel(*refs, experts, head, peers, misc):
    (
        z_ref, gout_ref, xn_ref, wq_ref, small_ref, dh_ref, gain_two_ref, x_ref, ln_ref, place_ref,
    ) = refs[:10]
    pieces = experts // 2 + 1
    part_refs = refs[10 : 10 + peers * pieces]
    grads_ref, pair_ref, misc_ref, dx_ref, send, far_ref = refs[10 + peers * pieces :]
    length = xn_ref.shape[0]
    wide, pair = experts * head, 2 * head
    grads_ref[...] = nn(z_ref[...], xn_ref[...])
    for expert in range(experts):
        rows = slice(expert * head, (expert + 1) * head)
        pair_ref[expert * pair : expert * pair + head, :] = grads_ref[rows, :].astype(BF)
        pair_ref[expert * pair + head : (expert + 1) * pair, :] = gout_ref[rows, :]
    gain = ln_ref[0:1, :]
    total = jnp.zeros_like(gain)
    for start in range(0, length, ROWS):
        rows = slice(start, start + ROWS)
        normed_grad = tn(z_ref[:wide, rows], wq_ref[...]) + tn(z_ref[wide:, rows], small_ref[...])
        normalized, inverse = normalize(x_ref[rows, :].astype(F32))
        total = total + jnp.sum(normed_grad * normalized, axis=0, keepdims=True)
        back = normalize_back(normed_grad, normalized, inverse, gain)
        dx_ref[rows, :] = (dh_ref[rows, :] + back).astype(BF)
        send(dx_ref.at[rows, :], far_ref.at[rows, :])
    misc_ref[...] = jnp.zeros_like(misc_ref)
    misc_ref[:pair, :] = grads_ref[wide : wide + pair, :]
    misc_ref[pair : pair + 16, :] = jnp.concatenate(
        [
            grads_ref[wide + pair : wide + pair + experts, :],
            total,
            gain_two_ref[...],
            jnp.zeros((14 - experts, total.shape[1]), F32),
        ],
        axis=0,
    )
    each, share = pair // peers, misc // peers
    for k in range(peers):
        part = place_ref[0] ^ k
        for expert in range(experts):
            rows = pl.ds(expert * pair + part * each, each)
            low = expert % 2 * each
            part_refs[k * pieces + expert // 2][low : low + each, :] = pair_ref[rows, :]
        part_refs[(k + 1) * pieces - 1][...] = misc_ref[pl.ds(part * share, share), :].astype(BF)


def exchange(parts, axis):
    size = len(parts)
    return [
        lax.ppermute(parts[k], axis, [(i, i ^ k) for i in range(size)]) for k in range(1, size)
    ]


def tok_views(parts, peers):
    pieces = len(parts) // peers
    others = [exchange(parts[i::pieces], "tok") for i in range(pieces)]
    own = [View(parts[0], more=parts[1:pieces])]
    return own + [View(others[0][k], more=[o[k] for o in others[1:]]) for k in range(peers - 1)]


def bits(size):
    return size.bit_length() - 1


def swap(array, key):
    kind, stage = key
    if kind == "expert":
        size = lax.axis_size("expert")
        return lax.ppermute(array, "expert", [(i, i ^ (1 << stage)) for i in range(size)])
    dp, expert, tok = (lax.axis_size(axis) for axis in AXES)
    pairs = []
    for d in range(dp):
        for e in range(expert):
            for t in range(tok):
                other = d ^ (1 << ((stage + t) % bits(dp)))
                pairs.append(((d * expert + e) * tok + t, (other * expert + e) * tok + t))
    return lax.ppermute(array, AXES, pairs)


def place_row(key):
    kind, stage = key
    return 2 + stage if kind == "dp" else 2 + bits(lax.axis_size("dp")) + stage


class View:
    def __init__(self, array, start=0, rows=None, more=()):
        self.arrays, self.start = [array, *more], start
        self.rows = sum(a.shape[0] for a in self.arrays) if rows is None else rows
        self.array = array

    def read(self, refs, base, stride, bit, rows):
        if len(self.arrays) == 1:
            return refs[0][pl.ds(self.start + base + bit * stride, rows), :].astype(F32)
        size = self.arrays[0].shape[0]
        if stride == 0:
            at = min(base // size, len(self.arrays) - 1)
            return refs[at][base - at * size : base - at * size + rows, :].astype(F32)
        near, far = base // size, (base + stride) // size
        if near == far:
            return refs[near][pl.ds(base - near * size + bit * stride, rows), :].astype(F32)
        if rows > size:
            parts = [
                self.read(refs, base + i * size, stride, bit, size) for i in range(rows // size)
            ]
            return jnp.concatenate(parts, axis=0)
        one = refs[near][base - near * size : base - near * size + rows, :]
        two = refs[far][base + stride - far * size : base + stride - far * size + rows, :]
        return jnp.where(bit == 0, one.astype(F32), two.astype(F32))


class Job:
    def __init__(self, kind, views, key, row=0, count=0, each=0):
        self.kind, self.views, self.key, self.row = kind, views, key, row
        self.count, self.each = count, each
        rows = views[0].rows
        self.kept = rows // 2
        if kind == "add":
            self.sent = rows
        elif kind == "join":
            self.sent = 2 * rows
        elif kind == "weave":
            self.sent = 2 * rows
        elif kind in ("split", "halve"):
            self.sent = rows // 2
        else:
            self.sent = self.kept = count // 2 * each + rows - count * each
        self.keeps = kind in ("split", "pick", "halve")


def glue(line, place, jobs):
    arrays = []
    for job in jobs:
        for view in job.views:
            for array in view.arrays:
                if not any(array is a for a in arrays):
                    arrays.append(array)
    width = arrays[0].shape[1]
    offsets, total = [], 0
    for job in jobs:
        offsets.append(total)
        total += job.sent
    n = len(arrays)

    def kernel(*refs):
        place_ref, send_ref, keep_refs = refs[n], refs[n + 1], list(refs[n + 2 :])

        def ref_of(array):
            return refs[[array is a for a in arrays].index(True)]

        def added(job, base, rows, stride=0, bit=0):
            value = None
            for view in job.views:
                part = view.read([ref_of(a) for a in view.arrays], base, stride, bit, rows)
                value = part if value is None else value + part
            return value.astype(BF)

        for job, offset in zip(jobs, offsets):
            rows, bit = job.views[0].rows, place_ref[job.row]
            if job.kind == "add":
                send_ref[offset : offset + rows, :] = added(job, 0, rows)
            elif job.kind == "join":
                for view, turn in zip(job.views, (bit, 1 - bit)):
                    send_ref[pl.ds(offset + turn * rows, rows), :] = ref_of(view.array)[
                        view.start : view.start + rows, :
                    ]
            elif job.kind == "weave":
                spans = [(q * job.each, job.each) for q in range(job.count)]
                if rows > job.count * job.each:
                    spans.append((job.count * job.each, rows - job.count * job.each))
                for view, turn in zip(job.views, (bit, 1 - bit)):
                    ref = ref_of(view.array)
                    for base, size in spans:
                        send_ref[pl.ds(offset + 2 * base + turn * size, size), :] = ref[
                            view.start + base : view.start + base + size, :
                        ]
            elif job.kind == "halve":
                keep_ref, to = keep_refs.pop(0), 0
                spans = [(q * job.each, job.each) for q in range(job.count)]
                if rows > job.count * job.each:
                    spans.append((job.count * job.each, rows - job.count * job.each))
                for base, size in spans:
                    half = size // 2
                    keep_ref[to : to + half, :] = added(job, base, half, half, bit)
                    send_ref[offset + to : offset + to + half, :] = added(job, base, half, half, 1 - bit)
                    to += half
            elif job.kind == "split":
                half, keep_ref = job.sent, keep_refs.pop(0)
                keep_ref[...] = added(job, 0, half, half, bit)
                send_ref[offset : offset + half, :] = added(job, 0, half, half, 1 - bit)
            else:
                keep_ref, each = keep_refs.pop(0), job.each
                for q in range(job.count // 2):
                    keep_ref[q * each : (q + 1) * each, :] = added(job, 2 * q * each, each, each, bit)
                    send_ref[offset + q * each : offset + (q + 1) * each, :] = added(
                        job, 2 * q * each, each, each, 1 - bit
                    )
                done, base = job.count // 2 * each, job.count * each
                rest = added(job, base, rows - base)
                keep_ref[done:, :] = rest
                send_ref[offset + done : offset + job.sent, :] = rest

    outs = [sds((total, width), BF)] + [sds((job.kept, width), BF) for job in jobs if job.keeps]
    send, *keeps = line.call(kernel, arrays, outs, scalars=(place,), weight=GLUE)
    owns = []
    for job, offset in zip(jobs, offsets):
        owns.append(View(keeps.pop(0)) if job.keeps else View(send, offset, job.sent))
    return send, owns, offsets


class Chains:
    def __init__(self, line, place):
        self.line, self.place = line, place
        self.walks, self.jobs, self.done = {}, {}, {}

    def take(self, name, value):
        try:
            self.jobs[name] = self.walks[name].send(value)
        except StopIteration as end:
            self.done[name] = end.value
            del self.walks[name]

    def begin(self, name, walk):
        self.walks[name] = walk
        self.take(name, None)

    def advance(self, *names):
        names = [name for name in names if name in self.walks]
        while names:
            key = self.jobs[names[0]].key
            group = [name for name in names if self.jobs[name].key == key]
            names = [name for name in names if name not in group]
            jobs = [self.jobs[name] for name in group]
            send, owns, offsets = glue(self.line, self.place, jobs)
            if key[0] == "tok":
                others = exchange([send] * lax.axis_size("tok"), "tok")
            else:
                others = [swap(send, key)]
            for name, job, own, offset in zip(group, jobs, owns, offsets):
                self.take(name, [own] + [View(other, offset, job.sent) for other in others])

    def finish(self, name):
        while name in self.walks:
            self.advance(name)
        return self.done[name]


def chunk_walk(views, mirror, count, each):
    order = [("dp", (s + mirror) % 2) for s in range(bits(lax.axis_size("dp")))]
    experts = [("expert", s) for s in range(bits(lax.axis_size("expert")))]
    halved = []
    for key in order + experts[:-1]:
        if each < 32:
            break
        views = yield Job("halve", views, key, place_row(key), count, each)
        each //= 2
        halved.append(key)
    for key in (order + experts)[len(halved) :]:
        views = yield Job("add", views, key)
    views = [views]
    for key in reversed(halved):
        if len(views) == 1:
            views = yield Job("add", views[0], key)
        else:
            views = yield Job("weave", views, key, place_row(before), count, each)
            each *= 2
        before = key
    views = yield Job("weave", views, ("tok", 0), place_row(before), count, each)
    return views


def tail_walk(views, experts, each, mirror):
    stages = bits(lax.axis_size("dp"))
    order = [("dp", (s + mirror) % 2) for s in range(stages)]
    halves = each >> stages >= 16
    for key in order if halves else ():
        views = yield Job("halve", views, key, place_row(key), experts, each)
        each //= 2
    for stage in range(bits(experts)):
        key = ("expert", stage)
        views = yield Job("pick", views, key, place_row(key), experts >> stage, each)
    before = None
    for key in reversed(order):
        if before is None or not halves:
            views = yield Job("add", views, key)
        else:
            views = yield Job("weave", views, key, place_row(before), 1, each)
            each *= 2
        before = key
    if halves:
        views = yield Job("weave", views, ("tok", 0), place_row(before), 1, each)
    else:
        views = yield Job("add", views, ("tok", 0))
    return views


def place_part(line, place, view, turn, first, hidden, full, before):
    rows, width = view.rows, view.array.shape[1]
    many = hidden // width
    block = rows // many

    def kernel(part_ref, place_ref, _, wide_ref, send, gin_ref, gout_ref):
        part = place_ref[0] ^ turn
        for i in range(many):
            span = slice(i * block, (i + 1) * block)
            wide_ref[span, :] = part_ref[
                view.start + i * block : view.start + (i + 1) * block, :
            ].astype(F32)
            column, at = first + i * width, part * block
            to = pl.multiple_of(column + jnp.minimum(at, width - block), block)
            row = pl.multiple_of(jnp.maximum(at - width, 0), block)
            send(
                wide_ref.at[span, :],
                gout_ref.at[pl.ds(to, block), :],
                gin_ref.at[pl.ds(row, block), column : column + width],
                at < width,
            )

    _, *grads = line.call(
        kernel,
        (view.array,),
        (),
        scalars=(place,),
        scratch=(sds((rows, width), F32),),
        sent=(sds((width, full), F32), sds((full, width), F32)),
        aliased=before,
    )
    return tuple(grads)


def place_tail(line, place, views, experts, head, misc):
    peers = len(views)
    parts = [view.array for view in views]
    pair, width = 2 * head, parts[0].shape[1]
    each, share = pair // peers, misc // peers

    def last(*refs):
        part_refs, place_ref = refs[:peers], refs[peers]
        query_ref, output_ref, kv_ref, router_ref, one_ref, two_ref, pair_ref, misc_ref = refs[
            peers + 1 :
        ]
        for k, view in enumerate(views):
            part, start = place_ref[0] ^ k, view.start
            pair_ref[pl.ds(part * each, each), :] = part_refs[k][start : start + each, :].astype(F32)
            misc_ref[pl.ds(part * share, share), :] = part_refs[k][
                start + each : start + view.rows, :
            ].astype(F32)
        query_ref[0] = pair_ref[:head, :]
        output_ref[0] = pair_ref[head:, :]
        kv_ref[...] = misc_ref[:pair, :].T
        router_ref[...] = misc_ref[pair : pair + experts, :]
        one_ref[...] = misc_ref[pair + experts : pair + experts + 1, :]
        two_ref[...] = misc_ref[pair + experts + 1 : pair + experts + 2, :]

    return line.call(
        last,
        parts,
        [
            sds((1, head, width), F32),
            sds((1, head, width), F32),
            sds((width, pair), F32),
            sds((experts, width), F32),
            sds((1, width), F32),
            sds((1, width), F32),
        ],
        scalars=(place,),
        scratch=(sds((pair, width), F32), sds((misc, width), F32)),
    )


def join_all(line, arrays):
    rows, width = arrays[0].shape
    count = len(arrays)

    def kernel(*refs):
        for k in range(count):
            refs[count][k * rows : (k + 1) * rows, :] = refs[k][...]

    return line.call(kernel, arrays, [sds((count * rows, width), BF)])[0]


def body(
    tokens, out_grad, expert_ids, sentence_ids, ln_attn, w_kv, w_router, w_query, w_output, ln_ffn, w_in, w_out
):
    length, width = tokens.shape
    head = w_query.shape[2]
    pair = w_kv.shape[1]
    full = w_in.shape[1]
    experts = lax.axis_size("expert")
    peers = lax.axis_size("tok")
    choose = expert_ids.shape[1]
    tok, dp, expert = lax.axis_index("tok"), lax.axis_index("dp"), lax.axis_index("expert")
    stages = bits(lax.axis_size("dp"))
    dp_bits = [(dp >> ((s + tok) % stages)) & 1 for s in range(stages)]
    spots = jnp.stack(
        [tok, expert] + dp_bits + [(expert >> s) & 1 for s in range(bits(experts))]
    ).astype(jnp.int32)
    weights = jnp.concatenate([w_query[0].T, w_output[0]], axis=0)
    each = weights.shape[0] // peers
    weights = lax.dynamic_slice_in_dim(weights, tok * each, each, axis=0)
    pieces = exchange([weights] * experts, "expert")
    ids = expert_ids.T
    ln_one = ln_attn.reshape(1, width)
    ln_two = ln_ffn.reshape(1, width)
    line = Line()
    line.last = spots
    (
        normed, kv, kvt, gates, gt, small, sent, gains, keyid, place, ids, own_query, own_output, x, g, out_weight,
    ) = line.call(
        prepare_kernel,
        (),
        [
            sds((length, width), BF),
            sds((length, pair), BF),
            sds((pair, length), BF),
            sds((choose, length), F32),
            sds((width, length), BF),
            sds((pair + 16, width), BF),
            sds((1, length), F32),
            sds((2, width), F32),
            sds((length, BAND), F32),
            sds((8, 128), jnp.int32),
        ],
        fetched=(ln_one, w_kv, w_router.T, sentence_ids, ln_two),
        numbers=(spots,),
        kept=(ids, w_query[0].T, w_output[0], tokens, out_grad, w_out),
        room=8 << 20,
    )
    ag, in_weight = line.call(
        upstream_kernel, (g, out_weight), [sds((length, full), BF)], kept=(w_in,), room=8 << 20,
    )
    slab = join_all(line, pieces)
    slabs = [slab] + exchange([slab] * peers, "tok")
    wq, wo, qt, at, lse, gat, h, hn, hnt = line.call(
        functools.partial(attend_kernel, experts=experts, head=head, peers=peers),
        (*slabs, normed, kv, kvt, gates, x, ids, sent, gains, keyid, own_query, own_output),
        [
            sds((experts * head, width), BF),
            sds((experts * head, width), BF),
            sds((head, choose * length), BF),
            sds((head, choose * length), BF),
            sds((1, choose * length), F32),
            sds((experts * head, length), BF),
            sds((length, width), F32),
            sds((length, width), BF),
            sds((width, length), BF),
        ],
        scalars=(place,),
        scratch=(
            sds((experts * head, length), F32),
            sds((2 * head, width), BF),
            sds((length // BAND, 3 * BAND, choose * BAND), F32),
            sds((length // BAND, 3 * BAND, choose * BAND), BF),
        ),
        room=8 << 20,
    )

    chains = Chains(line, place)
    us, dpres, sums, spans = [], [], [], {}

    def ffn(last=None, mirror=0):
        rows = 2 * width // peers
        pieces = max(1, rows // PIECE)
        rows = rows // pieces
        u, dpre, *parts = line.call(
            functools.partial(ffn_kernel, first=len(us) * width, peers=peers),
            (hn, hnt, gt, ag, in_weight),
            [sds((length, width), BF)] * 2 + [sds((rows, width), BF)] * (peers * pieces),
            scalars=(place,),
            scratch=() if peers == 2 else (sds((2 * width, width), BF),),
            room=6 << 20,
        )
        us.append(u)
        dpres.append(dpre)
        for i in range(pieces):
            sums.append([parts[i]] + exchange(parts[i::pieces], "tok"))
        if last is not None:
            views = [View(same[0], more=same[1:]) for same in zip(*sums)]
            chains.begin(last, chunk_walk(views, mirror, len(sums), rows))
            hidden = len(sums) // pieces * width
            spans[last] = (len(us) * width - hidden, hidden)
            sums.clear()

    misc = -(-(pair + 16) // (64 * peers)) * 64 * peers

    def hidden():
        made["dh"], made["low"], made["gain"] = line.call(
            hidden_kernel,
            (h, g, in_weight, gains, *dpres),
            [sds((length, width), F32), sds((length, width), BF), sds((1, width), F32)],
            room=6 << 20,
        )

    def heads_back():
        made["z"], made["gout"] = line.call(
            functools.partial(heads_back_kernel, experts=experts, head=head),
            (kv, kvt, gates, wo, qt, at, lse, gat, made["low"], ids, sent, keyid),
            [sds((experts * head + pair + 16, length), BF), sds((experts * head, width), BF)],
            scratch=(
                sds((experts * head, length), F32),
                sds((pair, length), F32),
                sds((head, choose * length), BF),
                *[sds((length // BAND, 3 * BAND, choose * BAND), t) for t in (F32, F32, BF, BF)],
            ),
            room=6 << 20,
        )

    def rows_back():
        *parts, made["dx"] = line.call(
            functools.partial(rows_back_kernel, experts=experts, head=head, peers=peers, misc=misc),
            (made["z"], made["gout"], normed, wq, small, made["dh"], made["gain"], x, gains),
            ([sds((2 * pair // peers, width), BF)] * (experts // 2) + [sds((misc // peers, width), BF)])
            * peers,
            sent=(sds((length, width), BF),),
            scalars=(place,),
            scratch=(
                sds((experts * head + pair + 16, width), F32),
                sds((experts * pair, width), BF),
                sds((misc, width), F32),
                sds((length, width), BF),
            ),
            room=6 << 20,
        )
        chains.begin("t", tail_walk(tok_views(parts, peers), experts, pair // peers, 1))

    def out():
        _, made["output"] = line.call(
            output_kernel,
            (h, out_weight, *us),
            (),
            sent=(sds((length, width), BF),),
            scratch=(sds((length, width), BF),),
            room=6 << 20,
        )

    def place_one(name, turn):
        if turn == 0:
            made[name] = chains.finish(name)
        views = made[name][:1] if turn == 0 else made[name][1:]
        for view in views:
            made["both"] = place_part(
                line, place, view, turn, *spans[name], full, made.get("both", ())
            )
            turn += 1

    def last():
        made["t"] = place_tail(line, place, chains.finish("t"), experts, head, misc)

    made = {}
    acts = {"f": ffn, "n": hidden, "h": heads_back, "r": rows_back, "o": out, "T": last}
    for i, name in enumerate("abc"):
        acts[name.upper()] = functools.partial(ffn, name, i % 2)
        acts[str(2 * i + 1)] = functools.partial(place_one, name, 0)
        acts[str(2 * i + 2)] = functools.partial(place_one, name, 1)
    for word in ORDER:
        if word in acts:
            acts[word]()
        else:
            chains.advance(*word)
    query, outp, kv_grad, router, one, two = made["t"]
    output, dx, both = made["output"], made["dx"], made["both"]
    return (
        output,
        dx,
        one.reshape(width),
        kv_grad,
        router.T,
        jnp.swapaxes(query, 1, 2),
        outp,
        two.reshape(width),
        both[0],
        both[1],
    )


def solution(mesh):
    rows = P(AXES, None)
    heads = P("expert", None, None)
    return jax.shard_map(
        body,
        mesh=mesh,
        in_specs=(rows, rows, rows, rows, P(), P(), P(), heads, heads, P(), P(), P()),
        out_specs=(rows, rows, P(), P(), P(), heads, heads, P(), P(), P()),
        check_vma=False,
    )
```

```python
import functools

import jax
import jax.numpy as jnp
from jax import lax
from jax.experimental import pallas as pl
from jax.experimental.pallas import tpu as pltpu
from jax.sharding import PartitionSpec as P

BF = jnp.bfloat16
F32 = jnp.float32
MASKED = -1e30
BAND = 128
ROWS = 256
PIECE = 512
AXES = ("dp", "expert", "tok")
GLUE = 23 * 10**9
WORK = 1
ORDER = (
    "f", "A", "f", "a", "B", "n", "a", "b", "h", "a", "r", "b", "a", "o", "b", "t", "a", "b", "t",
    "a", "t", "b", "a", "t", "b", "t", "b", "1", "t", "2", "t", "3", "T",
)


def nn(left, right):
    return lax.dot_general(left, right, (((1,), (0,)), ((), ())), preferred_element_type=F32)


def nt(left, right):
    return lax.dot_general(left, right, (((1,), (1,)), ((), ())), preferred_element_type=F32)


def tn(left, right):
    return lax.dot_general(left, right, (((0,), (0,)), ((), ())), preferred_element_type=F32)


def normalize(values):
    centre = values - jnp.mean(values, axis=-1, keepdims=True)
    spread = jnp.mean(centre * centre, axis=-1, keepdims=True)
    inverse = lax.rsqrt(spread + 1e-05)
    return centre * inverse, inverse


def normalize_back(upstream, normalized, inverse, gain):
    scaled = upstream * gain
    inner = (
        scaled
        - jnp.mean(scaled, axis=-1, keepdims=True)
        - normalized * jnp.mean(scaled * normalized, axis=-1, keepdims=True)
    )
    return inner * inverse


def sds(shape, dtype):
    return jax.ShapeDtypeStruct(shape, dtype)


def size_of(array):
    lanes = -(-array.shape[-1] // 128) * 128
    rows = -(-array.shape[-2] // 16) * 16
    lead = 1
    for extent in array.shape[:-2]:
        lead = lead * extent
    return lead * rows * lanes * jnp.dtype(array.dtype).itemsize


class Place:
    def __init__(self, ref):
        self.ref = ref

    def __getitem__(self, row):
        return self.ref[row, 0]


class Line:
    def __init__(self):
        self.last = None

    def call(
        self, kernel, operands, outs, fetched=(), scalars=(), scratch=(), room=2 << 20, weight=WORK,
        sent=(), aliased=(), kept=(), numbers=(), delayed=0, copies=8,
    ):
        n, f, s = len(operands), len(fetched) + len(kept), len(scalars)
        late = () if self.last is None else (self.last,)
        skip = len(late) + len(aliased)
        outs = list(outs)
        h = len(sent)
        if not outs:
            outs = [sds((8, 128), F32)]
        outs = outs + [sds(a.shape, a.dtype) for a in kept]
        scratch_copies, fetched = len(fetched), (*fetched, *kept)

        def wrapped(*refs):
            ins = refs[:n]
            sources = refs[n : n + f]
            smem = [Place(ref) for ref in refs[n + f : n + f + s]]
            rest = list(refs[n + f + s + len(numbers) + skip :])
            if numbers:
                number_sem, number_ref = rest.pop(), rest.pop()
                number = pltpu.make_async_copy(refs[n + f + s], number_ref, number_sem.at[0])
                number.start()

                def number_wait():
                    number.wait()
                    return number_ref

                smem = smem + [number_wait]
            far = rest[len(outs) : len(outs) + h]
            del rest[len(outs) : len(outs) + h]
            open_copies, send_sem = [], rest.pop() if h else None
            sems = rest.pop() if f else None
            buffers = rest[len(rest) - scratch_copies :] if scratch_copies else []
            del rest[len(rest) - scratch_copies :]
            first = len(outs) - len(kept)
            buffers = buffers + rest[first : len(outs)]
            del rest[first : len(outs)]
            body, waits, waiting = rest, [], {}
            for i in range(f):
                copy = pltpu.make_async_copy(sources[i], buffers[i], sems.at[i])
                if i < f - delayed:
                    copy.start()
                waiting[i] = copy

                def wait(i=i):
                    if i in waiting:
                        waiting.pop(i).wait()
                        if i == f - delayed - 1:
                            for j in range(f - delayed, f):
                                waiting[j].start()
                    return buffers[i]

                waits.append(wait)
            def send(source, target, other=None, near=None):
                sem = send_sem.at[len(open_copies)]
                copy = pltpu.make_async_copy(source, target, sem)
                open_copies.append(copy)
                if other is None:
                    copy.start()
                    return
                pl.when(near)(copy.start)
                pl.when(jnp.logical_not(near))(pltpu.make_async_copy(source, other, sem).start)

            if h:
                kernel(*ins, *waits, *smem, *body, send, *far)
                for copy in open_copies:
                    copy.wait()
            else:
                kernel(*ins, *waits, *smem, *body)
            for copy in waiting.values():
                copy.wait()

        need = sum(size_of(a) for a in (*fetched[:scratch_copies], *scratch))
        extra = [pltpu.VMEM(a.shape, a.dtype) for a in fetched[:scratch_copies]]
        if f:
            extra.append(pltpu.SemaphoreType.DMA((f,)))
        if h:
            extra.append(pltpu.SemaphoreType.DMA((copies,)))
        if numbers:
            extra += [pltpu.SMEM(numbers[0].shape, jnp.int32), pltpu.SemaphoreType.DMA((1,))]
        results = pl.pallas_call(
            wrapped,
            out_shape=outs + list(sent),
            in_specs=[pl.BlockSpec(memory_space=pltpu.VMEM)] * n
            + [pl.BlockSpec(memory_space=pltpu.HBM)] * f
            + [pl.BlockSpec(memory_space=pltpu.VMEM)] * s
            + [pl.BlockSpec(memory_space=pl.ANY)] * len(numbers)
            + [pl.BlockSpec(memory_space=pl.ANY)] * skip,
            out_specs=[pl.BlockSpec(memory_space=pltpu.VMEM)] * len(outs)
            + [pl.BlockSpec(memory_space=pltpu.HBM)] * h,
            input_output_aliases={
                n + f + s + len(numbers) + len(late) + i: len(outs) + i for i in range(len(aliased))
            },
            scratch_shapes=[pltpu.VMEM(a.shape, a.dtype) for a in scratch] + extra,
            compiler_params=pltpu.CompilerParams(vmem_limit_bytes=need + room),
            cost_estimate=pl.CostEstimate(flops=weight, bytes_accessed=1024, transcendentals=0),
        )(
            *operands,
            *[pltpu.with_memory_space_constraint(a, pltpu.HBM) for a in fetched],
            *scalars,
            *numbers,
            *late,
            *aliased,
        )
        self.last = min(results[: len(outs)], key=lambda a: a.size)
        return results


def prepare_kernel(
    ln_wait, wkv_wait, wr_wait, sent_wait, ln_two_wait, ids_wait, wq_wait, wo_wait, x_wait, g_wait, wout_wait,
    spots_wait, xn_ref, kv_ref, kvt_ref, gates_ref, gt_ref, small_ref, sent_keep, gains_keep, keyid_ref,
    place_ref,
):
    ln_ref, ln_two_ref, sent_ref = ln_wait(), ln_two_wait(), sent_wait()
    gain = ln_ref[...]
    gains_keep[0:1, :] = gain
    gains_keep[1:2, :] = ln_two_ref[...]
    sent_keep[...] = sent_ref[...].astype(F32)
    column_ids(sent_keep, keyid_ref)
    wkv_ref, wr_ref, ids_ref = wkv_wait(), wr_wait(), ids_wait()
    pair = wkv_ref.shape[1]
    experts = wr_ref.shape[0]
    small_ref[:pair, :] = wkv_ref[...].T
    small_ref[pair:, :] = jnp.concatenate(
        [wr_ref[...].astype(F32), jnp.zeros((16 - experts, wr_ref.shape[1]), F32)], axis=0
    ).astype(BF)
    spots_ref = spots_wait()
    for i in range(spots_ref.shape[0]):
        place_ref[i : i + 1, :] = jnp.full((1, place_ref.shape[1]), spots_ref[i], jnp.int32)
    x_ref = x_wait()
    length = x_ref.shape[0]
    for start in range(0, length, ROWS):
        rows = pl.ds(start, ROWS)
        normalized, _ = normalize(x_ref[rows, :].astype(F32))
        xn_ref[rows, :] = (normalized * gain).astype(BF)
    normed = xn_ref[...]
    small = small_ref[...]
    both = nt(small, normed)
    kvt_ref[...] = both[:pair].astype(BF)
    kv_ref[...] = nn(normed, wkv_ref[...]).astype(BF)
    choose = ids_ref.shape[0]
    picked = []
    for route in range(choose):
        ids = ids_ref[route : route + 1, :]
        value = jnp.zeros((1, length), F32)
        for expert in range(experts):
            value = jnp.where(ids == expert, both[pair + expert : pair + expert + 1], value)
        picked.append(value)
    top = functools.reduce(jnp.maximum, picked)
    raised = [jnp.exp(value - top) for value in picked]
    total = functools.reduce(lambda a, b: a + b, raised)
    for route in range(choose):
        gates_ref[route : route + 1, :] = raised[route] / total
    g_ref = g_wait()
    gt_ref[...] = g_ref[...].T


def upstream_kernel(g_ref, wout_ref, win_wait, ag_ref):
    for start in range(0, g_ref.shape[0], ROWS):
        rows = slice(start, start + ROWS)
        ag_ref[rows, :] = nt(g_ref[rows, :], wout_ref[...]).astype(BF)


def column_ids(sent_ref, keyid_ref):
    length = sent_ref.shape[1]
    for start in range(0, length, BAND):
        row = jnp.broadcast_to(sent_ref[:, start : start + BAND], (BAND, BAND))
        keyid_ref[pl.ds(start, BAND), :] = row.T


def masked_scores(kv_ref, keyid_ref, sent_ref, queries, start, low, high, choose):
    padded = jnp.concatenate([queries * 0.125, jnp.zeros_like(queries)], axis=0)
    scores = nn(kv_ref[low:high, :], padded)
    same = keyid_ref[low:high, :] == sent_ref[:, start : start + BAND]
    parts = [
        jnp.where(same, scores[:, route * BAND : (route + 1) * BAND], MASKED)
        for route in range(choose)
    ]
    return jnp.concatenate(parts, axis=1)


def window(start, length):
    return max(start - BAND, 0), min(start + 2 * BAND, length)


def attend_kernel(*refs, experts, head, peers):
    slab_refs, refs = refs[:peers], refs[peers:]
    (
        xn_ref, kv_ref, kvt_ref, gates_ref, x_ref, ids_ref, sent_ref, ln_ref, keyid_ref, wq_own, wo_own,
        place_ref, wq_ref, wo_ref, qt_ref, at_ref, lse_ref, gat_ref, h_ref, hn_ref, hnt_ref, all_ref,
        pair_ref, score_ref, prob_ref,
    ) = refs
    own = place_ref[1]
    each = 2 * head // peers
    wq_ref[pl.ds(own * head, head), :] = wq_own[...]
    wo_ref[pl.ds(own * head, head), :] = wo_own[...]
    for k in range(1, experts):
        for j in range(peers):
            rows = pl.ds((place_ref[0] ^ j) * each, each)
            pair_ref[rows, :] = slab_refs[j][(k - 1) * each : k * each, :]
        rows = pl.ds((own ^ k) * head, head)
        wq_ref[rows, :] = pair_ref[:head, :]
        wo_ref[rows, :] = pair_ref[head:, :]
    length = xn_ref.shape[0]
    choose = ids_ref.shape[0]
    all_ref[...] = nt(wq_ref[...], xn_ref[...])
    starts = range(0, length, BAND)
    spans = [slice(start * choose, (start + BAND) * choose) for start in starts]
    bounds = [window(start, length) for start in starts]
    for start, block in zip(starts, spans):
        lanes = slice(start, start + BAND)
        chosen = []
        for route in range(choose):
            ids = ids_ref[route : route + 1, lanes]
            value = all_ref[:head, lanes]
            for expert in range(1, experts):
                value = jnp.where(
                    ids == expert, all_ref[expert * head : (expert + 1) * head, lanes], value
                )
            chosen.append(value)
        qt_ref[:, block] = jnp.concatenate(chosen, axis=1).astype(BF)
    for i, start in enumerate(starts):
        low, high = bounds[i]
        score_ref[i, : high - low, :] = masked_scores(
            kv_ref, keyid_ref, sent_ref, qt_ref[:, spans[i]], start, low, high, choose
        )
    for i, block in enumerate(spans):
        size = bounds[i][1] - bounds[i][0]
        scores = score_ref[i, :size, :]
        largest = jnp.max(scores, axis=0, keepdims=True)
        raised = jnp.exp(scores - largest)
        total = jnp.sum(raised, axis=0, keepdims=True)
        prob_ref[i, :size, :] = (raised * (1.0 / total)).astype(BF)
        lse_ref[:, block] = largest + jnp.log(total)
    for i, block in enumerate(spans):
        low, high = bounds[i]
        at_ref[:, block] = nn(kvt_ref[head:, low:high], prob_ref[i, : high - low, :]).astype(BF)
    for start in starts:
        lanes = slice(start, start + BAND)
        spread = [jnp.zeros((head, BAND), F32) for _ in range(experts)]
        for route in range(choose):
            ids = ids_ref[route : route + 1, lanes]
            first = start * choose + route * BAND
            gated = at_ref[:, first : first + BAND].astype(F32) * gates_ref[route : route + 1, lanes]
            for expert in range(experts):
                spread[expert] = jnp.where(ids == expert, gated, spread[expert])
        for expert in range(experts):
            gat_ref[expert * head : (expert + 1) * head, lanes] = spread[expert].astype(BF)
    gain = ln_ref[1:2, :]
    for start in range(0, length, ROWS):
        rows = slice(start, start + ROWS)
        mixed = tn(gat_ref[:, rows], wo_ref[...])
        hidden = x_ref[rows, :].astype(F32) + mixed
        h_ref[rows, :] = hidden
        normalized, _ = normalize(hidden)
        low_value = (normalized * gain).astype(BF)
        hn_ref[rows, :] = low_value
        hnt_ref[:, rows] = low_value.T


def gelu_both(values):
    bell = jnp.exp2(values * values * -0.7213475204444817)
    t = 1.0 / (1.0 + 0.23164188 * jnp.abs(values))
    poly = t * (
        0.127414796
        + t * (-0.142248368 + t * (0.7107068705 + t * (-0.7265760135 + t * 0.5307027145)))
    )
    tail = poly * bell
    cumulative = jnp.where(values >= 0.0, 1.0 - tail, tail)
    return values * cumulative, cumulative + values * (bell * 0.3989422804014327)


def ffn_block(refs, first):
    hn_ref, hnt_ref, gt_ref, ag_ref, win_ref, u_ref, dpre_ref = refs
    length, width = hn_ref.shape
    far = slice(first, first + width)
    out_grad = in_grad = None
    for start in range(0, length, 2 * ROWS):
        rows = slice(start, start + 2 * ROWS)
        activated, slope = gelu_both(nn(hn_ref[rows, :], win_ref[:, far]))
        activated = activated.astype(BF)
        before = (ag_ref[rows, far].astype(F32) * slope).astype(BF)
        u_ref[rows, :], dpre_ref[rows, :] = activated, before
        out_part, in_part = nn(gt_ref[:, rows], activated), nn(hnt_ref[:, rows], before)
        out_grad = out_part if out_grad is None else out_grad + out_part
        in_grad = in_part if in_grad is None else in_grad + in_part
    return out_grad.astype(BF).T, in_grad.astype(BF)


def ffn_kernel(*refs, first, peers):
    place_ref, part_refs = refs[5], list(refs[8:])
    width = refs[0].shape[1]
    tok = place_ref[0]
    out_grad, in_grad = ffn_block((*refs[:5], *refs[6:8]), first)
    if peers == 2:
        pieces = len(part_refs) // 2
        size = part_refs[0].shape[0]
        for i in range(pieces):
            span = slice(i * size, (i + 1) * size)
            one, two = out_grad[span, :], in_grad[span, :]
            part_refs[i][...] = jnp.where(tok == 0, one, two)
            part_refs[pieces + i][...] = jnp.where(tok == 0, two, one)
        return
    sum_ref = part_refs.pop()
    sum_ref[:width, :], sum_ref[width:, :] = out_grad, in_grad
    size = part_refs[0].shape[0]
    pieces = len(part_refs) // peers
    for k in range(peers):
        for i in range(pieces):
            start = (tok ^ k) * size * pieces + i * size
            part_refs[k * pieces + i][...] = sum_ref[pl.ds(start, size), :]


def output_kernel(*refs):
    h_ref, wout_ref = refs[:2]
    out_ref, send, far_ref = refs[-3:]
    u_refs = refs[2:-4]
    for start in range(0, h_ref.shape[0], ROWS):
        rows = slice(start, start + ROWS)
        total, first = h_ref[rows, :], 0
        for ref in u_refs:
            size = ref.shape[1]
            total = total + nn(ref[rows, :], wout_ref[first : first + size, :])
            first = first + size
        out_ref[rows, :] = total.astype(BF)
        send(out_ref.at[rows, :], far_ref.at[rows, :])


def hidden_kernel(*refs):
    h_ref, g_ref, win_ref, ln_ref = refs[:4]
    dh_ref, low_ref, gain_ref = refs[-3:]
    dpre_refs = refs[4:-3]
    gain = ln_ref[1:2, :]
    gain_sum = jnp.zeros_like(gain)
    for start in range(0, h_ref.shape[0], ROWS):
        rows = slice(start, start + ROWS)
        upstream, first = None, 0
        for ref in dpre_refs:
            size = ref.shape[1]
            part = nt(ref[rows, :], win_ref[:, first : first + size])
            upstream = part if upstream is None else upstream + part
            first = first + size
        normalized, inverse = normalize(h_ref[rows, :])
        value = g_ref[rows, :].astype(F32) + normalize_back(upstream, normalized, inverse, gain)
        dh_ref[rows, :] = value
        low_ref[rows, :] = value.astype(BF)
        gain_sum = gain_sum + jnp.sum(upstream * normalized, axis=0, keepdims=True)
    gain_ref[...] = gain_sum


def heads_back_kernel(
    kv_ref, kvt_ref, gates_ref, wo_ref, qt_ref, at_ref, lse_ref, gat_ref, low_ref, ids_ref, sent_ref,
    keyid_ref, z_ref, gout_ref, all_ref, dkv_ref, up_ref, prob_ref, grad_ref, soft_ref, ds_ref, *, experts,
    head,
):
    length = kv_ref.shape[0]
    wide, pair = experts * head, 2 * head
    choose = ids_ref.shape[0]
    all_ref[...] = nt(wo_ref[...], low_ref[...])
    gout_ref[...] = nn(gat_ref[...], low_ref[...]).astype(BF)
    dkv_ref[...] = jnp.zeros_like(dkv_ref)
    starts = range(0, length, BAND)
    spans = [slice(start * choose, (start + BAND) * choose) for start in starts]
    bounds = [window(start, length) for start in starts]
    for start, block in zip(starts, spans):
        lanes = slice(start, start + BAND)
        raw, gate_grads = [], []
        for route in range(choose):
            ids = ids_ref[route : route + 1, lanes]
            value = all_ref[:head, lanes]
            for expert in range(1, experts):
                value = jnp.where(
                    ids == expert, all_ref[expert * head : (expert + 1) * head, lanes], value
                )
            raw.append(value)
            first = start * choose + route * BAND
            attended = at_ref[:, first : first + BAND].astype(F32)
            gate_grads.append(jnp.sum(value * attended, axis=0, keepdims=True))
        gates = [gates_ref[route : route + 1, lanes] for route in range(choose)]
        common = functools.reduce(
            lambda a, b: a + b, [gate * grad for gate, grad in zip(gates, gate_grads)]
        )
        logit_rows = [jnp.zeros((1, BAND), F32) for _ in range(experts)]
        for route in range(choose):
            ids = ids_ref[route : route + 1, lanes]
            picked = gates[route] * (gate_grads[route] - common)
            for expert in range(experts):
                logit_rows[expert] = jnp.where(ids == expert, picked, logit_rows[expert])
        logit_pad = jnp.concatenate(
            logit_rows + [jnp.zeros((16 - experts, BAND), F32)], axis=0
        )
        z_ref[wide + pair :, lanes] = logit_pad.astype(BF)
        up_ref[:, block] = jnp.concatenate(
            [gate * value for gate, value in zip(gates, raw)], axis=1
        ).astype(BF)
    for i, start in enumerate(starts):
        low, high = bounds[i]
        prob_ref[i, : high - low, :] = masked_scores(
            kv_ref, keyid_ref, sent_ref, qt_ref[:, spans[i]], start, low, high, choose
        )
        upstream = up_ref[:, spans[i]]
        padded = jnp.concatenate([jnp.zeros_like(upstream), upstream], axis=0)
        grad_ref[i, : high - low, :] = nn(kv_ref[low:high, :], padded)
    for i, block in enumerate(spans):
        size = bounds[i][1] - bounds[i][0]
        probs = jnp.exp(prob_ref[i, :size, :] - lse_ref[:, block])
        soft_ref[i, :size, :] = probs.astype(BF)
        prob_grad = grad_ref[i, :size, :]
        mean = jnp.sum(probs * prob_grad, axis=0, keepdims=True)
        ds_ref[i, :size, :] = (probs * (prob_grad - mean)).astype(BF)
    for i, start in enumerate(starts):
        low, high = bounds[i]
        lanes = slice(start, start + BAND)
        score_grad = ds_ref[i, : high - low, :]
        query_grad = (nn(kvt_ref[:head, low:high], score_grad) * 0.125).astype(BF)
        spread = [jnp.zeros((head, BAND), BF) for _ in range(experts)]
        for route in range(choose):
            ids = ids_ref[route : route + 1, lanes]
            piece = query_grad[:, route * BAND : (route + 1) * BAND]
            for expert in range(experts):
                spread[expert] = jnp.where(ids == expert, piece, spread[expert])
        for expert in range(experts):
            z_ref[expert * head : (expert + 1) * head, lanes] = spread[expert]
        dkv_ref[:head, low:high] += nt(qt_ref[:, spans[i]], score_grad) * 0.125
        dkv_ref[head:, low:high] += nt(up_ref[:, spans[i]], soft_ref[i, : high - low, :])
    z_ref[wide : wide + pair, :] = dkv_ref[...].astype(BF)


def rows_back_kernel(*refs, experts, head, peers, misc):
    (
        z_ref, gout_ref, xn_ref, wq_ref, small_ref, dh_ref, gain_two_ref, x_ref, ln_ref, place_ref,
    ) = refs[:10]
    pieces = experts // 2 + 1
    part_refs = refs[10 : 10 + peers * pieces]
    grads_ref, pair_ref, misc_ref, dx_ref, send, far_ref = refs[10 + peers * pieces :]
    length = xn_ref.shape[0]
    wide, pair = experts * head, 2 * head
    grads_ref[...] = nn(z_ref[...], xn_ref[...])
    for expert in range(experts):
        rows = slice(expert * head, (expert + 1) * head)
        pair_ref[expert * pair : expert * pair + head, :] = grads_ref[rows, :].astype(BF)
        pair_ref[expert * pair + head : (expert + 1) * pair, :] = gout_ref[rows, :]
    gain = ln_ref[0:1, :]
    total = jnp.zeros_like(gain)
    for start in range(0, length, ROWS):
        rows = slice(start, start + ROWS)
        normed_grad = tn(z_ref[:wide, rows], wq_ref[...]) + tn(z_ref[wide:, rows], small_ref[...])
        normalized, inverse = normalize(x_ref[rows, :].astype(F32))
        total = total + jnp.sum(normed_grad * normalized, axis=0, keepdims=True)
        back = normalize_back(normed_grad, normalized, inverse, gain)
        dx_ref[rows, :] = (dh_ref[rows, :] + back).astype(BF)
        send(dx_ref.at[rows, :], far_ref.at[rows, :])
    misc_ref[...] = jnp.zeros_like(misc_ref)
    misc_ref[:pair, :] = grads_ref[wide : wide + pair, :]
    misc_ref[pair : pair + 16, :] = jnp.concatenate(
        [
            grads_ref[wide + pair : wide + pair + experts, :],
            total,
            gain_two_ref[...],
            jnp.zeros((14 - experts, total.shape[1]), F32),
        ],
        axis=0,
    )
    each, share = pair // peers, misc // peers
    for k in range(peers):
        part = place_ref[0] ^ k
        for expert in range(experts):
            rows = pl.ds(expert * pair + part * each, each)
            low = expert % 2 * each
            part_refs[k * pieces + expert // 2][low : low + each, :] = pair_ref[rows, :]
        part_refs[(k + 1) * pieces - 1][...] = misc_ref[pl.ds(part * share, share), :].astype(BF)


def exchange(parts, axis):
    size = len(parts)
    return [
        lax.ppermute(parts[k], axis, [(i, i ^ k) for i in range(size)]) for k in range(1, size)
    ]


def tok_views(parts, peers):
    pieces = len(parts) // peers
    others = [exchange(parts[i::pieces], "tok") for i in range(pieces)]
    own = [View(parts[0], more=parts[1:pieces])]
    return own + [View(others[0][k], more=[o[k] for o in others[1:]]) for k in range(peers - 1)]


def bits(size):
    return size.bit_length() - 1


def swap(array, key):
    kind, stage = key
    if kind == "expert":
        size = lax.axis_size("expert")
        return lax.ppermute(array, "expert", [(i, i ^ (1 << stage)) for i in range(size)])
    dp, expert, tok = (lax.axis_size(axis) for axis in AXES)
    pairs = []
    for d in range(dp):
        for e in range(expert):
            for t in range(tok):
                if kind == "dp":
                    there = (d ^ (1 << ((stage + t) % bits(dp)))) * expert + e
                else:
                    there = d * expert + (e ^ (1 << ((stage + t) % bits(expert))))
                pairs.append(((d * expert + e) * tok + t, there * tok + t))
    return lax.ppermute(array, AXES, pairs)


def place_row(key):
    kind, stage = key
    return 2 + stage if kind == "dp" else 2 + bits(lax.axis_size("dp")) + stage


class View:
    def __init__(self, array, start=0, rows=None, more=()):
        self.arrays, self.start = [array, *more], start
        self.rows = sum(a.shape[0] for a in self.arrays) if rows is None else rows
        self.array = array

    def read(self, refs, base, stride, bit, rows):
        if len(self.arrays) == 1:
            return refs[0][pl.ds(self.start + base + bit * stride, rows), :].astype(F32)
        size = self.arrays[0].shape[0]
        if stride == 0:
            at = min(base // size, len(self.arrays) - 1)
            return refs[at][base - at * size : base - at * size + rows, :].astype(F32)
        near, far = base // size, (base + stride) // size
        if near == far:
            return refs[near][pl.ds(base - near * size + bit * stride, rows), :].astype(F32)
        if rows > size:
            parts = [
                self.read(refs, base + i * size, stride, bit, size) for i in range(rows // size)
            ]
            return jnp.concatenate(parts, axis=0)
        one = refs[near][base - near * size : base - near * size + rows, :]
        two = refs[far][base + stride - far * size : base + stride - far * size + rows, :]
        return jnp.where(bit == 0, one.astype(F32), two.astype(F32))


class Job:
    def __init__(self, kind, views, key, row=0, count=0, each=0, shared=False):
        self.kind, self.views, self.key, self.row = kind, views, key, row
        self.shared = shared
        self.count, self.each = count, each
        rows = views[0].rows
        self.kept = rows // 2
        if kind == "add":
            self.sent = rows
        elif kind == "join":
            self.sent = 2 * rows
        elif kind == "weave":
            self.sent = 2 * rows
        elif kind in ("split", "halve"):
            self.sent = rows // 2
        else:
            self.sent = self.kept = count // 2 * each + rows - count * each
        self.keeps = kind in ("split", "pick", "halve")


def glue(line, place, jobs):
    arrays = []
    for job in jobs:
        for view in job.views:
            for array in view.arrays:
                if not any(array is a for a in arrays):
                    arrays.append(array)
    width = arrays[0].shape[1]
    offsets, total = [], 0
    for job in jobs:
        offsets.append(total)
        total += job.sent
    n = len(arrays)

    def kernel(*refs):
        place_ref, send_ref, keep_refs = refs[n], refs[n + 1], list(refs[n + 2 :])

        def ref_of(array):
            return refs[[array is a for a in arrays].index(True)]

        def added(job, base, rows, stride=0, bit=0):
            value = None
            for view in job.views:
                part = view.read([ref_of(a) for a in view.arrays], base, stride, bit, rows)
                value = part if value is None else value + part
            return value.astype(BF)

        for job, offset in zip(jobs, offsets):
            rows, bit = job.views[0].rows, place_ref[job.row]
            if job.kind == "add":
                send_ref[offset : offset + rows, :] = added(job, 0, rows)
            elif job.kind == "join":
                for view, turn in zip(job.views, (bit, 1 - bit)):
                    send_ref[pl.ds(offset + turn * rows, rows), :] = ref_of(view.array)[
                        view.start : view.start + rows, :
                    ]
            elif job.kind == "weave":
                spans = [(q * job.each, job.each) for q in range(job.count)]
                if rows > job.count * job.each:
                    spans.append((job.count * job.each, rows - job.count * job.each))
                for view, turn in zip(job.views, (bit, 1 - bit)):
                    ref = ref_of(view.array)
                    for base, size in spans:
                        send_ref[pl.ds(offset + 2 * base + turn * size, size), :] = ref[
                            view.start + base : view.start + base + size, :
                        ]
            elif job.kind == "halve":
                keep_ref, to = keep_refs.pop(0), 0
                spans = [(q * job.each, job.each) for q in range(job.count)]
                if rows > job.count * job.each:
                    spans.append((job.count * job.each, rows - job.count * job.each))
                for base, size in spans:
                    half = size // 2
                    keep_ref[to : to + half, :] = added(job, base, half, half, bit)
                    send_ref[offset + to : offset + to + half, :] = added(job, base, half, half, 1 - bit)
                    to += half
            elif job.kind == "split":
                half, keep_ref = job.sent, keep_refs.pop(0)
                keep_ref[...] = added(job, 0, half, half, bit)
                send_ref[offset : offset + half, :] = added(job, 0, half, half, 1 - bit)
            else:
                keep_ref, each = keep_refs.pop(0), job.each
                for q in range(job.count // 2):
                    keep_ref[q * each : (q + 1) * each, :] = added(job, 2 * q * each, each, each, bit)
                    send_ref[offset + q * each : offset + (q + 1) * each, :] = added(
                        job, 2 * q * each, each, each, 1 - bit
                    )
                done, base = job.count // 2 * each, job.count * each
                rest = added(job, base, rows - base)
                keep_ref[done:, :] = rest
                send_ref[offset + done : offset + job.sent, :] = rest

    outs = [sds((total, width), BF)] + [sds((job.kept, width), BF) for job in jobs if job.keeps]
    send, *keeps = line.call(kernel, arrays, outs, scalars=(place,), weight=GLUE)
    owns = []
    for job, offset in zip(jobs, offsets):
        owns.append(View(keeps.pop(0)) if job.keeps else View(send, offset, job.sent))
    return send, owns, offsets


class Chains:
    def __init__(self, line, place):
        self.line, self.place = line, place
        self.walks, self.jobs, self.done = {}, {}, {}

    def take(self, name, value):
        try:
            self.jobs[name] = self.walks[name].send(value)
        except StopIteration as end:
            self.done[name] = end.value
            del self.walks[name]

    def begin(self, name, walk):
        self.walks[name] = walk
        self.take(name, None)

    def advance(self, *names):
        names = [name for name in names if name in self.walks]
        while names:
            key = self.jobs[names[0]].key
            group = [name for name in names if self.jobs[name].key == key]
            names = [name for name in names if name not in group]
            jobs = [self.jobs[name] for name in group]
            send, owns, offsets = glue(self.line, self.place, jobs)
            if key[0] == "tok":
                others = exchange([send] * lax.axis_size("tok"), "tok")
            else:
                others = [swap(send, key)]
            more = []
            if any(job.shared for job in jobs):
                more = [exchange([a] * lax.axis_size("tok"), "tok") for a in (send, others[0])]
            for name, job, own, offset in zip(group, jobs, owns, offsets):
                views = [own] + [View(other, offset, job.sent) for other in others]
                if job.shared:
                    views = [views] + [[View(a, offset, job.sent) for a in same] for same in zip(*more)]
                self.take(name, views)

    def finish(self, name):
        while name in self.walks:
            self.advance(name)
        return self.done[name]


def chunk_walk(views, mirror, count, each):
    order = [("dp", (s + mirror) % 2) for s in range(bits(lax.axis_size("dp")))]
    experts = [("expert", s) for s in range(bits(lax.axis_size("expert")))]
    halved = []
    for key in order + experts[:-1]:
        if each < 32:
            break
        views = yield Job("halve", views, key, place_row(key), count, each)
        each //= 2
        halved.append(key)
    for key in (order + experts)[len(halved) :]:
        views = yield Job("add", views, key)
    views = yield Job("add", views, halved[-1])
    for before, key in zip(halved[:0:-1], halved[-2::-1]):
        views = yield Job(
            "weave", views, key, place_row(before), count, each, shared=key == order[0]
        )
        each *= 2
    return views, order[0], count, each


def tail_walk(views, experts, each, mirror):
    stages = bits(lax.axis_size("dp"))
    order = [("dp", (s + mirror) % 2) for s in range(stages)]
    halves = each >> stages >= 16
    for key in order if halves else ():
        views = yield Job("halve", views, key, place_row(key), experts, each)
        each //= 2
    for stage in range(bits(experts)):
        key = ("expert", stage)
        views = yield Job("pick", views, key, place_row(key), experts >> stage, each)
    before = None
    for key in reversed(order):
        if before is None or not halves:
            views = yield Job("add", views, key)
        else:
            views = yield Job("weave", views, key, place_row(before), 1, each)
            each *= 2
        before = key
    if halves:
        views = yield Job("weave", views, ("tok", 0), place_row(before), 1, each)
    else:
        views = yield Job("add", views, ("tok", 0))
    return views


def place_parts(line, place, items, walk, first, width, full, before):
    _, (_, phase), count, each = walk
    peers, stages = lax.axis_size("tok"), bits(lax.axis_size("dp"))
    share = 2 * width // peers
    arrays = []
    for view, _, _ in items:
        if not any(view.array is a for a in arrays):
            arrays.append(view.array)
    n = len(arrays)

    def kernel(*refs):
        place_ref, _, wide_ref, send, gin_ref, gout_ref = refs[n:]
        top = 0
        for view, turn, far in items:
            part_ref = refs[[view.array is a for a in arrays].index(True)]
            part, bit = place_ref[0] ^ turn, place_ref[place_row(("dp", (phase + turn) % stages))]
            if far:
                bit = 1 - bit
            for i in range(count):
                span = slice(top, top + each)
                top = top + each
                wide_ref[span, :] = part_ref[
                    view.start + i * each : view.start + (i + 1) * each, :
                ].astype(F32)
                base = 2 * i * each
                column, at = first + base // share * width, part * share + base % share + bit * each
                to = pl.multiple_of(column + jnp.minimum(at, width - each), each)
                across = pl.multiple_of(jnp.maximum(at - width, 0), each)
                send(
                    wide_ref.at[span, :],
                    gout_ref.at[pl.ds(to, each), :],
                    gin_ref.at[pl.ds(across, each), column : column + width],
                    at < width,
                )

    _, *grads = line.call(
        kernel,
        arrays,
        (),
        scalars=(place,),
        scratch=(sds((len(items) * count * each, width), F32),),
        sent=(sds((width, full), F32), sds((full, width), F32)),
        aliased=before,
        copies=len(items) * count,
    )
    return tuple(grads)


def place_tail(line, place, views, experts, head, misc):
    peers = len(views)
    parts = [view.array for view in views]
    pair, width = 2 * head, parts[0].shape[1]
    each, share = pair // peers, misc // peers

    def last(*refs):
        part_refs, place_ref = refs[:peers], refs[peers]
        query_ref, output_ref, kv_ref, router_ref, one_ref, two_ref, pair_ref, misc_ref = refs[
            peers + 1 :
        ]
        for k, view in enumerate(views):
            part, start = place_ref[0] ^ k, view.start
            pair_ref[pl.ds(part * each, each), :] = part_refs[k][start : start + each, :].astype(F32)
            misc_ref[pl.ds(part * share, share), :] = part_refs[k][
                start + each : start + view.rows, :
            ].astype(F32)
        query_ref[0] = pair_ref[:head, :]
        output_ref[0] = pair_ref[head:, :]
        kv_ref[...] = misc_ref[:pair, :].T
        router_ref[...] = misc_ref[pair : pair + experts, :]
        one_ref[...] = misc_ref[pair + experts : pair + experts + 1, :]
        two_ref[...] = misc_ref[pair + experts + 1 : pair + experts + 2, :]

    return line.call(
        last,
        parts,
        [
            sds((1, head, width), F32),
            sds((1, head, width), F32),
            sds((width, pair), F32),
            sds((experts, width), F32),
            sds((1, width), F32),
            sds((1, width), F32),
        ],
        scalars=(place,),
        scratch=(sds((pair, width), F32), sds((misc, width), F32)),
    )


def join_all(line, arrays):
    rows, width = arrays[0].shape
    count = len(arrays)

    def kernel(*refs):
        for k in range(count):
            refs[count][k * rows : (k + 1) * rows, :] = refs[k][...]

    return line.call(kernel, arrays, [sds((count * rows, width), BF)])[0]


def body(
    tokens, out_grad, expert_ids, sentence_ids, ln_attn, w_kv, w_router, w_query, w_output, ln_ffn, w_in, w_out
):
    length, width = tokens.shape
    head = w_query.shape[2]
    pair = w_kv.shape[1]
    full = w_in.shape[1]
    experts = lax.axis_size("expert")
    peers = lax.axis_size("tok")
    choose = expert_ids.shape[1]
    tok, dp, expert = lax.axis_index("tok"), lax.axis_index("dp"), lax.axis_index("expert")
    stages = bits(lax.axis_size("dp"))
    dp_bits = [(dp >> ((s + tok) % stages)) & 1 for s in range(stages)]
    spots = jnp.stack(
        [tok, expert] + dp_bits + [(expert >> s) & 1 for s in range(bits(experts))]
    ).astype(jnp.int32)
    weights = jnp.concatenate([w_query[0].T, w_output[0]], axis=0)
    each = weights.shape[0] // peers
    weights = lax.dynamic_slice_in_dim(weights, tok * each, each, axis=0)
    pieces = exchange([weights] * experts, "expert")
    ids = expert_ids.T
    ln_one = ln_attn.reshape(1, width)
    ln_two = ln_ffn.reshape(1, width)
    line = Line()
    line.last = spots
    (
        normed, kv, kvt, gates, gt, small, sent, gains, keyid, place, ids, own_query, own_output, x, g, out_weight,
    ) = line.call(
        prepare_kernel,
        (),
        [
            sds((length, width), BF),
            sds((length, pair), BF),
            sds((pair, length), BF),
            sds((choose, length), F32),
            sds((width, length), BF),
            sds((pair + 16, width), BF),
            sds((1, length), F32),
            sds((2, width), F32),
            sds((length, BAND), F32),
            sds((8, 128), jnp.int32),
        ],
        fetched=(ln_one, w_kv, w_router.T, sentence_ids, ln_two),
        numbers=(spots,),
        kept=(ids, w_query[0].T, w_output[0], tokens, out_grad, w_out),
        room=8 << 20,
    )
    ag, in_weight = line.call(
        upstream_kernel, (g, out_weight), [sds((length, full), BF)], kept=(w_in,), room=8 << 20,
    )
    slab = join_all(line, pieces)
    slabs = [slab] + exchange([slab] * peers, "tok")
    wq, wo, qt, at, lse, gat, h, hn, hnt = line.call(
        functools.partial(attend_kernel, experts=experts, head=head, peers=peers),
        (*slabs, normed, kv, kvt, gates, x, ids, sent, gains, keyid, own_query, own_output),
        [
            sds((experts * head, width), BF),
            sds((experts * head, width), BF),
            sds((head, choose * length), BF),
            sds((head, choose * length), BF),
            sds((1, choose * length), F32),
            sds((experts * head, length), BF),
            sds((length, width), F32),
            sds((length, width), BF),
            sds((width, length), BF),
        ],
        scalars=(place,),
        scratch=(
            sds((experts * head, length), F32),
            sds((2 * head, width), BF),
            sds((length // BAND, 3 * BAND, choose * BAND), F32),
            sds((length // BAND, 3 * BAND, choose * BAND), BF),
        ),
        room=8 << 20,
    )

    chains = Chains(line, place)
    us, dpres, sums, spans = [], [], [], {}

    def ffn(last=None, mirror=0):
        rows = 2 * width // peers
        pieces = max(1, rows // PIECE)
        rows = rows // pieces
        u, dpre, *parts = line.call(
            functools.partial(ffn_kernel, first=len(us) * width, peers=peers),
            (hn, hnt, gt, ag, in_weight),
            [sds((length, width), BF)] * 2 + [sds((rows, width), BF)] * (peers * pieces),
            scalars=(place,),
            scratch=() if peers == 2 else (sds((2 * width, width), BF),),
            room=6 << 20,
        )
        us.append(u)
        dpres.append(dpre)
        for i in range(pieces):
            sums.append([parts[i]] + exchange(parts[i::pieces], "tok"))
        if last is not None:
            views = [View(same[0], more=same[1:]) for same in zip(*sums)]
            chains.begin(last, chunk_walk(views, mirror, len(sums), rows))
            hidden = len(sums) // pieces * width
            spans[last] = (len(us) * width - hidden, hidden)
            sums.clear()

    misc = -(-(pair + 16) // (64 * peers)) * 64 * peers

    def hidden():
        made["dh"], made["low"], made["gain"] = line.call(
            hidden_kernel,
            (h, g, in_weight, gains, *dpres),
            [sds((length, width), F32), sds((length, width), BF), sds((1, width), F32)],
            room=6 << 20,
        )

    def heads_back():
        made["z"], made["gout"] = line.call(
            functools.partial(heads_back_kernel, experts=experts, head=head),
            (kv, kvt, gates, wo, qt, at, lse, gat, made["low"], ids, sent, keyid),
            [sds((experts * head + pair + 16, length), BF), sds((experts * head, width), BF)],
            scratch=(
                sds((experts * head, length), F32),
                sds((pair, length), F32),
                sds((head, choose * length), BF),
                *[sds((length // BAND, 3 * BAND, choose * BAND), t) for t in (F32, F32, BF, BF)],
            ),
            room=6 << 20,
        )

    def rows_back():
        *parts, made["dx"] = line.call(
            functools.partial(rows_back_kernel, experts=experts, head=head, peers=peers, misc=misc),
            (made["z"], made["gout"], normed, wq, small, made["dh"], made["gain"], x, gains),
            ([sds((2 * pair // peers, width), BF)] * (experts // 2) + [sds((misc // peers, width), BF)])
            * peers,
            sent=(sds((length, width), BF),),
            scalars=(place,),
            scratch=(
                sds((experts * head + pair + 16, width), F32),
                sds((experts * pair, width), BF),
                sds((misc, width), F32),
                sds((length, width), BF),
            ),
            room=6 << 20,
        )
        chains.begin("t", tail_walk(tok_views(parts, peers), experts, pair // peers, 1))

    def out():
        _, made["output"] = line.call(
            output_kernel,
            (h, out_weight, *us),
            (),
            sent=(sds((length, width), BF),),
            scratch=(sds((length, width), BF),),
            room=6 << 20,
        )

    def place_some(name, wanted):
        walk = chains.finish(name)
        items = [
            (views[far], turn, far)
            for far in (0, 1)
            for turn, views in enumerate(walk[0])
            if wanted(turn > 0, far == 1)
        ]
        made["both"] = place_parts(
            line, place, items, walk, spans[name][0], width, full, made.get("both", ())
        )

    def last():
        made["t"] = place_tail(line, place, chains.finish("t"), experts, head, misc)

    made = {}
    acts = {"f": ffn, "n": hidden, "h": heads_back, "r": rows_back, "o": out, "T": last}
    for i, name in enumerate("ab"):
        acts[name.upper()] = functools.partial(ffn, name, i)
    acts["1"] = lambda: place_some("a", lambda other, far: True)
    acts["2"] = lambda: place_some("b", lambda other, far: not (other and far))
    acts["3"] = lambda: place_some("b", lambda other, far: other and far)
    for word in ORDER:
        if word in acts:
            acts[word]()
        else:
            chains.advance(*word)
    query, outp, kv_grad, router, one, two = made["t"]
    output, dx, both = made["output"], made["dx"], made["both"]
    return (
        output,
        dx,
        one.reshape(width),
        kv_grad,
        router.T,
        jnp.swapaxes(query, 1, 2),
        outp,
        two.reshape(width),
        both[0],
        both[1],
    )


def solution(mesh):
    rows = P(AXES, None)
    heads = P("expert", None, None)
    return jax.shard_map(
        body,
        mesh=mesh,
        in_specs=(rows, rows, rows, rows, P(), P(), P(), heads, heads, P(), P(), P()),
        out_specs=(rows, rows, P(), P(), P(), heads, heads, P(), P(), P()),
        check_vma=False,
    )
```

```python
import functools

import jax
import jax.numpy as jnp
from jax import lax
from jax.experimental import pallas as pl
from jax.experimental.pallas import tpu as pltpu
from jax.sharding import PartitionSpec as P

BF = jnp.bfloat16
F32 = jnp.float32
MASKED = -1e30
BAND = 128
ROWS = 256
PIECE = 512
AXES = ("dp", "expert", "tok")
GLUE = 23 * 10**9
WORK = 0 * 10**9 + 1
ORDER = (
    "f", "A", "f", "a", "B", "n", "a", "b", "h", "a", "r", "b", "a", "o", "b", "t", "a", "b", "a",
    "t", "b", "a", "t", "b", "t", "b", "1", "t", "2", "t", "3", "T",
)


def nn(left, right):
    return lax.dot_general(left, right, (((1,), (0,)), ((), ())), preferred_element_type=F32)


def nt(left, right):
    return lax.dot_general(left, right, (((1,), (1,)), ((), ())), preferred_element_type=F32)


def tn(left, right):
    return lax.dot_general(left, right, (((0,), (0,)), ((), ())), preferred_element_type=F32)


def normalize(values):
    centre = values - jnp.mean(values, axis=-1, keepdims=True)
    spread = jnp.mean(centre * centre, axis=-1, keepdims=True)
    inverse = lax.rsqrt(spread + 1e-05)
    return centre * inverse, inverse


def normalize_back(upstream, normalized, inverse, gain):
    scaled = upstream * gain
    inner = (
        scaled
        - jnp.mean(scaled, axis=-1, keepdims=True)
        - normalized * jnp.mean(scaled * normalized, axis=-1, keepdims=True)
    )
    return inner * inverse


def sds(shape, dtype):
    return jax.ShapeDtypeStruct(shape, dtype)


def size_of(array):
    lanes = -(-array.shape[-1] // 128) * 128
    rows = -(-array.shape[-2] // 16) * 16
    lead = 1
    for extent in array.shape[:-2]:
        lead = lead * extent
    return lead * rows * lanes * jnp.dtype(array.dtype).itemsize


class Place:
    def __init__(self, ref):
        self.ref = ref

    def __getitem__(self, row):
        return self.ref[row, 0]


class Line:
    def __init__(self):
        self.last = None

    def call(
        self, kernel, operands, outs, fetched=(), scalars=(), scratch=(), room=2 << 20, weight=WORK,
        sent=(), aliased=(), kept=(), numbers=(), delayed=0, copies=8,
    ):
        n, f, s = len(operands), len(fetched) + len(kept), len(scalars)
        late = () if self.last is None else (self.last,)
        skip = len(late) + len(aliased)
        outs = list(outs)
        h = len(sent)
        if not outs:
            outs = [sds((8, 128), F32)]
        outs = outs + [sds(a.shape, a.dtype) for a in kept]
        scratch_copies, fetched = len(fetched), (*fetched, *kept)

        def wrapped(*refs):
            ins = refs[:n]
            sources = refs[n : n + f]
            smem = [Place(ref) for ref in refs[n + f : n + f + s]]
            rest = list(refs[n + f + s + len(numbers) + skip :])
            if numbers:
                number_sem, number_ref = rest.pop(), rest.pop()
                number = pltpu.make_async_copy(refs[n + f + s], number_ref, number_sem.at[0])
                number.start()

                def number_wait():
                    number.wait()
                    return number_ref

                smem = smem + [number_wait]
            far = rest[len(outs) : len(outs) + h]
            del rest[len(outs) : len(outs) + h]
            open_copies, send_sem = [], rest.pop() if h else None
            sems = rest.pop() if f else None
            buffers = rest[len(rest) - scratch_copies :] if scratch_copies else []
            del rest[len(rest) - scratch_copies :]
            first = len(outs) - len(kept)
            buffers = buffers + rest[first : len(outs)]
            del rest[first : len(outs)]
            body, waits, waiting = rest, [], {}
            for i in range(f):
                copy = pltpu.make_async_copy(sources[i], buffers[i], sems.at[i])
                if i < f - delayed:
                    copy.start()
                waiting[i] = copy

                def wait(i=i):
                    if i in waiting:
                        waiting.pop(i).wait()
                        if i == f - delayed - 1:
                            for j in range(f - delayed, f):
                                waiting[j].start()
                    return buffers[i]

                waits.append(wait)
            def send(source, target, other=None, near=None):
                sem = send_sem.at[len(open_copies)]
                copy = pltpu.make_async_copy(source, target, sem)
                open_copies.append(copy)
                if other is None:
                    copy.start()
                    return
                pl.when(near)(copy.start)
                pl.when(jnp.logical_not(near))(pltpu.make_async_copy(source, other, sem).start)

            if h:
                kernel(*ins, *waits, *smem, *body, send, *far)
                for copy in open_copies:
                    copy.wait()
            else:
                kernel(*ins, *waits, *smem, *body)
            for copy in waiting.values():
                copy.wait()

        need = sum(size_of(a) for a in (*fetched[:scratch_copies], *scratch))
        extra = [pltpu.VMEM(a.shape, a.dtype) for a in fetched[:scratch_copies]]
        if f:
            extra.append(pltpu.SemaphoreType.DMA((f,)))
        if h:
            extra.append(pltpu.SemaphoreType.DMA((copies,)))
        if numbers:
            extra += [pltpu.SMEM(numbers[0].shape, jnp.int32), pltpu.SemaphoreType.DMA((1,))]
        results = pl.pallas_call(
            wrapped,
            out_shape=outs + list(sent),
            in_specs=[pl.BlockSpec(memory_space=pltpu.VMEM)] * n
            + [pl.BlockSpec(memory_space=pltpu.HBM)] * f
            + [pl.BlockSpec(memory_space=pltpu.VMEM)] * s
            + [pl.BlockSpec(memory_space=pl.ANY)] * len(numbers)
            + [pl.BlockSpec(memory_space=pl.ANY)] * skip,
            out_specs=[pl.BlockSpec(memory_space=pltpu.VMEM)] * len(outs)
            + [pl.BlockSpec(memory_space=pltpu.HBM)] * h,
            input_output_aliases={
                n + f + s + len(numbers) + len(late) + i: len(outs) + i for i in range(len(aliased))
            },
            scratch_shapes=[pltpu.VMEM(a.shape, a.dtype) for a in scratch] + extra,
            compiler_params=pltpu.CompilerParams(vmem_limit_bytes=need + room),
            cost_estimate=pl.CostEstimate(flops=weight, bytes_accessed=1024, transcendentals=0),
        )(
            *operands,
            *[pltpu.with_memory_space_constraint(a, pltpu.HBM) for a in fetched],
            *scalars,
            *numbers,
            *late,
            *aliased,
        )
        self.last = min(results[: len(outs)], key=lambda a: a.size)
        return results


def prepare_kernel(
    ln_wait, wkv_wait, wr_wait, sent_wait, ln_two_wait, ids_wait, wq_wait, wo_wait, x_wait, g_wait, wout_wait,
    spots_wait, xn_ref, kv_ref, kvt_ref, gates_ref, gt_ref, small_ref, sent_keep, gains_keep, keyid_ref,
    place_ref,
):
    ln_ref, ln_two_ref, sent_ref = ln_wait(), ln_two_wait(), sent_wait()
    gain = ln_ref[...]
    gains_keep[0:1, :] = gain
    gains_keep[1:2, :] = ln_two_ref[...]
    sent_keep[...] = sent_ref[...].astype(F32)
    column_ids(sent_keep, keyid_ref)
    wkv_ref, wr_ref, ids_ref = wkv_wait(), wr_wait(), ids_wait()
    pair = wkv_ref.shape[1]
    experts = wr_ref.shape[0]
    small_ref[:pair, :] = wkv_ref[...].T
    small_ref[pair:, :] = jnp.concatenate(
        [wr_ref[...].astype(F32), jnp.zeros((16 - experts, wr_ref.shape[1]), F32)], axis=0
    ).astype(BF)
    spots_ref = spots_wait()
    for i in range(spots_ref.shape[0]):
        place_ref[i : i + 1, :] = jnp.full((1, place_ref.shape[1]), spots_ref[i], jnp.int32)
    x_ref = x_wait()
    length = x_ref.shape[0]
    for start in range(0, length, ROWS):
        rows = pl.ds(start, ROWS)
        normalized, _ = normalize(x_ref[rows, :].astype(F32))
        xn_ref[rows, :] = (normalized * gain).astype(BF)
    normed = xn_ref[...]
    small = small_ref[...]
    both = nt(small, normed)
    kvt_ref[...] = both[:pair].astype(BF)
    kv_ref[...] = nn(normed, wkv_ref[...]).astype(BF)
    choose = ids_ref.shape[0]
    picked = []
    for route in range(choose):
        ids = ids_ref[route : route + 1, :]
        value = jnp.zeros((1, length), F32)
        for expert in range(experts):
            value = jnp.where(ids == expert, both[pair + expert : pair + expert + 1], value)
        picked.append(value)
    top = functools.reduce(jnp.maximum, picked)
    raised = [jnp.exp(value - top) for value in picked]
    total = functools.reduce(lambda a, b: a + b, raised)
    for route in range(choose):
        gates_ref[route : route + 1, :] = raised[route] / total
    g_ref = g_wait()
    gt_ref[...] = g_ref[...].T


def upstream_kernel(g_ref, wout_ref, win_wait, ag_ref):
    for start in range(0, g_ref.shape[0], ROWS):
        rows = slice(start, start + ROWS)
        ag_ref[rows, :] = nt(g_ref[rows, :], wout_ref[...]).astype(BF)


def column_ids(sent_ref, keyid_ref):
    length = sent_ref.shape[1]
    for start in range(0, length, BAND):
        row = jnp.broadcast_to(sent_ref[:, start : start + BAND], (BAND, BAND))
        keyid_ref[pl.ds(start, BAND), :] = row.T


def masked_scores(kv_ref, keyid_ref, sent_ref, queries, start, low, high, choose):
    padded = jnp.concatenate([queries * 0.125, jnp.zeros_like(queries)], axis=0)
    scores = nn(kv_ref[low:high, :], padded)
    same = keyid_ref[low:high, :] == sent_ref[:, start : start + BAND]
    parts = [
        jnp.where(same, scores[:, route * BAND : (route + 1) * BAND], MASKED)
        for route in range(choose)
    ]
    return jnp.concatenate(parts, axis=1)


def window(start, length):
    return max(start - BAND, 0), min(start + 2 * BAND, length)


def attend_kernel(*refs, experts, head, peers):
    slab_refs, refs = refs[:peers], refs[peers:]
    (
        xn_ref, kv_ref, kvt_ref, gates_ref, x_ref, ids_ref, sent_ref, ln_ref, keyid_ref, wq_own, wo_own,
        place_ref, wq_ref, wo_ref, qt_ref, at_ref, lse_ref, gat_ref, h_ref, hn_ref, hnt_ref, all_ref,
        pair_ref, score_ref, prob_ref,
    ) = refs
    own = place_ref[1]
    each = 2 * head // peers
    wq_ref[pl.ds(own * head, head), :] = wq_own[...]
    wo_ref[pl.ds(own * head, head), :] = wo_own[...]
    for k in range(1, experts):
        for j in range(peers):
            rows = pl.ds((place_ref[0] ^ j) * each, each)
            pair_ref[rows, :] = slab_refs[j][(k - 1) * each : k * each, :]
        rows = pl.ds((own ^ k) * head, head)
        wq_ref[rows, :] = pair_ref[:head, :]
        wo_ref[rows, :] = pair_ref[head:, :]
    length = xn_ref.shape[0]
    choose = ids_ref.shape[0]
    all_ref[...] = nt(wq_ref[...], xn_ref[...])
    starts = range(0, length, BAND)
    spans = [slice(start * choose, (start + BAND) * choose) for start in starts]
    bounds = [window(start, length) for start in starts]
    for start, block in zip(starts, spans):
        lanes = slice(start, start + BAND)
        chosen = []
        for route in range(choose):
            ids = ids_ref[route : route + 1, lanes]
            value = all_ref[:head, lanes]
            for expert in range(1, experts):
                value = jnp.where(
                    ids == expert, all_ref[expert * head : (expert + 1) * head, lanes], value
                )
            chosen.append(value)
        qt_ref[:, block] = jnp.concatenate(chosen, axis=1).astype(BF)
    for i, start in enumerate(starts):
        low, high = bounds[i]
        score_ref[i, : high - low, :] = masked_scores(
            kv_ref, keyid_ref, sent_ref, qt_ref[:, spans[i]], start, low, high, choose
        )
    for i, block in enumerate(spans):
        size = bounds[i][1] - bounds[i][0]
        scores = score_ref[i, :size, :]
        largest = jnp.max(scores, axis=0, keepdims=True)
        raised = jnp.exp(scores - largest)
        total = jnp.sum(raised, axis=0, keepdims=True)
        prob_ref[i, :size, :] = (raised * (1.0 / total)).astype(BF)
        lse_ref[:, block] = largest + jnp.log(total)
    for i, block in enumerate(spans):
        low, high = bounds[i]
        at_ref[:, block] = nn(kvt_ref[head:, low:high], prob_ref[i, : high - low, :]).astype(BF)
    for start in starts:
        lanes = slice(start, start + BAND)
        spread = [jnp.zeros((head, BAND), F32) for _ in range(experts)]
        for route in range(choose):
            ids = ids_ref[route : route + 1, lanes]
            first = start * choose + route * BAND
            gated = at_ref[:, first : first + BAND].astype(F32) * gates_ref[route : route + 1, lanes]
            for expert in range(experts):
                spread[expert] = jnp.where(ids == expert, gated, spread[expert])
        for expert in range(experts):
            gat_ref[expert * head : (expert + 1) * head, lanes] = spread[expert].astype(BF)
    gain = ln_ref[1:2, :]
    for start in range(0, length, ROWS):
        rows = slice(start, start + ROWS)
        mixed = tn(gat_ref[:, rows], wo_ref[...])
        hidden = x_ref[rows, :].astype(F32) + mixed
        h_ref[rows, :] = hidden
        normalized, _ = normalize(hidden)
        low_value = (normalized * gain).astype(BF)
        hn_ref[rows, :] = low_value
        hnt_ref[:, rows] = low_value.T


def gelu_both(values):
    bell = jnp.exp2(values * values * -0.7213475204444817)
    t = 1.0 / (1.0 + 0.23164188 * jnp.abs(values))
    poly = t * (
        0.127414796
        + t * (-0.142248368 + t * (0.7107068705 + t * (-0.7265760135 + t * 0.5307027145)))
    )
    tail = poly * bell
    cumulative = jnp.where(values >= 0.0, 1.0 - tail, tail)
    return values * cumulative, cumulative + values * (bell * 0.3989422804014327)


def ffn_block(refs, first):
    hn_ref, hnt_ref, gt_ref, ag_ref, win_ref, u_ref, dpre_ref = refs
    length, width = hn_ref.shape
    far = slice(first, first + width)
    out_grad = in_grad = None
    for start in range(0, length, 2 * ROWS):
        rows = slice(start, start + 2 * ROWS)
        activated, slope = gelu_both(nn(hn_ref[rows, :], win_ref[:, far]))
        activated = activated.astype(BF)
        before = (ag_ref[rows, far].astype(F32) * slope).astype(BF)
        u_ref[rows, :], dpre_ref[rows, :] = activated, before
        out_part, in_part = nn(gt_ref[:, rows], activated), nn(hnt_ref[:, rows], before)
        out_grad = out_part if out_grad is None else out_grad + out_part
        in_grad = in_part if in_grad is None else in_grad + in_part
    return out_grad.astype(BF).T, in_grad.astype(BF)


def ffn_kernel(*refs, first, peers):
    place_ref, part_refs = refs[5], list(refs[8:])
    width = refs[0].shape[1]
    tok = place_ref[0]
    out_grad, in_grad = ffn_block((*refs[:5], *refs[6:8]), first)
    if peers == 2:
        pieces = len(part_refs) // 2
        size = part_refs[0].shape[0]
        for i in range(pieces):
            span = slice(i * size, (i + 1) * size)
            one, two = out_grad[span, :], in_grad[span, :]
            part_refs[i][...] = jnp.where(tok == 0, one, two)
            part_refs[pieces + i][...] = jnp.where(tok == 0, two, one)
        return
    sum_ref = part_refs.pop()
    sum_ref[:width, :], sum_ref[width:, :] = out_grad, in_grad
    size = part_refs[0].shape[0]
    pieces = len(part_refs) // peers
    for k in range(peers):
        for i in range(pieces):
            start = (tok ^ k) * size * pieces + i * size
            part_refs[k * pieces + i][...] = sum_ref[pl.ds(start, size), :]


def output_kernel(*refs):
    h_ref, wout_ref = refs[:2]
    out_ref, send, far_ref = refs[-3:]
    u_refs = refs[2:-4]
    for start in range(0, h_ref.shape[0], ROWS):
        rows = slice(start, start + ROWS)
        total, first = h_ref[rows, :], 0
        for ref in u_refs:
            size = ref.shape[1]
            total = total + nn(ref[rows, :], wout_ref[first : first + size, :])
            first = first + size
        out_ref[rows, :] = total.astype(BF)
        send(out_ref.at[rows, :], far_ref.at[rows, :])


def hidden_kernel(*refs):
    h_ref, g_ref, win_ref, ln_ref = refs[:4]
    dh_ref, low_ref, gain_ref = refs[-3:]
    dpre_refs = refs[4:-3]
    gain = ln_ref[1:2, :]
    gain_sum = jnp.zeros_like(gain)
    for start in range(0, h_ref.shape[0], ROWS):
        rows = slice(start, start + ROWS)
        upstream, first = None, 0
        for ref in dpre_refs:
            size = ref.shape[1]
            part = nt(ref[rows, :], win_ref[:, first : first + size])
            upstream = part if upstream is None else upstream + part
            first = first + size
        normalized, inverse = normalize(h_ref[rows, :])
        value = g_ref[rows, :].astype(F32) + normalize_back(upstream, normalized, inverse, gain)
        dh_ref[rows, :] = value
        low_ref[rows, :] = value.astype(BF)
        gain_sum = gain_sum + jnp.sum(upstream * normalized, axis=0, keepdims=True)
    gain_ref[...] = gain_sum


def heads_back_kernel(
    kv_ref, kvt_ref, gates_ref, wo_ref, qt_ref, at_ref, lse_ref, gat_ref, low_ref, ids_ref, sent_ref,
    keyid_ref, z_ref, gout_ref, all_ref, dkv_ref, up_ref, prob_ref, grad_ref, soft_ref, ds_ref, *, experts,
    head,
):
    length = kv_ref.shape[0]
    wide, pair = experts * head, 2 * head
    choose = ids_ref.shape[0]
    all_ref[...] = nt(wo_ref[...], low_ref[...])
    gout_ref[...] = nn(gat_ref[...], low_ref[...]).astype(BF)
    dkv_ref[...] = jnp.zeros_like(dkv_ref)
    starts = range(0, length, BAND)
    spans = [slice(start * choose, (start + BAND) * choose) for start in starts]
    bounds = [window(start, length) for start in starts]
    for start, block in zip(starts, spans):
        lanes = slice(start, start + BAND)
        raw, gate_grads = [], []
        for route in range(choose):
            ids = ids_ref[route : route + 1, lanes]
            value = all_ref[:head, lanes]
            for expert in range(1, experts):
                value = jnp.where(
                    ids == expert, all_ref[expert * head : (expert + 1) * head, lanes], value
                )
            raw.append(value)
            first = start * choose + route * BAND
            attended = at_ref[:, first : first + BAND].astype(F32)
            gate_grads.append(jnp.sum(value * attended, axis=0, keepdims=True))
        gates = [gates_ref[route : route + 1, lanes] for route in range(choose)]
        common = functools.reduce(
            lambda a, b: a + b, [gate * grad for gate, grad in zip(gates, gate_grads)]
        )
        logit_rows = [jnp.zeros((1, BAND), F32) for _ in range(experts)]
        for route in range(choose):
            ids = ids_ref[route : route + 1, lanes]
            picked = gates[route] * (gate_grads[route] - common)
            for expert in range(experts):
                logit_rows[expert] = jnp.where(ids == expert, picked, logit_rows[expert])
        logit_pad = jnp.concatenate(
            logit_rows + [jnp.zeros((16 - experts, BAND), F32)], axis=0
        )
        z_ref[wide + pair :, lanes] = logit_pad.astype(BF)
        up_ref[:, block] = jnp.concatenate(
            [gate * value for gate, value in zip(gates, raw)], axis=1
        ).astype(BF)
    for i, start in enumerate(starts):
        low, high = bounds[i]
        prob_ref[i, : high - low, :] = masked_scores(
            kv_ref, keyid_ref, sent_ref, qt_ref[:, spans[i]], start, low, high, choose
        )
        upstream = up_ref[:, spans[i]]
        padded = jnp.concatenate([jnp.zeros_like(upstream), upstream], axis=0)
        grad_ref[i, : high - low, :] = nn(kv_ref[low:high, :], padded)
    for i, block in enumerate(spans):
        size = bounds[i][1] - bounds[i][0]
        probs = jnp.exp(prob_ref[i, :size, :] - lse_ref[:, block])
        soft_ref[i, :size, :] = probs.astype(BF)
        prob_grad = grad_ref[i, :size, :]
        mean = jnp.sum(probs * prob_grad, axis=0, keepdims=True)
        ds_ref[i, :size, :] = (probs * (prob_grad - mean)).astype(BF)
    for i, start in enumerate(starts):
        low, high = bounds[i]
        lanes = slice(start, start + BAND)
        score_grad = ds_ref[i, : high - low, :]
        query_grad = (nn(kvt_ref[:head, low:high], score_grad) * 0.125).astype(BF)
        spread = [jnp.zeros((head, BAND), BF) for _ in range(experts)]
        for route in range(choose):
            ids = ids_ref[route : route + 1, lanes]
            piece = query_grad[:, route * BAND : (route + 1) * BAND]
            for expert in range(experts):
                spread[expert] = jnp.where(ids == expert, piece, spread[expert])
        for expert in range(experts):
            z_ref[expert * head : (expert + 1) * head, lanes] = spread[expert]
        dkv_ref[:head, low:high] += nt(qt_ref[:, spans[i]], score_grad) * 0.125
        dkv_ref[head:, low:high] += nt(up_ref[:, spans[i]], soft_ref[i, : high - low, :])
    z_ref[wide : wide + pair, :] = dkv_ref[...].astype(BF)


def rows_back_kernel(*refs, experts, head, peers, misc):
    (
        z_ref, gout_ref, xn_ref, wq_ref, small_ref, dh_ref, gain_two_ref, x_ref, ln_ref, place_ref,
    ) = refs[:10]
    pieces = experts // 2 + 1
    part_refs = refs[10 : 10 + peers * pieces]
    grads_ref, pair_ref, misc_ref, dx_ref, send, far_ref = refs[10 + peers * pieces :]
    length = xn_ref.shape[0]
    wide, pair = experts * head, 2 * head
    grads_ref[...] = nn(z_ref[...], xn_ref[...])
    for expert in range(experts):
        rows = slice(expert * head, (expert + 1) * head)
        pair_ref[expert * pair : expert * pair + head, :] = grads_ref[rows, :].astype(BF)
        pair_ref[expert * pair + head : (expert + 1) * pair, :] = gout_ref[rows, :]
    gain = ln_ref[0:1, :]
    total = jnp.zeros_like(gain)
    for start in range(0, length, ROWS):
        rows = slice(start, start + ROWS)
        normed_grad = tn(z_ref[:wide, rows], wq_ref[...]) + tn(z_ref[wide:, rows], small_ref[...])
        normalized, inverse = normalize(x_ref[rows, :].astype(F32))
        total = total + jnp.sum(normed_grad * normalized, axis=0, keepdims=True)
        back = normalize_back(normed_grad, normalized, inverse, gain)
        dx_ref[rows, :] = (dh_ref[rows, :] + back).astype(BF)
        send(dx_ref.at[rows, :], far_ref.at[rows, :])
    misc_ref[...] = jnp.zeros_like(misc_ref)
    misc_ref[:pair, :] = grads_ref[wide : wide + pair, :]
    misc_ref[pair : pair + 16, :] = jnp.concatenate(
        [
            grads_ref[wide + pair : wide + pair + experts, :],
            total,
            gain_two_ref[...],
            jnp.zeros((14 - experts, total.shape[1]), F32),
        ],
        axis=0,
    )
    each, share = pair // peers, misc // peers
    for k in range(peers):
        part = place_ref[0] ^ k
        for expert in range(experts):
            rows = pl.ds(expert * pair + part * each, each)
            low = expert % 2 * each
            part_refs[k * pieces + expert // 2][low : low + each, :] = pair_ref[rows, :]
        part_refs[(k + 1) * pieces - 1][...] = misc_ref[pl.ds(part * share, share), :].astype(BF)


def exchange(parts, axis):
    size = len(parts)
    return [
        lax.ppermute(parts[k], axis, [(i, i ^ k) for i in range(size)]) for k in range(1, size)
    ]


def tok_views(parts, peers):
    pieces = len(parts) // peers
    others = [exchange(parts[i::pieces], "tok") for i in range(pieces)]
    own = [View(parts[0], more=parts[1:pieces])]
    return own + [View(others[0][k], more=[o[k] for o in others[1:]]) for k in range(peers - 1)]


def bits(size):
    return size.bit_length() - 1


def swap(array, key):
    kind, stage = key
    if kind == "expert":
        size = lax.axis_size("expert")
        return lax.ppermute(array, "expert", [(i, i ^ (1 << stage)) for i in range(size)])
    dp, expert, tok = (lax.axis_size(axis) for axis in AXES)
    pairs = []
    for d in range(dp):
        for e in range(expert):
            for t in range(tok):
                if kind == "dp":
                    there = (d ^ (1 << ((stage + t) % bits(dp)))) * expert + e
                else:
                    there = d * expert + (e ^ (1 << ((stage + t) % bits(expert))))
                pairs.append(((d * expert + e) * tok + t, there * tok + t))
    return lax.ppermute(array, AXES, pairs)


def place_row(key):
    kind, stage = key
    return 2 + stage if kind == "dp" else 2 + bits(lax.axis_size("dp")) + stage


class View:
    def __init__(self, array, start=0, rows=None, more=()):
        self.arrays, self.start = [array, *more], start
        self.rows = sum(a.shape[0] for a in self.arrays) if rows is None else rows
        self.array = array

    def read(self, refs, base, stride, bit, rows):
        if len(self.arrays) == 1:
            return refs[0][pl.ds(self.start + base + bit * stride, rows), :].astype(F32)
        size = self.arrays[0].shape[0]
        if stride == 0:
            at = min(base // size, len(self.arrays) - 1)
            return refs[at][base - at * size : base - at * size + rows, :].astype(F32)
        near, far = base // size, (base + stride) // size
        if near == far:
            return refs[near][pl.ds(base - near * size + bit * stride, rows), :].astype(F32)
        if rows > size:
            parts = [
                self.read(refs, base + i * size, stride, bit, size) for i in range(rows // size)
            ]
            return jnp.concatenate(parts, axis=0)
        one = refs[near][base - near * size : base - near * size + rows, :]
        two = refs[far][base + stride - far * size : base + stride - far * size + rows, :]
        return jnp.where(bit == 0, one.astype(F32), two.astype(F32))


class Job:
    def __init__(self, kind, views, key, row=0, count=0, each=0, shared=False):
        self.kind, self.views, self.key, self.row = kind, views, key, row
        self.shared = shared
        self.count, self.each = count, each
        rows = views[0].rows
        self.kept = rows // 2
        if kind == "add":
            self.sent = rows
        elif kind == "join":
            self.sent = 2 * rows
        elif kind == "weave":
            self.sent = 2 * rows
        elif kind in ("split", "halve"):
            self.sent = rows // 2
        else:
            self.sent = self.kept = count // 2 * each + rows - count * each
        self.keeps = kind in ("split", "pick", "halve")


def glue(line, place, jobs):
    arrays = []
    for job in jobs:
        for view in job.views:
            for array in view.arrays:
                if not any(array is a for a in arrays):
                    arrays.append(array)
    width = arrays[0].shape[1]
    offsets, total = [], 0
    for job in jobs:
        offsets.append(total)
        total += job.sent
    n = len(arrays)

    def kernel(*refs):
        place_ref, send_ref, keep_refs = refs[n], refs[n + 1], list(refs[n + 2 :])

        def ref_of(array):
            return refs[[array is a for a in arrays].index(True)]

        def added(job, base, rows, stride=0, bit=0):
            value = None
            for view in job.views:
                part = view.read([ref_of(a) for a in view.arrays], base, stride, bit, rows)
                value = part if value is None else value + part
            return value.astype(BF)

        for job, offset in zip(jobs, offsets):
            rows, bit = job.views[0].rows, place_ref[job.row]
            if job.kind == "add":
                send_ref[offset : offset + rows, :] = added(job, 0, rows)
            elif job.kind == "join":
                for view, turn in zip(job.views, (bit, 1 - bit)):
                    send_ref[pl.ds(offset + turn * rows, rows), :] = ref_of(view.array)[
                        view.start : view.start + rows, :
                    ]
            elif job.kind == "weave":
                spans = [(q * job.each, job.each) for q in range(job.count)]
                if rows > job.count * job.each:
                    spans.append((job.count * job.each, rows - job.count * job.each))
                for view, turn in zip(job.views, (bit, 1 - bit)):
                    ref = ref_of(view.array)
                    for base, size in spans:
                        send_ref[pl.ds(offset + 2 * base + turn * size, size), :] = ref[
                            view.start + base : view.start + base + size, :
                        ]
            elif job.kind == "halve":
                keep_ref, to = keep_refs.pop(0), 0
                spans = [(q * job.each, job.each) for q in range(job.count)]
                if rows > job.count * job.each:
                    spans.append((job.count * job.each, rows - job.count * job.each))
                for base, size in spans:
                    half = size // 2
                    keep_ref[to : to + half, :] = added(job, base, half, half, bit)
                    send_ref[offset + to : offset + to + half, :] = added(job, base, half, half, 1 - bit)
                    to += half
            elif job.kind == "split":
                half, keep_ref = job.sent, keep_refs.pop(0)
                keep_ref[...] = added(job, 0, half, half, bit)
                send_ref[offset : offset + half, :] = added(job, 0, half, half, 1 - bit)
            else:
                keep_ref, each = keep_refs.pop(0), job.each
                for q in range(job.count // 2):
                    keep_ref[q * each : (q + 1) * each, :] = added(job, 2 * q * each, each, each, bit)
                    send_ref[offset + q * each : offset + (q + 1) * each, :] = added(
                        job, 2 * q * each, each, each, 1 - bit
                    )
                done, base = job.count // 2 * each, job.count * each
                rest = added(job, base, rows - base)
                keep_ref[done:, :] = rest
                send_ref[offset + done : offset + job.sent, :] = rest

    outs = [sds((total, width), BF)] + [sds((job.kept, width), BF) for job in jobs if job.keeps]
    send, *keeps = line.call(kernel, arrays, outs, scalars=(place,), weight=GLUE)
    owns = []
    for job, offset in zip(jobs, offsets):
        owns.append(View(keeps.pop(0)) if job.keeps else View(send, offset, job.sent))
    return send, owns, offsets


class Chains:
    def __init__(self, line, place):
        self.line, self.place = line, place
        self.walks, self.jobs, self.done = {}, {}, {}

    def take(self, name, value):
        try:
            self.jobs[name] = self.walks[name].send(value)
        except StopIteration as end:
            self.done[name] = end.value
            del self.walks[name]

    def begin(self, name, walk):
        self.walks[name] = walk
        self.take(name, None)

    def advance(self, *names):
        names = [name for name in names if name in self.walks]
        while names:
            key = self.jobs[names[0]].key
            group = [name for name in names if self.jobs[name].key == key]
            names = [name for name in names if name not in group]
            jobs = [self.jobs[name] for name in group]
            send, owns, offsets = glue(self.line, self.place, jobs)
            if key[0] == "tok":
                others = exchange([send] * lax.axis_size("tok"), "tok")
            else:
                others = [swap(send, key)]
            more = []
            if any(job.shared for job in jobs):
                more = [exchange([a] * lax.axis_size("tok"), "tok") for a in (send, others[0])]
            for name, job, own, offset in zip(group, jobs, owns, offsets):
                views = [own] + [View(other, offset, job.sent) for other in others]
                if job.shared:
                    views = [views] + [[View(a, offset, job.sent) for a in same] for same in zip(*more)]
                self.take(name, views)

    def finish(self, name):
        while name in self.walks:
            self.advance(name)
        return self.done[name]


def chunk_walk(views, mirror, count, each):
    order = [("dp", (s + mirror) % 2) for s in range(bits(lax.axis_size("dp")))]
    experts = [("expert", s) for s in range(bits(lax.axis_size("expert")))]
    halved = []
    for key in order + experts[:-1]:
        if each < 32:
            break
        views = yield Job("halve", views, key, place_row(key), count, each)
        each //= 2
        halved.append(key)
    for key in (order + experts)[len(halved) :]:
        views = yield Job("add", views, key)
    views = yield Job("add", views, halved[-1])
    for before, key in zip(halved[:0:-1], halved[-2::-1]):
        views = yield Job(
            "weave", views, key, place_row(before), count, each, shared=key == order[0]
        )
        each *= 2
    return views, order[0], count, each


def tail_walk(views, experts, each, mirror):
    stages = bits(lax.axis_size("dp"))
    first, *others = [("dp", (s + mirror) % stages) for s in range(stages)]
    halves = each >= 32
    if halves:
        views = yield Job("halve", views, first, place_row(first), experts, each)
        each //= 2
    for stage in range(bits(experts)):
        key = ("expert", stage)
        views = yield Job("pick", views, key, place_row(key), experts >> stage, each)
    for key in [*others, first]:
        views = yield Job("add", views, key)
    if halves:
        views = yield Job("weave", views, ("tok", 0), place_row(first), 1, each)
    else:
        views = yield Job("add", views, ("tok", 0))
    return views


def place_parts(line, place, items, walk, first, width, full, before):
    _, (_, phase), count, each = walk
    peers, stages = lax.axis_size("tok"), bits(lax.axis_size("dp"))
    share = 2 * width // peers
    arrays = []
    for view, _, _ in items:
        if not any(view.array is a for a in arrays):
            arrays.append(view.array)
    n = len(arrays)

    def kernel(*refs):
        place_ref, _, wide_ref, send, gin_ref, gout_ref = refs[n:]
        top = 0
        for view, turn, far in items:
            part_ref = refs[[view.array is a for a in arrays].index(True)]
            part, bit = place_ref[0] ^ turn, place_ref[place_row(("dp", (phase + turn) % stages))]
            if far:
                bit = 1 - bit
            for i in range(count):
                span = slice(top, top + each)
                top = top + each
                wide_ref[span, :] = part_ref[
                    view.start + i * each : view.start + (i + 1) * each, :
                ].astype(F32)
                base = 2 * i * each
                column, at = first + base // share * width, part * share + base % share + bit * each
                to = pl.multiple_of(column + jnp.minimum(at, width - each), each)
                across = pl.multiple_of(jnp.maximum(at - width, 0), each)
                send(
                    wide_ref.at[span, :],
                    gout_ref.at[pl.ds(to, each), :],
                    gin_ref.at[pl.ds(across, each), column : column + width],
                    at < width,
                )

    _, *grads = line.call(
        kernel,
        arrays,
        (),
        scalars=(place,),
        scratch=(sds((len(items) * count * each, width), F32),),
        sent=(sds((width, full), F32), sds((full, width), F32)),
        aliased=before,
        copies=len(items) * count,
    )
    return tuple(grads)


def place_tail(line, place, views, experts, head, misc):
    peers = len(views)
    parts = [view.array for view in views]
    pair, width = 2 * head, parts[0].shape[1]
    each, share = pair // peers, misc // peers

    def last(*refs):
        part_refs, place_ref = refs[:peers], refs[peers]
        query_ref, output_ref, kv_ref, router_ref, one_ref, two_ref, pair_ref, misc_ref = refs[
            peers + 1 :
        ]
        for k, view in enumerate(views):
            part, start = place_ref[0] ^ k, view.start
            pair_ref[pl.ds(part * each, each), :] = part_refs[k][start : start + each, :].astype(F32)
            misc_ref[pl.ds(part * share, share), :] = part_refs[k][
                start + each : start + view.rows, :
            ].astype(F32)
        query_ref[0] = pair_ref[:head, :]
        output_ref[0] = pair_ref[head:, :]
        kv_ref[...] = misc_ref[:pair, :].T
        router_ref[...] = misc_ref[pair : pair + experts, :]
        one_ref[...] = misc_ref[pair + experts : pair + experts + 1, :]
        two_ref[...] = misc_ref[pair + experts + 1 : pair + experts + 2, :]

    return line.call(
        last,
        parts,
        [
            sds((1, head, width), F32),
            sds((1, head, width), F32),
            sds((width, pair), F32),
            sds((experts, width), F32),
            sds((1, width), F32),
            sds((1, width), F32),
        ],
        scalars=(place,),
        scratch=(sds((pair, width), F32), sds((misc, width), F32)),
    )


def join_all(line, arrays):
    rows, width = arrays[0].shape
    count = len(arrays)

    def kernel(*refs):
        for k in range(count):
            refs[count][k * rows : (k + 1) * rows, :] = refs[k][...]

    return line.call(kernel, arrays, [sds((count * rows, width), BF)])[0]


def body(
    tokens, out_grad, expert_ids, sentence_ids, ln_attn, w_kv, w_router, w_query, w_output, ln_ffn, w_in, w_out
):
    length, width = tokens.shape
    head = w_query.shape[2]
    pair = w_kv.shape[1]
    full = w_in.shape[1]
    experts = lax.axis_size("expert")
    peers = lax.axis_size("tok")
    choose = expert_ids.shape[1]
    tok, dp, expert = lax.axis_index("tok"), lax.axis_index("dp"), lax.axis_index("expert")
    stages = bits(lax.axis_size("dp"))
    dp_bits = [(dp >> ((s + tok) % stages)) & 1 for s in range(stages)]
    spots = jnp.stack(
        [tok, expert] + dp_bits + [(expert >> s) & 1 for s in range(bits(experts))]
    ).astype(jnp.int32)
    weights = jnp.concatenate([w_query[0].T, w_output[0]], axis=0)
    each = weights.shape[0] // peers
    weights = lax.dynamic_slice_in_dim(weights, tok * each, each, axis=0)
    pieces = exchange([weights] * experts, "expert")
    ids = expert_ids.T
    ln_one = ln_attn.reshape(1, width)
    ln_two = ln_ffn.reshape(1, width)
    line = Line()
    line.last = spots
    (
        normed, kv, kvt, gates, gt, small, sent, gains, keyid, place, ids, own_query, own_output, x, g, out_weight,
    ) = line.call(
        prepare_kernel,
        (),
        [
            sds((length, width), BF),
            sds((length, pair), BF),
            sds((pair, length), BF),
            sds((choose, length), F32),
            sds((width, length), BF),
            sds((pair + 16, width), BF),
            sds((1, length), F32),
            sds((2, width), F32),
            sds((length, BAND), F32),
            sds((8, 128), jnp.int32),
        ],
        fetched=(ln_one, w_kv, w_router.T, sentence_ids, ln_two),
        numbers=(spots,),
        kept=(ids, w_query[0].T, w_output[0], tokens, out_grad, w_out),
        room=8 << 20,
    )
    ag, in_weight = line.call(
        upstream_kernel, (g, out_weight), [sds((length, full), BF)], kept=(w_in,), room=8 << 20,
    )
    slab = join_all(line, pieces)
    slabs = [slab] + exchange([slab] * peers, "tok")
    wq, wo, qt, at, lse, gat, h, hn, hnt = line.call(
        functools.partial(attend_kernel, experts=experts, head=head, peers=peers),
        (*slabs, normed, kv, kvt, gates, x, ids, sent, gains, keyid, own_query, own_output),
        [
            sds((experts * head, width), BF),
            sds((experts * head, width), BF),
            sds((head, choose * length), BF),
            sds((head, choose * length), BF),
            sds((1, choose * length), F32),
            sds((experts * head, length), BF),
            sds((length, width), F32),
            sds((length, width), BF),
            sds((width, length), BF),
        ],
        scalars=(place,),
        scratch=(
            sds((experts * head, length), F32),
            sds((2 * head, width), BF),
            sds((length // BAND, 3 * BAND, choose * BAND), F32),
            sds((length // BAND, 3 * BAND, choose * BAND), BF),
        ),
        room=8 << 20,
    )

    chains = Chains(line, place)
    us, dpres, sums, spans = [], [], [], {}

    def ffn(last=None, mirror=0):
        rows = 2 * width // peers
        pieces = max(1, rows // PIECE)
        rows = rows // pieces
        u, dpre, *parts = line.call(
            functools.partial(ffn_kernel, first=len(us) * width, peers=peers),
            (hn, hnt, gt, ag, in_weight),
            [sds((length, width), BF)] * 2 + [sds((rows, width), BF)] * (peers * pieces),
            scalars=(place,),
            scratch=() if peers == 2 else (sds((2 * width, width), BF),),
            room=6 << 20,
        )
        us.append(u)
        dpres.append(dpre)
        for i in range(pieces):
            sums.append([parts[i]] + exchange(parts[i::pieces], "tok"))
        if last is not None:
            views = [View(same[0], more=same[1:]) for same in zip(*sums)]
            chains.begin(last, chunk_walk(views, mirror, len(sums), rows))
            hidden = len(sums) // pieces * width
            spans[last] = (len(us) * width - hidden, hidden)
            sums.clear()

    misc = -(-(pair + 16) // (64 * peers)) * 64 * peers

    def hidden():
        made["dh"], made["low"], made["gain"] = line.call(
            hidden_kernel,
            (h, g, in_weight, gains, *dpres),
            [sds((length, width), F32), sds((length, width), BF), sds((1, width), F32)],
            room=6 << 20,
        )

    def heads_back():
        made["z"], made["gout"] = line.call(
            functools.partial(heads_back_kernel, experts=experts, head=head),
            (kv, kvt, gates, wo, qt, at, lse, gat, made["low"], ids, sent, keyid),
            [sds((experts * head + pair + 16, length), BF), sds((experts * head, width), BF)],
            scratch=(
                sds((experts * head, length), F32),
                sds((pair, length), F32),
                sds((head, choose * length), BF),
                *[sds((length // BAND, 3 * BAND, choose * BAND), t) for t in (F32, F32, BF, BF)],
            ),
            room=6 << 20,
        )

    def rows_back():
        *parts, made["dx"] = line.call(
            functools.partial(rows_back_kernel, experts=experts, head=head, peers=peers, misc=misc),
            (made["z"], made["gout"], normed, wq, small, made["dh"], made["gain"], x, gains),
            ([sds((2 * pair // peers, width), BF)] * (experts // 2) + [sds((misc // peers, width), BF)])
            * peers,
            sent=(sds((length, width), BF),),
            scalars=(place,),
            scratch=(
                sds((experts * head + pair + 16, width), F32),
                sds((experts * pair, width), BF),
                sds((misc, width), F32),
                sds((length, width), BF),
            ),
            room=6 << 20,
        )
        chains.begin("t", tail_walk(tok_views(parts, peers), experts, pair // peers, 1))

    def out():
        _, made["output"] = line.call(
            output_kernel,
            (h, out_weight, *us),
            (),
            sent=(sds((length, width), BF),),
            scratch=(sds((length, width), BF),),
            room=6 << 20,
        )

    def place_some(name, wanted):
        walk = chains.finish(name)
        items = [
            (views[far], turn, far)
            for far in (0, 1)
            for turn, views in enumerate(walk[0])
            if wanted(turn > 0, far == 1)
        ]
        made["both"] = place_parts(
            line, place, items, walk, spans[name][0], width, full, made.get("both", ())
        )

    def last():
        made["t"] = place_tail(line, place, chains.finish("t"), experts, head, misc)

    made = {}
    acts = {"f": ffn, "n": hidden, "h": heads_back, "r": rows_back, "o": out, "T": last}
    for i, name in enumerate("ab"):
        acts[name.upper()] = functools.partial(ffn, name, i)
    acts["1"] = lambda: place_some("a", lambda other, far: True)
    acts["2"] = lambda: place_some("b", lambda other, far: not (other and far))
    acts["3"] = lambda: place_some("b", lambda other, far: other and far)
    for word in ORDER:
        if word in acts:
            acts[word]()
        else:
            chains.advance(*word)
    query, outp, kv_grad, router, one, two = made["t"]
    output, dx, both = made["output"], made["dx"], made["both"]
    return (
        output,
        dx,
        one.reshape(width),
        kv_grad,
        router.T,
        jnp.swapaxes(query, 1, 2),
        outp,
        two.reshape(width),
        both[0],
        both[1],
    )


def solution(mesh):
    rows = P(AXES, None)
    heads = P("expert", None, None)
    return jax.shard_map(
        body,
        mesh=mesh,
        in_specs=(rows, rows, rows, rows, P(), P(), P(), heads, heads, P(), P(), P()),
        out_specs=(rows, rows, P(), P(), P(), heads, heads, P(), P(), P()),
        check_vma=False,
    )
```

```python
import functools

import jax
import jax.numpy as jnp
from jax import lax
from jax.experimental import pallas as pl
from jax.experimental.pallas import tpu as pltpu
from jax.sharding import PartitionSpec as P

BF = jnp.bfloat16
F32 = jnp.float32
MASKED = -1e30
BAND = 128
ROWS = 256
PIECE = 512
AXES = ("dp", "expert", "tok")
GLUE = 23 * 10**9
WORK = 0 * 10**9 + 1
ORDER = (
    "f", "A", "f", "a", "B", "n", "a", "b", "h", "a", "r", "b", "a", "o", "b", "t", "a", "b", "a",
    "t", "b", "a", "t", "b", "t", "b", "1", "t", "2", "t", "3", "T",
)


def nn(left, right):
    return lax.dot_general(left, right, (((1,), (0,)), ((), ())), preferred_element_type=F32)


def nt(left, right):
    return lax.dot_general(left, right, (((1,), (1,)), ((), ())), preferred_element_type=F32)


def tn(left, right):
    return lax.dot_general(left, right, (((0,), (0,)), ((), ())), preferred_element_type=F32)


def normalize(values):
    centre = values - jnp.mean(values, axis=-1, keepdims=True)
    spread = jnp.mean(centre * centre, axis=-1, keepdims=True)
    inverse = lax.rsqrt(spread + 1e-05)
    return centre * inverse, inverse


def normalize_back(upstream, normalized, inverse, gain):
    scaled = upstream * gain
    inner = (
        scaled
        - jnp.mean(scaled, axis=-1, keepdims=True)
        - normalized * jnp.mean(scaled * normalized, axis=-1, keepdims=True)
    )
    return inner * inverse


def sds(shape, dtype):
    return jax.ShapeDtypeStruct(shape, dtype)


def size_of(array):
    lanes = -(-array.shape[-1] // 128) * 128
    rows = -(-array.shape[-2] // 16) * 16
    lead = 1
    for extent in array.shape[:-2]:
        lead = lead * extent
    return lead * rows * lanes * jnp.dtype(array.dtype).itemsize


class Place:
    def __init__(self, ref):
        self.ref = ref

    def __getitem__(self, row):
        return self.ref[row, 0]


class Line:
    def __init__(self):
        self.last = None

    def call(
        self, kernel, operands, outs, fetched=(), scalars=(), scratch=(), room=2 << 20, weight=WORK,
        sent=(), aliased=(), kept=(), numbers=(), delayed=0, copies=8,
    ):
        n, f, s = len(operands), len(fetched) + len(kept), len(scalars)
        late = () if self.last is None else (self.last,)
        skip = len(late) + len(aliased)
        outs = list(outs)
        h = len(sent)
        if not outs:
            outs = [sds((8, 128), F32)]
        outs = outs + [sds(a.shape, a.dtype) for a in kept]
        scratch_copies, fetched = len(fetched), (*fetched, *kept)

        def wrapped(*refs):
            ins = refs[:n]
            sources = refs[n : n + f]
            smem = [Place(ref) for ref in refs[n + f : n + f + s]]
            rest = list(refs[n + f + s + len(numbers) + skip :])
            if numbers:
                number_sem, number_ref = rest.pop(), rest.pop()
                number = pltpu.make_async_copy(refs[n + f + s], number_ref, number_sem.at[0])
                number.start()

                def number_wait():
                    number.wait()
                    return number_ref

                smem = smem + [number_wait]
            far = rest[len(outs) : len(outs) + h]
            del rest[len(outs) : len(outs) + h]
            open_copies, send_sem = [], rest.pop() if h else None
            sems = rest.pop() if f else None
            buffers = rest[len(rest) - scratch_copies :] if scratch_copies else []
            del rest[len(rest) - scratch_copies :]
            first = len(outs) - len(kept)
            buffers = buffers + rest[first : len(outs)]
            del rest[first : len(outs)]
            body, waits, waiting = rest, [], {}
            for i in range(f):
                copy = pltpu.make_async_copy(sources[i], buffers[i], sems.at[i])
                if i < f - delayed:
                    copy.start()
                waiting[i] = copy

                def wait(i=i):
                    if i in waiting:
                        waiting.pop(i).wait()
                        if i == f - delayed - 1:
                            for j in range(f - delayed, f):
                                waiting[j].start()
                    return buffers[i]

                waits.append(wait)
            def send(source, target, other=None, near=None):
                sem = send_sem.at[len(open_copies)]
                copy = pltpu.make_async_copy(source, target, sem)
                open_copies.append(copy)
                if other is None:
                    copy.start()
                    return
                pl.when(near)(copy.start)
                pl.when(jnp.logical_not(near))(pltpu.make_async_copy(source, other, sem).start)

            if h:
                kernel(*ins, *waits, *smem, *body, send, *far)
                for copy in open_copies:
                    copy.wait()
            else:
                kernel(*ins, *waits, *smem, *body)
            for copy in waiting.values():
                copy.wait()

        need = sum(size_of(a) for a in (*fetched[:scratch_copies], *scratch))
        extra = [pltpu.VMEM(a.shape, a.dtype) for a in fetched[:scratch_copies]]
        if f:
            extra.append(pltpu.SemaphoreType.DMA((f,)))
        if h:
            extra.append(pltpu.SemaphoreType.DMA((copies,)))
        if numbers:
            extra += [pltpu.SMEM(numbers[0].shape, jnp.int32), pltpu.SemaphoreType.DMA((1,))]
        results = pl.pallas_call(
            wrapped,
            out_shape=outs + list(sent),
            in_specs=[pl.BlockSpec(memory_space=pltpu.VMEM)] * n
            + [pl.BlockSpec(memory_space=pltpu.HBM)] * f
            + [pl.BlockSpec(memory_space=pltpu.VMEM)] * s
            + [pl.BlockSpec(memory_space=pl.ANY)] * len(numbers)
            + [pl.BlockSpec(memory_space=pl.ANY)] * skip,
            out_specs=[pl.BlockSpec(memory_space=pltpu.VMEM)] * len(outs)
            + [pl.BlockSpec(memory_space=pltpu.HBM)] * h,
            input_output_aliases={
                n + f + s + len(numbers) + len(late) + i: len(outs) + i for i in range(len(aliased))
            },
            scratch_shapes=[pltpu.VMEM(a.shape, a.dtype) for a in scratch] + extra,
            compiler_params=pltpu.CompilerParams(vmem_limit_bytes=need + room),
            cost_estimate=pl.CostEstimate(flops=weight, bytes_accessed=1024, transcendentals=0),
        )(
            *operands,
            *[pltpu.with_memory_space_constraint(a, pltpu.HBM) for a in fetched],
            *scalars,
            *numbers,
            *late,
            *aliased,
        )
        self.last = min(results[: len(outs)], key=lambda a: a.size)
        return results


def prepare_kernel(
    ln_wait, wkv_wait, wr_wait, sent_wait, ln_two_wait, ids_wait, wq_wait, wo_wait, x_wait, g_wait, wout_wait,
    spots_wait, xn_ref, kv_ref, kvt_ref, gates_ref, gt_ref, small_ref, sent_keep, gains_keep, keyid_ref,
    place_ref,
):
    ln_ref, ln_two_ref, sent_ref = ln_wait(), ln_two_wait(), sent_wait()
    gain = ln_ref[...]
    gains_keep[0:1, :] = gain
    gains_keep[1:2, :] = ln_two_ref[...]
    sent_keep[...] = sent_ref[...].astype(F32)
    column_ids(sent_keep, keyid_ref)
    wkv_ref, wr_ref, ids_ref = wkv_wait(), wr_wait(), ids_wait()
    pair = wkv_ref.shape[1]
    experts = wr_ref.shape[0]
    small_ref[:pair, :] = wkv_ref[...].T
    small_ref[pair:, :] = jnp.concatenate(
        [wr_ref[...].astype(F32), jnp.zeros((16 - experts, wr_ref.shape[1]), F32)], axis=0
    ).astype(BF)
    spots_ref = spots_wait()
    for i in range(spots_ref.shape[0]):
        place_ref[i : i + 1, :] = jnp.full((1, place_ref.shape[1]), spots_ref[i], jnp.int32)
    x_ref = x_wait()
    length = x_ref.shape[0]
    for start in range(0, length, ROWS):
        rows = pl.ds(start, ROWS)
        normalized, _ = normalize(x_ref[rows, :].astype(F32))
        xn_ref[rows, :] = (normalized * gain).astype(BF)
    normed = xn_ref[...]
    small = small_ref[...]
    both = nt(small, normed)
    kvt_ref[...] = both[:pair].astype(BF)
    kv_ref[...] = nn(normed, wkv_ref[...]).astype(BF)
    choose = ids_ref.shape[0]
    picked = []
    for route in range(choose):
        ids = ids_ref[route : route + 1, :]
        value = jnp.zeros((1, length), F32)
        for expert in range(experts):
            value = jnp.where(ids == expert, both[pair + expert : pair + expert + 1], value)
        picked.append(value)
    top = functools.reduce(jnp.maximum, picked)
    raised = [jnp.exp(value - top) for value in picked]
    total = functools.reduce(lambda a, b: a + b, raised)
    for route in range(choose):
        gates_ref[route : route + 1, :] = raised[route] / total
    g_ref = g_wait()
    gt_ref[...] = g_ref[...].T


def upstream_kernel(g_ref, wout_ref, win_wait, ag_ref):
    for start in range(0, g_ref.shape[0], ROWS):
        rows = slice(start, start + ROWS)
        ag_ref[rows, :] = nt(g_ref[rows, :], wout_ref[...]).astype(BF)


def column_ids(sent_ref, keyid_ref):
    length = sent_ref.shape[1]
    for start in range(0, length, BAND):
        row = jnp.broadcast_to(sent_ref[:, start : start + BAND], (BAND, BAND))
        keyid_ref[pl.ds(start, BAND), :] = row.T


def masked_scores(kv_ref, keyid_ref, sent_ref, queries, start, low, high, choose):
    padded = jnp.concatenate([queries * 0.125, jnp.zeros_like(queries)], axis=0)
    scores = nn(kv_ref[low:high, :], padded)
    same = keyid_ref[low:high, :] == sent_ref[:, start : start + BAND]
    parts = [
        jnp.where(same, scores[:, route * BAND : (route + 1) * BAND], MASKED)
        for route in range(choose)
    ]
    return jnp.concatenate(parts, axis=1)


def window(start, length):
    return max(start - BAND, 0), min(start + 2 * BAND, length)


def attend_kernel(*refs, experts, head, peers):
    slab_refs, refs = refs[:peers], refs[peers:]
    (
        xn_ref, kv_ref, kvt_ref, gates_ref, x_ref, ids_ref, sent_ref, ln_ref, keyid_ref, wq_own, wo_own,
        place_ref, wq_ref, wo_ref, qt_ref, at_ref, lse_ref, gat_ref, h_ref, hn_ref, hnt_ref, all_ref,
        pair_ref, score_ref, prob_ref,
    ) = refs
    own = place_ref[1]
    each = 2 * head // peers
    wq_ref[pl.ds(own * head, head), :] = wq_own[...]
    wo_ref[pl.ds(own * head, head), :] = wo_own[...]
    for k in range(1, experts):
        for j in range(peers):
            rows = pl.ds((place_ref[0] ^ j) * each, each)
            pair_ref[rows, :] = slab_refs[j][(k - 1) * each : k * each, :]
        rows = pl.ds((own ^ k) * head, head)
        wq_ref[rows, :] = pair_ref[:head, :]
        wo_ref[rows, :] = pair_ref[head:, :]
    length = xn_ref.shape[0]
    choose = ids_ref.shape[0]
    all_ref[...] = nt(wq_ref[...], xn_ref[...])
    starts = range(0, length, BAND)
    spans = [slice(start * choose, (start + BAND) * choose) for start in starts]
    bounds = [window(start, length) for start in starts]
    for start, block in zip(starts, spans):
        lanes = slice(start, start + BAND)
        chosen = []
        for route in range(choose):
            ids = ids_ref[route : route + 1, lanes]
            value = all_ref[:head, lanes]
            for expert in range(1, experts):
                value = jnp.where(
                    ids == expert, all_ref[expert * head : (expert + 1) * head, lanes], value
                )
            chosen.append(value)
        qt_ref[:, block] = jnp.concatenate(chosen, axis=1).astype(BF)
    for i, start in enumerate(starts):
        low, high = bounds[i]
        score_ref[i, : high - low, :] = masked_scores(
            kv_ref, keyid_ref, sent_ref, qt_ref[:, spans[i]], start, low, high, choose
        )
    for i, block in enumerate(spans):
        size = bounds[i][1] - bounds[i][0]
        scores = score_ref[i, :size, :]
        largest = jnp.max(scores, axis=0, keepdims=True)
        raised = jnp.exp(scores - largest)
        total = jnp.sum(raised, axis=0, keepdims=True)
        prob_ref[i, :size, :] = (raised * (1.0 / total)).astype(BF)
        lse_ref[:, block] = largest + jnp.log(total)
    for i, block in enumerate(spans):
        low, high = bounds[i]
        at_ref[:, block] = nn(kvt_ref[head:, low:high], prob_ref[i, : high - low, :]).astype(BF)
    for start in starts:
        lanes = slice(start, start + BAND)
        spread = [jnp.zeros((head, BAND), F32) for _ in range(experts)]
        for route in range(choose):
            ids = ids_ref[route : route + 1, lanes]
            first = start * choose + route * BAND
            gated = at_ref[:, first : first + BAND].astype(F32) * gates_ref[route : route + 1, lanes]
            for expert in range(experts):
                spread[expert] = jnp.where(ids == expert, gated, spread[expert])
        for expert in range(experts):
            gat_ref[expert * head : (expert + 1) * head, lanes] = spread[expert].astype(BF)
    gain = ln_ref[1:2, :]
    for start in range(0, length, ROWS):
        rows = slice(start, start + ROWS)
        mixed = tn(gat_ref[:, rows], wo_ref[...])
        hidden = x_ref[rows, :].astype(F32) + mixed
        h_ref[rows, :] = hidden
        normalized, _ = normalize(hidden)
        low_value = (normalized * gain).astype(BF)
        hn_ref[rows, :] = low_value
        hnt_ref[:, rows] = low_value.T


def gelu_both(values):
    bell = jnp.exp2(values * values * -0.7213475204444817)
    t = 1.0 / (1.0 + 0.23164188 * jnp.abs(values))
    poly = t * (
        0.127414796
        + t * (-0.142248368 + t * (0.7107068705 + t * (-0.7265760135 + t * 0.5307027145)))
    )
    tail = poly * bell
    cumulative = jnp.where(values >= 0.0, 1.0 - tail, tail)
    return values * cumulative, cumulative + values * (bell * 0.3989422804014327)


def ffn_block(refs, first):
    hn_ref, hnt_ref, gt_ref, ag_ref, win_ref, u_ref, dpre_ref = refs
    length, width = hn_ref.shape
    far = slice(first, first + width)
    out_grad = in_grad = None
    for start in range(0, length, 2 * ROWS):
        rows = slice(start, start + 2 * ROWS)
        activated, slope = gelu_both(nn(hn_ref[rows, :], win_ref[:, far]))
        activated = activated.astype(BF)
        before = (ag_ref[rows, far].astype(F32) * slope).astype(BF)
        u_ref[rows, :], dpre_ref[rows, :] = activated, before
        out_part, in_part = nn(gt_ref[:, rows], activated), nn(hnt_ref[:, rows], before)
        out_grad = out_part if out_grad is None else out_grad + out_part
        in_grad = in_part if in_grad is None else in_grad + in_part
    return out_grad.astype(BF).T, in_grad.astype(BF)


def ffn_kernel(*refs, first, peers):
    place_ref, part_refs = refs[5], list(refs[8:])
    width = refs[0].shape[1]
    tok = place_ref[0]
    out_grad, in_grad = ffn_block((*refs[:5], *refs[6:8]), first)
    if peers == 2:
        pieces = len(part_refs) // 2
        size = part_refs[0].shape[0]
        for i in range(pieces):
            span = slice(i * size, (i + 1) * size)
            one, two = out_grad[span, :], in_grad[span, :]
            part_refs[i][...] = jnp.where(tok == 0, one, two)
            part_refs[pieces + i][...] = jnp.where(tok == 0, two, one)
        return
    sum_ref = part_refs.pop()
    sum_ref[:width, :], sum_ref[width:, :] = out_grad, in_grad
    size = part_refs[0].shape[0]
    pieces = len(part_refs) // peers
    for k in range(peers):
        for i in range(pieces):
            start = (tok ^ k) * size * pieces + i * size
            part_refs[k * pieces + i][...] = sum_ref[pl.ds(start, size), :]


def output_kernel(*refs):
    h_ref, wout_ref = refs[:2]
    out_ref, send, far_ref = refs[-3:]
    u_refs = refs[2:-4]
    for start in range(0, h_ref.shape[0], ROWS):
        rows = slice(start, start + ROWS)
        total, first = h_ref[rows, :], 0
        for ref in u_refs:
            size = ref.shape[1]
            total = total + nn(ref[rows, :], wout_ref[first : first + size, :])
            first = first + size
        out_ref[rows, :] = total.astype(BF)
        send(out_ref.at[rows, :], far_ref.at[rows, :])


def hidden_kernel(*refs):
    h_ref, g_ref, win_ref, ln_ref = refs[:4]
    dh_ref, low_ref, gain_ref = refs[-3:]
    dpre_refs = refs[4:-3]
    gain = ln_ref[1:2, :]
    gain_sum = jnp.zeros_like(gain)
    for start in range(0, h_ref.shape[0], ROWS):
        rows = slice(start, start + ROWS)
        upstream, first = None, 0
        for ref in dpre_refs:
            size = ref.shape[1]
            part = nt(ref[rows, :], win_ref[:, first : first + size])
            upstream = part if upstream is None else upstream + part
            first = first + size
        normalized, inverse = normalize(h_ref[rows, :])
        value = g_ref[rows, :].astype(F32) + normalize_back(upstream, normalized, inverse, gain)
        dh_ref[rows, :] = value
        low_ref[rows, :] = value.astype(BF)
        gain_sum = gain_sum + jnp.sum(upstream * normalized, axis=0, keepdims=True)
    gain_ref[...] = gain_sum


def heads_back_kernel(
    kv_ref, kvt_ref, gates_ref, wo_ref, qt_ref, at_ref, lse_ref, gat_ref, low_ref, ids_ref, sent_ref,
    keyid_ref, z_ref, gout_ref, all_ref, dkv_ref, up_ref, prob_ref, grad_ref, soft_ref, ds_ref, *, experts,
    head,
):
    length = kv_ref.shape[0]
    wide, pair = experts * head, 2 * head
    choose = ids_ref.shape[0]
    all_ref[...] = nt(wo_ref[...], low_ref[...])
    gout_ref[...] = nn(gat_ref[...], low_ref[...]).astype(BF)
    dkv_ref[...] = jnp.zeros_like(dkv_ref)
    starts = range(0, length, BAND)
    spans = [slice(start * choose, (start + BAND) * choose) for start in starts]
    bounds = [window(start, length) for start in starts]
    for start, block in zip(starts, spans):
        lanes = slice(start, start + BAND)
        raw, gate_grads = [], []
        for route in range(choose):
            ids = ids_ref[route : route + 1, lanes]
            value = all_ref[:head, lanes]
            for expert in range(1, experts):
                value = jnp.where(
                    ids == expert, all_ref[expert * head : (expert + 1) * head, lanes], value
                )
            raw.append(value)
            first = start * choose + route * BAND
            attended = at_ref[:, first : first + BAND].astype(F32)
            gate_grads.append(jnp.sum(value * attended, axis=0, keepdims=True))
        gates = [gates_ref[route : route + 1, lanes] for route in range(choose)]
        common = functools.reduce(
            lambda a, b: a + b, [gate * grad for gate, grad in zip(gates, gate_grads)]
        )
        logit_rows = [jnp.zeros((1, BAND), F32) for _ in range(experts)]
        for route in range(choose):
            ids = ids_ref[route : route + 1, lanes]
            picked = gates[route] * (gate_grads[route] - common)
            for expert in range(experts):
                logit_rows[expert] = jnp.where(ids == expert, picked, logit_rows[expert])
        logit_pad = jnp.concatenate(
            logit_rows + [jnp.zeros((16 - experts, BAND), F32)], axis=0
        )
        z_ref[wide + pair :, lanes] = logit_pad.astype(BF)
        up_ref[:, block] = jnp.concatenate(
            [gate * value for gate, value in zip(gates, raw)], axis=1
        ).astype(BF)
    for i, start in enumerate(starts):
        low, high = bounds[i]
        prob_ref[i, : high - low, :] = masked_scores(
            kv_ref, keyid_ref, sent_ref, qt_ref[:, spans[i]], start, low, high, choose
        )
        upstream = up_ref[:, spans[i]]
        padded = jnp.concatenate([jnp.zeros_like(upstream), upstream], axis=0)
        grad_ref[i, : high - low, :] = nn(kv_ref[low:high, :], padded)
    for i, block in enumerate(spans):
        size = bounds[i][1] - bounds[i][0]
        probs = jnp.exp(prob_ref[i, :size, :] - lse_ref[:, block])
        soft_ref[i, :size, :] = probs.astype(BF)
        prob_grad = grad_ref[i, :size, :]
        mean = jnp.sum(probs * prob_grad, axis=0, keepdims=True)
        ds_ref[i, :size, :] = (probs * (prob_grad - mean)).astype(BF)
    for i, start in enumerate(starts):
        low, high = bounds[i]
        lanes = slice(start, start + BAND)
        score_grad = ds_ref[i, : high - low, :]
        query_grad = (nn(kvt_ref[:head, low:high], score_grad) * 0.125).astype(BF)
        spread = [jnp.zeros((head, BAND), BF) for _ in range(experts)]
        for route in range(choose):
            ids = ids_ref[route : route + 1, lanes]
            piece = query_grad[:, route * BAND : (route + 1) * BAND]
            for expert in range(experts):
                spread[expert] = jnp.where(ids == expert, piece, spread[expert])
        for expert in range(experts):
            z_ref[expert * head : (expert + 1) * head, lanes] = spread[expert]
        dkv_ref[:head, low:high] += nt(qt_ref[:, spans[i]], score_grad) * 0.125
        dkv_ref[head:, low:high] += nt(up_ref[:, spans[i]], soft_ref[i, : high - low, :])
    z_ref[wide : wide + pair, :] = dkv_ref[...].astype(BF)


def rows_back_kernel(*refs, experts, head, peers, misc):
    (
        z_ref, gout_ref, xn_ref, wq_ref, small_ref, dh_ref, gain_two_ref, x_ref, ln_ref, place_ref,
    ) = refs[:10]
    pieces = experts // 2 + 1
    part_refs = refs[10 : 10 + peers * pieces]
    grads_ref, pair_ref, misc_ref, dx_ref, send, far_ref = refs[10 + peers * pieces :]
    length = xn_ref.shape[0]
    wide, pair = experts * head, 2 * head
    grads_ref[...] = nn(z_ref[...], xn_ref[...])
    for expert in range(experts):
        rows = slice(expert * head, (expert + 1) * head)
        pair_ref[expert * pair : expert * pair + head, :] = grads_ref[rows, :].astype(BF)
        pair_ref[expert * pair + head : (expert + 1) * pair, :] = gout_ref[rows, :]
    gain = ln_ref[0:1, :]
    total = jnp.zeros_like(gain)
    for start in range(0, length, ROWS):
        rows = slice(start, start + ROWS)
        normed_grad = tn(z_ref[:wide, rows], wq_ref[...]) + tn(z_ref[wide:, rows], small_ref[...])
        normalized, inverse = normalize(x_ref[rows, :].astype(F32))
        total = total + jnp.sum(normed_grad * normalized, axis=0, keepdims=True)
        back = normalize_back(normed_grad, normalized, inverse, gain)
        dx_ref[rows, :] = (dh_ref[rows, :] + back).astype(BF)
        send(dx_ref.at[rows, :], far_ref.at[rows, :])
    misc_ref[...] = jnp.zeros_like(misc_ref)
    misc_ref[:pair, :] = grads_ref[wide : wide + pair, :]
    misc_ref[pair : pair + 16, :] = jnp.concatenate(
        [
            grads_ref[wide + pair : wide + pair + experts, :],
            total,
            gain_two_ref[...],
            jnp.zeros((14 - experts, total.shape[1]), F32),
        ],
        axis=0,
    )
    each, share = pair // peers, misc // peers
    for k in range(peers):
        part = place_ref[0] ^ k
        for expert in range(experts):
            rows = pl.ds(expert * pair + part * each, each)
            low = expert % 2 * each
            part_refs[k * pieces + expert // 2][low : low + each, :] = pair_ref[rows, :]
        part_refs[(k + 1) * pieces - 1][...] = misc_ref[pl.ds(part * share, share), :].astype(BF)


def exchange(parts, axis):
    size = len(parts)
    return [
        lax.ppermute(parts[k], axis, [(i, i ^ k) for i in range(size)]) for k in range(1, size)
    ]


def tok_views(parts, peers):
    pieces = len(parts) // peers
    others = [exchange(parts[i::pieces], "tok") for i in range(pieces)]
    own = [View(parts[0], more=parts[1:pieces])]
    return own + [View(others[0][k], more=[o[k] for o in others[1:]]) for k in range(peers - 1)]


def bits(size):
    return size.bit_length() - 1


def swap(array, key):
    kind, stage = key
    if kind == "expert":
        size = lax.axis_size("expert")
        return lax.ppermute(array, "expert", [(i, i ^ (1 << stage)) for i in range(size)])
    dp, expert, tok = (lax.axis_size(axis) for axis in AXES)
    pairs = []
    for d in range(dp):
        for e in range(expert):
            for t in range(tok):
                if kind == "dp":
                    there = (d ^ (1 << ((stage + t) % bits(dp)))) * expert + e
                else:
                    there = d * expert + (e ^ (1 << ((stage + t) % bits(expert))))
                pairs.append(((d * expert + e) * tok + t, there * tok + t))
    return lax.ppermute(array, AXES, pairs)


def place_row(key):
    kind, stage = key
    return 2 + stage if kind == "dp" else 2 + bits(lax.axis_size("dp")) + stage


class View:
    def __init__(self, array, start=0, rows=None, more=()):
        self.arrays, self.start = [array, *more], start
        self.rows = sum(a.shape[0] for a in self.arrays) if rows is None else rows
        self.array = array

    def read(self, refs, base, stride, bit, rows):
        if len(self.arrays) == 1:
            return refs[0][pl.ds(self.start + base + bit * stride, rows), :].astype(F32)
        size = self.arrays[0].shape[0]
        if stride == 0:
            at = min(base // size, len(self.arrays) - 1)
            return refs[at][base - at * size : base - at * size + rows, :].astype(F32)
        near, far = base // size, (base + stride) // size
        if near == far:
            return refs[near][pl.ds(base - near * size + bit * stride, rows), :].astype(F32)
        if rows > size:
            parts = [
                self.read(refs, base + i * size, stride, bit, size) for i in range(rows // size)
            ]
            return jnp.concatenate(parts, axis=0)
        one = refs[near][base - near * size : base - near * size + rows, :]
        two = refs[far][base + stride - far * size : base + stride - far * size + rows, :]
        return jnp.where(bit == 0, one.astype(F32), two.astype(F32))


class Job:
    def __init__(self, kind, views, key, row=0, count=0, each=0, shared=False):
        self.kind, self.views, self.key, self.row = kind, views, key, row
        self.shared = shared
        self.count, self.each = count, each
        rows = views[0].rows
        self.kept = rows // 2
        if kind == "add":
            self.sent = rows
        elif kind == "join":
            self.sent = 2 * rows
        elif kind == "weave":
            self.sent = 2 * rows
        elif kind in ("split", "halve"):
            self.sent = rows // 2
        else:
            self.sent = self.kept = count // 2 * each + rows - count * each
        self.keeps = kind in ("split", "pick", "halve")


def glue(line, place, jobs):
    arrays = []
    for job in jobs:
        for view in job.views:
            for array in view.arrays:
                if not any(array is a for a in arrays):
                    arrays.append(array)
    width = arrays[0].shape[1]
    offsets, total = [], 0
    for job in jobs:
        offsets.append(total)
        total += job.sent
    n = len(arrays)

    def kernel(*refs):
        place_ref, send_ref, keep_refs = refs[n], refs[n + 1], list(refs[n + 2 :])

        def ref_of(array):
            return refs[[array is a for a in arrays].index(True)]

        def added(job, base, rows, stride=0, bit=0):
            value = None
            for view in job.views:
                part = view.read([ref_of(a) for a in view.arrays], base, stride, bit, rows)
                value = part if value is None else value + part
            return value.astype(BF)

        for job, offset in zip(jobs, offsets):
            rows, bit = job.views[0].rows, place_ref[job.row]
            if job.kind == "add":
                send_ref[offset : offset + rows, :] = added(job, 0, rows)
            elif job.kind == "join":
                for view, turn in zip(job.views, (bit, 1 - bit)):
                    send_ref[pl.ds(offset + turn * rows, rows), :] = ref_of(view.array)[
                        view.start : view.start + rows, :
                    ]
            elif job.kind == "weave":
                spans = [(q * job.each, job.each) for q in range(job.count)]
                if rows > job.count * job.each:
                    spans.append((job.count * job.each, rows - job.count * job.each))
                for view, turn in zip(job.views, (bit, 1 - bit)):
                    ref = ref_of(view.array)
                    for base, size in spans:
                        send_ref[pl.ds(offset + 2 * base + turn * size, size), :] = ref[
                            view.start + base : view.start + base + size, :
                        ]
            elif job.kind == "halve":
                keep_ref, to = keep_refs.pop(0), 0
                spans = [(q * job.each, job.each) for q in range(job.count)]
                if rows > job.count * job.each:
                    spans.append((job.count * job.each, rows - job.count * job.each))
                for base, size in spans:
                    half = size // 2
                    keep_ref[to : to + half, :] = added(job, base, half, half, bit)
                    send_ref[offset + to : offset + to + half, :] = added(job, base, half, half, 1 - bit)
                    to += half
            elif job.kind == "split":
                half, keep_ref = job.sent, keep_refs.pop(0)
                keep_ref[...] = added(job, 0, half, half, bit)
                send_ref[offset : offset + half, :] = added(job, 0, half, half, 1 - bit)
            else:
                keep_ref, each = keep_refs.pop(0), job.each
                for q in range(job.count // 2):
                    keep_ref[q * each : (q + 1) * each, :] = added(job, 2 * q * each, each, each, bit)
                    send_ref[offset + q * each : offset + (q + 1) * each, :] = added(
                        job, 2 * q * each, each, each, 1 - bit
                    )
                done, base = job.count // 2 * each, job.count * each
                rest = added(job, base, rows - base)
                keep_ref[done:, :] = rest
                send_ref[offset + done : offset + job.sent, :] = rest

    outs = [sds((total, width), BF)] + [sds((job.kept, width), BF) for job in jobs if job.keeps]
    send, *keeps = line.call(kernel, arrays, outs, scalars=(place,), weight=GLUE)
    owns = []
    for job, offset in zip(jobs, offsets):
        owns.append(View(keeps.pop(0)) if job.keeps else View(send, offset, job.sent))
    return send, owns, offsets


class Chains:
    def __init__(self, line, place):
        self.line, self.place = line, place
        self.walks, self.jobs, self.done = {}, {}, {}

    def take(self, name, value):
        try:
            self.jobs[name] = self.walks[name].send(value)
        except StopIteration as end:
            self.done[name] = end.value
            del self.walks[name]

    def begin(self, name, walk):
        self.walks[name] = walk
        self.take(name, None)

    def advance(self, *names):
        names = [name for name in names if name in self.walks]
        while names:
            key = self.jobs[names[0]].key
            group = [name for name in names if self.jobs[name].key == key]
            names = [name for name in names if name not in group]
            jobs = [self.jobs[name] for name in group]
            send, owns, offsets = glue(self.line, self.place, jobs)
            if key[0] == "tok":
                others = exchange([send] * lax.axis_size("tok"), "tok")
            else:
                others = [swap(send, key)]
            more = []
            if any(job.shared for job in jobs):
                more = [exchange([a] * lax.axis_size("tok"), "tok") for a in (send, others[0])]
            for name, job, own, offset in zip(group, jobs, owns, offsets):
                views = [own] + [View(other, offset, job.sent) for other in others]
                if job.shared:
                    views = [views] + [[View(a, offset, job.sent) for a in same] for same in zip(*more)]
                self.take(name, views)

    def finish(self, name):
        while name in self.walks:
            self.advance(name)
        return self.done[name]


def chunk_walk(views, mirror, count, each):
    order = [("dp", (s + mirror) % 2) for s in range(bits(lax.axis_size("dp")))]
    experts = [("expert", s) for s in range(bits(lax.axis_size("expert")))]
    halved = []
    for key in order + experts[:-1]:
        if each < 32:
            break
        views = yield Job("halve", views, key, place_row(key), count, each)
        each //= 2
        halved.append(key)
    for key in (order + experts)[len(halved) :]:
        views = yield Job("add", views, key)
    views = yield Job("add", views, halved[-1])
    for before, key in zip(halved[:0:-1], halved[-2::-1]):
        views = yield Job(
            "weave", views, key, place_row(before), count, each, shared=key == order[0]
        )
        each *= 2
    return views, order[0], count, each


def tail_walk(views, experts, each, mirror):
    stages = bits(lax.axis_size("dp"))
    first, *others = [("dp", (s + mirror) % stages) for s in range(stages)]
    halves = each >= 32
    if halves:
        views = yield Job("halve", views, first, place_row(first), experts, each)
        each //= 2
    for stage in range(bits(experts)):
        key = ("expert", stage)
        views = yield Job("pick", views, key, place_row(key), experts >> stage, each)
    for key in [*others, first]:
        views = yield Job("add", views, key)
    if halves:
        views = yield Job("weave", views, ("tok", 0), place_row(first), 1, each)
    else:
        views = yield Job("add", views, ("tok", 0))
    return views


def place_parts(line, place, items, walk, first, width, full, before):
    _, (_, phase), count, each = walk
    peers, stages = lax.axis_size("tok"), bits(lax.axis_size("dp"))
    share = 2 * width // peers
    arrays = []
    for view, _, _ in items:
        if not any(view.array is a for a in arrays):
            arrays.append(view.array)
    n = len(arrays)

    def kernel(*refs):
        place_ref, _, wide_ref, send, gin_ref, gout_ref = refs[n:]
        top = 0
        for view, turn, far in items:
            part_ref = refs[[view.array is a for a in arrays].index(True)]
            part, bit = place_ref[0] ^ turn, place_ref[place_row(("dp", (phase + turn) % stages))]
            if far:
                bit = 1 - bit
            for i in range(count):
                span = slice(top, top + each)
                top = top + each
                wide_ref[span, :] = part_ref[
                    view.start + i * each : view.start + (i + 1) * each, :
                ].astype(F32)
                base = 2 * i * each
                column, at = first + base // share * width, part * share + base % share + bit * each
                to = pl.multiple_of(column + jnp.minimum(at, width - each), each)
                across = pl.multiple_of(jnp.maximum(at - width, 0), each)
                send(
                    wide_ref.at[span, :],
                    gout_ref.at[pl.ds(to, each), :],
                    gin_ref.at[pl.ds(across, each), column : column + width],
                    at < width,
                )

    _, *grads = line.call(
        kernel,
        arrays,
        (),
        scalars=(place,),
        scratch=(sds((len(items) * count * each, width), F32),),
        sent=(sds((width, full), F32), sds((full, width), F32)),
        aliased=before,
        copies=len(items) * count,
    )
    return tuple(grads)


def place_tail(line, place, views, experts, head, misc):
    peers = len(views)
    parts = [view.array for view in views]
    pair, width = 2 * head, parts[0].shape[1]
    each, share = pair // peers, misc // peers

    def last(*refs):
        part_refs, place_ref = refs[:peers], refs[peers]
        query_ref, output_ref, kv_ref, router_ref, one_ref, two_ref, pair_ref, misc_ref = refs[
            peers + 1 :
        ]
        for k, view in enumerate(views):
            part, start = place_ref[0] ^ k, view.start
            pair_ref[pl.ds(part * each, each), :] = part_refs[k][start : start + each, :].astype(F32)
            misc_ref[pl.ds(part * share, share), :] = part_refs[k][
                start + each : start + view.rows, :
            ].astype(F32)
        query_ref[0] = pair_ref[:head, :]
        output_ref[0] = pair_ref[head:, :]
        kv_ref[...] = misc_ref[:pair, :].T
        router_ref[...] = misc_ref[pair : pair + experts, :]
        one_ref[...] = misc_ref[pair + experts : pair + experts + 1, :]
        two_ref[...] = misc_ref[pair + experts + 1 : pair + experts + 2, :]

    return line.call(
        last,
        parts,
        [
            sds((1, head, width), F32),
            sds((1, head, width), F32),
            sds((width, pair), F32),
            sds((experts, width), F32),
            sds((1, width), F32),
            sds((1, width), F32),
        ],
        scalars=(place,),
        scratch=(sds((pair, width), F32), sds((misc, width), F32)),
    )


def join_all(line, arrays):
    rows, width = arrays[0].shape
    count = len(arrays)

    def kernel(*refs):
        for k in range(count):
            refs[count][k * rows : (k + 1) * rows, :] = refs[k][...]

    return line.call(kernel, arrays, [sds((count * rows, width), BF)])[0]


def body(
    tokens, out_grad, expert_ids, sentence_ids, ln_attn, w_kv, w_router, w_query, w_output, ln_ffn, w_in, w_out
):
    length, width = tokens.shape
    head = w_query.shape[2]
    pair = w_kv.shape[1]
    full = w_in.shape[1]
    experts = lax.axis_size("expert")
    peers = lax.axis_size("tok")
    choose = expert_ids.shape[1]
    tok, dp, expert = lax.axis_index("tok"), lax.axis_index("dp"), lax.axis_index("expert")
    stages = bits(lax.axis_size("dp"))
    dp_bits = [(dp >> ((s + tok) % stages)) & 1 for s in range(stages)]
    spots = jnp.stack(
        [tok, expert] + dp_bits + [(expert >> s) & 1 for s in range(bits(experts))]
    ).astype(jnp.int32)
    weights = jnp.concatenate([w_query[0].T, w_output[0]], axis=0)
    each = weights.shape[0] // peers
    weights = lax.dynamic_slice_in_dim(weights, tok * each, each, axis=0)
    pieces = exchange([weights] * experts, "expert")
    ids = expert_ids.T
    ln_one = ln_attn.reshape(1, width)
    ln_two = ln_ffn.reshape(1, width)
    line = Line()
    line.last = spots
    (
        normed, kv, kvt, gates, gt, small, sent, gains, keyid, place, ids, own_query, own_output, x, g, out_weight,
    ) = line.call(
        prepare_kernel,
        (),
        [
            sds((length, width), BF),
            sds((length, pair), BF),
            sds((pair, length), BF),
            sds((choose, length), F32),
            sds((width, length), BF),
            sds((pair + 16, width), BF),
            sds((1, length), F32),
            sds((2, width), F32),
            sds((length, BAND), F32),
            sds((8, 128), jnp.int32),
        ],
        fetched=(ln_one, w_kv, w_router.T, sentence_ids, ln_two),
        numbers=(spots,),
        kept=(ids, w_query[0].T, w_output[0], tokens, out_grad, w_out),
        room=8 << 20,
    )
    ag, in_weight = line.call(
        upstream_kernel, (g, out_weight), [sds((length, full), BF)], kept=(w_in,), room=8 << 20,
    )
    slab = join_all(line, pieces)
    slabs = [slab] + exchange([slab] * peers, "tok")
    wq, wo, qt, at, lse, gat, h, hn, hnt = line.call(
        functools.partial(attend_kernel, experts=experts, head=head, peers=peers),
        (*slabs, normed, kv, kvt, gates, x, ids, sent, gains, keyid, own_query, own_output),
        [
            sds((experts * head, width), BF),
            sds((experts * head, width), BF),
            sds((head, choose * length), BF),
            sds((head, choose * length), BF),
            sds((1, choose * length), F32),
            sds((experts * head, length), BF),
            sds((length, width), F32),
            sds((length, width), BF),
            sds((width, length), BF),
        ],
        scalars=(place,),
        scratch=(
            sds((experts * head, length), F32),
            sds((2 * head, width), BF),
            sds((length // BAND, 3 * BAND, choose * BAND), F32),
            sds((length // BAND, 3 * BAND, choose * BAND), BF),
        ),
        room=8 << 20,
    )

    chains = Chains(line, place)
    us, dpres, sums, spans = [], [], [], {}

    def ffn(last=None, mirror=0):
        rows = 2 * width // peers
        pieces = max(1, rows // PIECE)
        rows = rows // pieces
        u, dpre, *parts = line.call(
            functools.partial(ffn_kernel, first=len(us) * width, peers=peers),
            (hn, hnt, gt, ag, in_weight),
            [sds((length, width), BF)] * 2 + [sds((rows, width), BF)] * (peers * pieces),
            scalars=(place,),
            scratch=() if peers == 2 else (sds((2 * width, width), BF),),
            room=6 << 20,
        )
        us.append(u)
        dpres.append(dpre)
        for i in range(pieces):
            sums.append([parts[i]] + exchange(parts[i::pieces], "tok"))
        if last is not None:
            views = [View(same[0], more=same[1:]) for same in zip(*sums)]
            chains.begin(last, chunk_walk(views, mirror, len(sums), rows))
            hidden = len(sums) // pieces * width
            spans[last] = (len(us) * width - hidden, hidden)
            sums.clear()

    misc = -(-(pair + 16) // (64 * peers)) * 64 * peers

    def hidden():
        made["dh"], made["low"], made["gain"] = line.call(
            hidden_kernel,
            (h, g, in_weight, gains, *dpres),
            [sds((length, width), F32), sds((length, width), BF), sds((1, width), F32)],
            room=6 << 20,
        )

    def heads_back():
        made["z"], made["gout"] = line.call(
            functools.partial(heads_back_kernel, experts=experts, head=head),
            (kv, kvt, gates, wo, qt, at, lse, gat, made["low"], ids, sent, keyid),
            [sds((experts * head + pair + 16, length), BF), sds((experts * head, width), BF)],
            scratch=(
                sds((experts * head, length), F32),
                sds((pair, length), F32),
                sds((head, choose * length), BF),
                *[sds((length // BAND, 3 * BAND, choose * BAND), t) for t in (F32, F32, BF, BF)],
            ),
            room=6 << 20,
        )

    def rows_back():
        *parts, made["dx"] = line.call(
            functools.partial(rows_back_kernel, experts=experts, head=head, peers=peers, misc=misc),
            (made["z"], made["gout"], normed, wq, small, made["dh"], made["gain"], x, gains),
            ([sds((2 * pair // peers, width), BF)] * (experts // 2) + [sds((misc // peers, width), BF)])
            * peers,
            sent=(sds((length, width), BF),),
            scalars=(place,),
            scratch=(
                sds((experts * head + pair + 16, width), F32),
                sds((experts * pair, width), BF),
                sds((misc, width), F32),
                sds((length, width), BF),
            ),
            room=6 << 20,
        )
        chains.begin("t", tail_walk(tok_views(parts, peers), experts, pair // peers, 1))

    def out():
        _, made["output"] = line.call(
            output_kernel,
            (h, out_weight, *us),
            (),
            sent=(sds((length, width), BF),),
            scratch=(sds((length, width), BF),),
            room=6 << 20,
        )

    def place_some(name, wanted):
        walk = chains.finish(name)
        items = [
            (views[far], turn, far)
            for far in (0, 1)
            for turn, views in enumerate(walk[0])
            if wanted(turn > 0, far == 1)
        ]
        made["both"] = place_parts(
            line, place, items, walk, spans[name][0], width, full, made.get("both", ())
        )

    def last():
        made["t"] = place_tail(line, place, chains.finish("t"), experts, head, misc)

    made = {}
    acts = {"f": ffn, "n": hidden, "h": heads_back, "r": rows_back, "o": out, "T": last}
    for i, name in enumerate("ab"):
        acts[name.upper()] = functools.partial(ffn, name, i)
    acts["1"] = lambda: place_some("a", lambda other, far: True)
    acts["2"] = lambda: place_some("b", lambda other, far: not far)
    acts["3"] = lambda: place_some("b", lambda other, far: far)
    for word in ORDER:
        if word in acts:
            acts[word]()
        else:
            chains.advance(*word)
    query, outp, kv_grad, router, one, two = made["t"]
    output, dx, both = made["output"], made["dx"], made["both"]
    return (
        output,
        dx,
        one.reshape(width),
        kv_grad,
        router.T,
        jnp.swapaxes(query, 1, 2),
        outp,
        two.reshape(width),
        both[0],
        both[1],
    )


def solution(mesh):
    rows = P(AXES, None)
    heads = P("expert", None, None)
    return jax.shard_map(
        body,
        mesh=mesh,
        in_specs=(rows, rows, rows, rows, P(), P(), P(), heads, heads, P(), P(), P()),
        out_specs=(rows, rows, P(), P(), P(), heads, heads, P(), P(), P()),
        check_vma=False,
    )
```
